32 devices in a mesh: dom: 32 (over z, y, x, core).
Axes of the slice: x: 2, y: 2, z: 4, core: 2. Of those that a mesh axis runs over, the one named last changes fastest.
Arguments:
- features: bfloat16 [64, 262144], P(None, 'dom'), may hold values from -6 to 6
- cheb_weight: bfloat16 [4, 64, 64], replicated, may hold values from -0.375 to 0.375
- lap_tiles: bfloat16 [2048, 3, 128, 128], P('dom'), may hold values from -0.25 to 0.25
- col_index: int32 [2048, 3], P('dom'), may hold values from 0 to 63
- cross_tiles: bfloat16 [32, 5, 2, 128, 128], P('dom'), may hold values from -0.25 to 0.25
- send_index: int32 [32, 5, 2], P('dom'), may hold values from 0 to 63
- row_index: int32 [32, 5, 2], P('dom'), may hold values from 0 to 63
- pair_on: int32 [32, 5], P('dom'), may hold values 0 or 1
- blk_live: int32 [32], P('dom'), may hold values from 1 to 64, 1536 in all
- cotangent: bfloat16 [64, 262144], P(None, 'dom'), may hold values from -6 to 6
Outputs:
- conv_out: bfloat16 [64, 262144], P(None, 'dom')
- grad_x: bfloat16 [64, 262144], P(None, 'dom')
- grad_w: float32 [4, 64, 64], replicated
The draws below stay inside these ranges and needn't reach their ends.
Inputs may be any that keep to these rules, and one draw needn't show every extreme that they name: `blk_live`: the counts sum to 1536 and the largest is exactly 64.
All inputs are finite; a program needn't handle non-finite values. No bound on the sum of `pair_on` or of `blk_live` on one device may be relied on, other than what follows from the above.
Results may differ from the reference program's by a relative error of at most 0.0059.
Values may be sent and summed in bfloat16 or wider, within the bound.
No kernel may reach another device: no remote copies, remote signals or barrier semaphores. Data moves between devices by JAX's collectives and lax.ppermute only.
A program may use at most 128 MiB of HBM per device.

```python
import math
import jax
import jax.numpy as jnp
import numpy as np
from jax import lax

F = 64
ORDER = 3
BLK = 128
NB = 64
NZ = 3
HB = 2
ROUNDS = 5
NBLOCKS = 2048
PIXELS = 262144
N_DOM = 32


def touch_ends(result, own_key, low, largest):
    longest = result.shape.index(max(result.shape))
    spots = []
    for shift in (0, 1):
        where = [jax.random.randint(jax.random.fold_in(own_key, axis), (), 0, length) for axis, length in enumerate(result.shape)]
        where[longest] = (where[longest] + shift) % result.shape[longest]
        spots.append(tuple(where))
    return result.at[spots[0]].set(low).at[spots[1]].set(largest)


def steps_of(rng, shape, shards, low, largest):
    factor_of, own = 1.0, jax.random.fold_in(rng, 6)
    for axis_at, blocks in shards:
        heights = jnp.exp(jax.random.uniform(jax.random.fold_in(own, axis_at), (blocks,), jnp.float32, low / len(shards), largest / len(shards)))
        factor_of = factor_of * jnp.repeat(heights, shape[axis_at] // blocks).reshape([-1 if axis == axis_at else 1 for axis in range(len(shape))])
    return factor_of


def profile(number_of, total, limit, slope):
    weights = [(1 << 20) // math.isqrt(rank ** slope) + 1 for rank in range(2, number_of + 1)]
    rest, counts = total - limit - (number_of - 1), [1] * (number_of - 1)
    while rest > 0:
        movable = [i for i in range(number_of - 1) if counts[i] < limit]
        mass, budget = sum([weights[i] for i in movable]), rest
        for i in movable:
            extra = min(limit - counts[i], max(1, budget * weights[i] // mass), rest)
            counts[i] = counts[i] + extra
            rest = rest - extra
    return np.array([limit] + counts)


def uneven_parts(key, number_of, total, reach, slope):
    if number_of == 2:
        one = jax.random.randint(key, (), max(1, total - reach), min(reach, total - 1) + 1)
        return jnp.stack([one, total - one])
    tallies = jnp.asarray(profile(number_of, total, reach, slope), jnp.int32)
    twos = (number_of - 1) // 2
    giver, sink = tallies[1:1 + 2 * twos:2], tallies[2:2 + 2 * twos:2]
    margin = jnp.minimum(giver - 1, reach - sink)
    shifted = jax.random.randint(jax.random.fold_in(key, 1), (twos,), 0, 1 << 20) % (margin + 1)
    tallies = tallies.at[1:1 + 2 * twos:2].set(giver - shifted).at[2:2 + 2 * twos:2].set(sink + shifted)
    return tallies[jax.random.permutation(jax.random.fold_in(key, 2), number_of)]


def gaussian(stream_key, shape, width, most, shards=(), kind=jnp.bfloat16):
    result = jax.random.normal(stream_key, shape, jnp.float32) * width
    if len(shards) > 0:
        result = steps_of(stream_key, shape, shards, -0.22, 0.18) * result
    return jnp.clip(result, min=-most, max=most).astype(kind)


def setup_inputs(seed: int = 0) -> dict:
    streams_of = jax.random.split(jax.random.key(seed), 11)
    features = gaussian(streams_of[0], (F, PIXELS), 1.0, 6.0, ((1, 32),))
    cheb_weight = gaussian(streams_of[1], (ORDER + 1, F, F), (F * (ORDER + 1)) ** -0.5, 0.375)
    lap_tiles = gaussian(streams_of[2], (NBLOCKS, NZ, BLK, BLK), (BLK * (NZ + 1)) ** -0.5, 0.25, ((0, 32),))
    col_index = touch_ends(jax.random.randint(streams_of[3], (NBLOCKS, NZ), 0, NB), jax.random.fold_in(streams_of[3], 1), 0, NB - 1).astype(jnp.int32)
    cross_tiles = gaussian(streams_of[4], (N_DOM, ROUNDS, HB, BLK, BLK), (BLK * (NZ + 1)) ** -0.5, 0.25, ((0, 32),))
    send_index = touch_ends(jax.random.randint(streams_of[5], (N_DOM, ROUNDS, HB), 0, NB), jax.random.fold_in(streams_of[5], 1), 0, NB - 1).astype(jnp.int32)
    row_index = touch_ends(jax.random.randint(streams_of[6], (N_DOM, ROUNDS, HB), 0, NB), jax.random.fold_in(streams_of[6], 1), 0, NB - 1).astype(jnp.int32)
    pair_on = touch_ends((jax.random.randint(streams_of[7], (N_DOM, ROUNDS), 0, 4) < 3).astype(jnp.int32), jax.random.fold_in(streams_of[7], 1), 0, 1)
    blk_live = uneven_parts(streams_of[8], N_DOM, (3 * NB * N_DOM) // 4, NB, 2).astype(jnp.int32)
    cotangent = gaussian(streams_of[9], (F, PIXELS), 1.0, 6.0, ((1, 32),))
    return dict(features=features, cheb_weight=cheb_weight, lap_tiles=lap_tiles, col_index=col_index, cross_tiles=cross_tiles, send_index=send_index, row_index=row_index, pair_on=pair_on, blk_live=blk_live, cotangent=cotangent)


def to_blocks(values):
    return values.reshape(values.shape[0], N_DOM, NB, BLK).transpose(1, 0, 2, 3)


def from_blocks(values):
    return values.transpose(1, 0, 2, 3).reshape(values.shape[1], N_DOM * NB * BLK)


def reference(features, cheb_weight, lap_tiles, col_index, cross_tiles, send_index, row_index, pair_on, blk_live, cotangent):
    highest = lax.Precision.HIGHEST
    tiles = lap_tiles.reshape(N_DOM, NB, NZ, BLK, BLK)
    columns = col_index.reshape(N_DOM, NB, NZ)
    owners = jnp.arange(N_DOM, dtype=jnp.int32)
    live_blocks = blk_live.astype(jnp.int32)
    mask_full = (jnp.arange(NB, dtype=jnp.int32)[None, :] < live_blocks[:, None]).astype(jnp.float32)[:, None, :, None]
    mask_half = mask_full.astype(jnp.bfloat16)
    send_rows = (send_index % live_blocks[:, None, None]).astype(jnp.int32)
    recv_rows = (row_index % live_blocks[:, None, None]).astype(jnp.int32)
    switch = pair_on.astype(jnp.float32)
    coupling = cross_tiles.astype(jnp.float32)
    weights = cheb_weight.astype(jnp.float32)

    take_rows = jax.vmap(lambda values, rows: jnp.take(values, rows, axis=1))
    add_rows = jax.vmap(lambda summed, rows, terms: summed.at[:, rows].add(terms))

    def local_forward(args):
        part_tiles, part_cols, part_values = args
        gathered = jnp.take(part_values, part_cols, axis=1).astype(jnp.float32)
        return jnp.einsum("inab,finb->fia", part_tiles.astype(jnp.float32), gathered, precision=highest)

    def local_adjoint(args):
        part_tiles, part_cols, part_values = args
        terms = jnp.einsum("inab,fia->finb", part_tiles.astype(jnp.float32), part_values.astype(jnp.float32), precision=highest)
        return jnp.zeros((F, NB, BLK), jnp.float32).at[:, part_cols].add(terms)

    def apply_forward(values):
        summed = lax.map(local_forward, (tiles, columns, values))
        for level in range(ROUNDS):
            partner = jnp.bitwise_xor(owners, 1 << level).astype(jnp.int32)
            incoming = take_rows(values, send_rows[:, level])[partner].astype(jnp.float32)
            product = jnp.einsum("nhab,nfhb->nfha", coupling[:, level], incoming, precision=highest)
            product = product * switch[:, level][:, None, None, None]
            summed = add_rows(summed, recv_rows[:, level], product)
        return summed

    def apply_adjoint(values):
        summed = lax.map(local_adjoint, (tiles, columns, values))
        for level in range(ROUNDS):
            partner = jnp.bitwise_xor(owners, 1 << level).astype(jnp.int32)
            pieces = take_rows(values, recv_rows[:, level]).astype(jnp.float32)
            terms = jnp.einsum("nhab,nfha->nfhb", coupling[:, level], pieces, precision=highest)
            terms = terms * switch[:, level][:, None, None, None]
            summed = add_rows(summed, send_rows[:, level], terms[partner])
        return summed

    zeroth = to_blocks(features) * mask_half
    first = (apply_forward(zeroth) * mask_full).astype(jnp.bfloat16)
    second = ((2.0 * apply_forward(first) - zeroth.astype(jnp.float32)) * mask_full).astype(jnp.bfloat16)
    third = ((2.0 * apply_forward(second) - first.astype(jnp.float32)) * mask_full).astype(jnp.bfloat16)
    orders = [zeroth, first, second, third]

    output = jnp.zeros((N_DOM, F, NB, BLK), jnp.float32)
    for level in range(ORDER + 1):
        output = output + jnp.einsum("fg,nfib->ngib", weights[level], orders[level].astype(jnp.float32), precision=highest)
    conv_out = from_blocks((output * mask_full).astype(jnp.bfloat16))

    upstream = (to_blocks(cotangent) * mask_half).astype(jnp.float32)
    grad_w = jnp.stack([jnp.einsum("nfib,ngib->fg", orders[level].astype(jnp.float32), upstream, precision=highest) for level in range(ORDER + 1)])
    lifted = [jnp.einsum("fg,ngib->nfib", weights[level], upstream, precision=highest) for level in range(ORDER + 1)]

    back_third = (lifted[3] * mask_full).astype(jnp.bfloat16)
    adjoint_two = lifted[2] + 2.0 * apply_adjoint(back_third)
    back_second = (adjoint_two * mask_full).astype(jnp.bfloat16)
    adjoint_one = lifted[1] + 2.0 * apply_adjoint(back_second) - back_third.astype(jnp.float32)
    back_first = (adjoint_one * mask_full).astype(jnp.bfloat16)
    adjoint_zero = lifted[0] + apply_adjoint(back_first) - back_second.astype(jnp.float32)
    grad_x = from_blocks((adjoint_zero * mask_full).astype(jnp.bfloat16))
    return (conv_out, grad_x, grad_w)
```

```python
import functools

import jax
import jax.numpy as jnp
from jax import lax
from jax.experimental import pallas as pl
from jax.experimental.pallas import tpu as pltpu
from jax.sharding import PartitionSpec as P

F32 = jnp.float32
BF16 = jnp.bfloat16
SUB = 8
LANES = 128
UNROLL = 4

VMEM = pl.BlockSpec(memory_space=pltpu.VMEM)
SMEM = pl.BlockSpec(memory_space=pltpu.SMEM)
ANY = pl.BlockSpec(memory_space=pl.ANY)


def shape(dims, dtype):
    return jax.ShapeDtypeStruct(dims, dtype)


def nt(a, b):
    return lax.dot_general(a, b, (((1,), (1,)), ((), ())), preferred_element_type=F32)


def nn(a, b):
    return lax.dot_general(a, b, (((1,), (0,)), ((), ())), preferred_element_type=F32)


class Sizes:
    def __init__(self, features, lap_tiles, cross_tiles):
        self.chan = features.shape[0]
        self.blocks, self.nz, self.blk = lap_tiles.shape[:3]
        self.rounds, self.hb = cross_tiles.shape[1:3]
        self.pairs = self.rounds * self.hb
        self.rows = 0
        self.sends = self.pairs
        self.first_row = 2 * self.pairs
        self.first_send = 3 * self.pairs
        self.flags = 4 * self.pairs
        self.live = self.flags + self.rounds
        self.meta = self.live + 1
        self.half = self.hb * self.chan

    def couplings(self):
        return [(r, h, r * self.hb + h) for r in range(self.rounds) for h in range(self.hb)]


def call(kernel, in_specs, out_specs, out_shape, scratch, flops, moved, limit, name):
    return pl.pallas_call(
        kernel,
        in_specs=in_specs,
        out_specs=out_specs,
        out_shape=out_shape,
        scratch_shapes=scratch,
        compiler_params=pltpu.CompilerParams(vmem_limit_bytes=limit << 20),
        cost_estimate=pl.CostEstimate(flops=flops, bytes_accessed=moved, transcendentals=0),
        name=name,
    )


def pack_kernel(sz, *refs):
    x4, u4, cross, send, row, pair, live = refs[:7]
    xb, ub, meta = refs[7:10]
    pays = refs[10 : 10 + sz.rounds]
    sem_x, sem_u, sem_t = refs[10 + sz.rounds :]
    copies = []
    for t in range(sz.chan // SUB):
        rows = pl.ds(t * SUB, SUB)
        copies.append(pltpu.make_async_copy(x4.at[t], xb.at[:, rows, :], sem_x.at[t]))
        copies.append(pltpu.make_async_copy(u4.at[t], ub.at[:, rows, :], sem_u.at[t]))
    tiles = []
    for r, h, j in sz.couplings():
        spot = pays[r].at[pl.ds(2 * sz.half + h * sz.blk, sz.blk), :]
        tiles.append(pltpu.make_async_copy(cross.at[0, r, h], spot, sem_t.at[j]))
    for copy in copies + tiles:
        copy.start()
    count = live[0]
    rows = [lax.rem(row[0, r, h], count) for r, h, _ in sz.couplings()]
    sends = [lax.rem(send[0, r, h], count) for r, h, _ in sz.couplings()]
    for values, spot, first in (
        (rows, sz.rows, sz.first_row),
        (sends, sz.sends, sz.first_send),
    ):
        for j, value in enumerate(values):
            earliest = jnp.int32(j)
            for q in reversed(range(j)):
                earliest = jnp.where(values[q] == value, q, earliest)
            meta[spot + j] = value
            meta[first + j] = earliest
    for r in range(sz.rounds):
        meta[sz.flags + r] = pair[0, r]
    meta[sz.live] = count
    for copy in copies:
        copy.wait()

    def clear(i, carry):
        xb[i] = jnp.zeros(xb.shape[1:], BF16)
        ub[i] = jnp.zeros(ub.shape[1:], BF16)
        return carry

    lax.fori_loop(count, sz.blocks, clear, 0)
    for r, h, j in sz.couplings():
        pays[r][pl.ds(h * sz.chan, sz.chan), :] = xb[sends[j]]
        pays[r][pl.ds(sz.half + h * sz.chan, sz.chan), :] = ub[rows[j]]
    for r, h, j in sz.couplings():
        tiles[j].wait()

        @pl.when(pair[0, r] == 0)
        def _():
            spot = pl.ds(2 * sz.half + h * sz.blk, sz.blk)
            pays[r][spot, :] = jnp.zeros((sz.blk, sz.blk), BF16)


def pack(sz, x4, u4, cross, send, row, pair, live):
    field = shape((sz.blocks, sz.chan, sz.blk), BF16)
    pay = shape((2 * sz.half + sz.hb * sz.blk, sz.blk), BF16)
    outs = [field, field, shape((sz.meta,), jnp.int32)] + [pay] * sz.rounds
    groups = sz.chan // SUB
    return call(
        functools.partial(pack_kernel, sz),
        [ANY, ANY, ANY, SMEM, SMEM, SMEM, SMEM],
        [VMEM, VMEM, SMEM] + [VMEM] * sz.rounds,
        outs,
        [
            pltpu.SemaphoreType.DMA((groups,)),
            pltpu.SemaphoreType.DMA((groups,)),
            pltpu.SemaphoreType.DMA((sz.pairs,)),
        ],
        1000,
        4 << 20,
        8,
        "pack",
    )(x4, u4, cross, send, row, pair, live)


def local_kernel(sz, first, grad, *refs):
    refs = list(refs)
    meta, col, tiles, tcur, scur = refs[:5]
    refs = refs[5:]
    tprev = sprev = None
    if not first:
        tprev, sprev = refs[:2]
        refs = refs[2:]
    tnew, snew, psel, qsel = refs[:4]
    refs = refs[4:]
    if grad:
        gram = refs[0]
        refs = refs[1:]
    held, summed = refs
    count = meta[sz.live]
    steps = (count + UNROLL - 1) // UNROLL

    def clear(i, carry):
        summed[i] = jnp.zeros(summed.shape[1:], F32)
        return carry

    lax.fori_loop(0, sz.blocks, clear, 0, unroll=4)

    def block_row(i):
        cols = [col[m, i] for m in range(sz.nz)]
        wide = jnp.concatenate([tiles[i, m] for m in range(sz.nz)], axis=1)
        gathered = jnp.concatenate([tcur[c] for c in cols], axis=1)
        forward = nt(gathered, wide)
        if not first:
            forward = 2.0 * forward - tprev[i].astype(F32)
        held[i] = forward
        tnew[i] = forward.astype(BF16)
        terms = nn(scur[i], wide)
        for m in range(sz.nz):
            summed[cols[m]] = summed[cols[m]] + terms[:, m * sz.blk : (m + 1) * sz.blk]

    def step(g, carry):
        for u in range(UNROLL):
            block_row(g * UNROLL + u)
        return carry

    lax.fori_loop(0, steps, step, 0)

    def adjoint(i):
        total = summed[i]
        if not first:
            total = 2.0 * total - sprev[i].astype(F32)
        return total

    def finish(g, carry):
        for u in range(UNROLL):
            i = g * UNROLL + u
            snew[i] = adjoint(i).astype(BF16)
        return carry

    lax.fori_loop(0, steps, finish, 0)

    def dead(i, carry):
        tnew[i] = jnp.zeros(tnew.shape[1:], BF16)
        snew[i] = jnp.zeros(snew.shape[1:], BF16)
        return carry

    lax.fori_loop(count, sz.blocks, dead, 0)
    for j in range(sz.pairs):
        psel[j] = held[meta[sz.rows + j]]
        qsel[j] = adjoint(meta[sz.sends + j])
    if grad:

        def products(g, total):
            for u in range(0, UNROLL, 2):
                i = g * UNROLL + u
                left = [jnp.concatenate([tprev[k], tcur[k]], axis=0) for k in (i, i + 1)]
                right = [jnp.concatenate([sprev[k], scur[k]], axis=0) for k in (i, i + 1)]
                total = total + nt(jnp.concatenate(left, axis=1), jnp.concatenate(right, axis=1))
            return total

        side = 2 * sz.chan
        gram[...] = lax.fori_loop(0, steps, products, jnp.zeros((side, side), F32))


def local_products(sz, meta, col, tiles, tcur, scur, tprev=None, sprev=None, grad=False):
    first = tprev is None
    field = shape((sz.blocks, sz.chan, sz.blk), BF16)
    picked = shape((sz.pairs, sz.chan, sz.blk), F32)
    outs = [field, field, picked, picked]
    if grad:
        outs.append(shape((2 * sz.chan, 2 * sz.chan), F32))
    args = [meta, col, tiles, tcur, scur] + ([] if first else [tprev, sprev])
    return call(
        functools.partial(local_kernel, sz, first, grad),
        [SMEM, SMEM] + [VMEM] * (len(args) - 2),
        [VMEM] * len(outs),
        outs,
        [pltpu.VMEM((sz.blocks, sz.chan, sz.blk), F32)] * 2,
        4 * sz.blocks * sz.nz * sz.chan * sz.blk * sz.blk,
        12 << 20,
        24,
        "local",
    )(*args)


def add_coupled(sz, scale, meta, got, tiles, cross, psel, qsel, pacc, qacc):
    for j in range(sz.pairs):
        pacc[j] = psel[j]
        qacc[j] = qsel[j]
    for r, h, j in sz.couplings():
        factor = scale * meta[sz.flags + r].astype(F32)
        term = nt(got[r][pl.ds(h * sz.chan, sz.chan), :], cross[0, r, h])
        spot = meta[sz.first_row + j]
        pacc[spot] = pacc[spot] + factor * term
        term = nn(
            got[r][pl.ds(sz.half + h * sz.chan, sz.chan), :],
            tiles[r][pl.ds(2 * sz.half + h * sz.blk, sz.blk), :],
        )
        spot = meta[sz.first_send + j]
        qacc[spot] = qacc[spot] + scale * term


def patch(sz, meta, tbase, sbase, tnew, snew, pacc, qacc):
    def move(i, carry):
        tnew[i] = tbase[i]
        snew[i] = sbase[i]
        return carry

    lax.fori_loop(0, sz.blocks, move, 0, unroll=4)
    for j in range(sz.pairs):
        tnew[meta[sz.rows + j]] = pacc[meta[sz.first_row + j]].astype(BF16)
        snew[meta[sz.sends + j]] = qacc[meta[sz.first_send + j]].astype(BF16)


def join_kernel(sz, scale, grad, *refs):
    refs = list(refs)
    meta, cross, tbase, sbase, psel, qsel = refs[:6]
    refs = refs[6:]
    got, refs = refs[: sz.rounds], refs[sz.rounds :]
    tiles, refs = refs[: sz.rounds], refs[sz.rounds :]
    if grad:
        gram, sold = refs[:2]
        refs = refs[2:]
    tnew, snew = refs[:2]
    refs = refs[2:]
    pays, refs = refs[: sz.rounds], refs[sz.rounds :]
    if grad:
        partial, refs = refs[0], refs[1:]
    pacc, qacc = refs
    add_coupled(sz, scale, meta, got, tiles, cross, psel, qsel, pacc, qacc)
    patch(sz, meta, tbase, sbase, tnew, snew, pacc, qacc)
    for r, h, j in sz.couplings():
        pays[r][pl.ds(h * sz.chan, sz.chan), :] = tnew[meta[sz.sends + j]]
        pays[r][pl.ds(sz.half + h * sz.chan, sz.chan), :] = snew[meta[sz.rows + j]]
    if grad:
        count = meta[sz.live]
        steps = (count + UNROLL - 1) // UNROLL

        def products(g, total):
            for u in range(0, UNROLL, 2):
                i = g * UNROLL + u
                left = jnp.concatenate([tnew[i], tnew[i + 1]], axis=1)
                right = jnp.concatenate([sold[i], sold[i + 1]], axis=1)
                total = total + nt(left, right)
            return total

        last = lax.fori_loop(0, steps, products, jnp.zeros((sz.chan, sz.chan), F32))
        partial[...] = gram[...]
        partial[pl.ds(0, sz.chan), pl.ds(sz.chan, sz.chan)] = last


def join(sz, scale, meta, cross, tbase, sbase, psel, qsel, got, tiles, gram=None, sold=None):
    field = shape((sz.blocks, sz.chan, sz.blk), BF16)
    pay = shape((2 * sz.half, sz.blk), BF16)
    outs = [field, field] + [pay] * sz.rounds
    args = [meta, cross, tbase, sbase, psel, qsel, *got, *tiles]
    if gram is not None:
        args += [gram, sold]
        outs.append(shape(gram.shape, F32))
    outs = call(
        functools.partial(join_kernel, sz, scale, gram is not None),
        [SMEM] + [VMEM] * (len(args) - 1),
        [VMEM] * len(outs),
        outs,
        [pltpu.VMEM((sz.pairs, sz.chan, sz.blk), F32)] * 2,
        4 * sz.pairs * sz.chan * sz.blk * sz.blk,
        6 << 20,
        12,
        "join",
    )(*args)
    tail = outs[2 + sz.rounds :]
    return outs[0], outs[1], outs[2 : 2 + sz.rounds], tail


def output_kernel(sz, *refs):
    refs = list(refs)
    meta, cross, weight, tbase, sbase, psel, qsel = refs[:7]
    refs = refs[7:]
    got, refs = refs[: sz.rounds], refs[sz.rounds :]
    tiles, refs = refs[: sz.rounds], refs[sz.rounds :]
    t0, t1, t2, s0, s1, s2, out4, grad4, tlast, slast, pacc, qacc = refs
    add_coupled(sz, 2.0, meta, got, tiles, cross, psel, qsel, pacc, qacc)
    patch(sz, meta, tbase, sbase, tlast, slast, pacc, qacc)
    count = meta[sz.live]
    steps = (count + UNROLL - 1) // UNROLL
    orders = weight.shape[0]
    back = jnp.concatenate([weight[k].astype(F32) for k in range(orders)], axis=1).astype(BF16)
    ahead = jnp.concatenate([weight[k].astype(F32).T for k in range(orders)], axis=1).astype(BF16)
    groups = sz.chan // SUB

    def block(i):
        field = jnp.concatenate([t[i] for t in (t0, t1, t2, tlast)], axis=0)
        value = nn(ahead, field).astype(BF16)
        for t in range(groups):
            out4[t, i] = value[t * SUB : (t + 1) * SUB]
        field = jnp.concatenate([s[i] for s in (s0, s1, s2, slast)], axis=0)
        value = nn(back, field).astype(BF16)
        for t in range(groups):
            grad4[t, i] = value[t * SUB : (t + 1) * SUB]

    def step(g, carry):
        for u in range(UNROLL):
            block(g * UNROLL + u)
        return carry

    lax.fori_loop(0, steps, step, 0)

    def dead(i, carry):
        for t in range(groups):
            out4[t, i] = jnp.zeros((SUB, sz.blk), BF16)
            grad4[t, i] = jnp.zeros((SUB, sz.blk), BF16)
        return carry

    lax.fori_loop(count, sz.blocks, dead, 0)


def outputs(sz, meta, cross, weight, tbase, sbase, psel, qsel, got, tiles, fields):
    out = shape((sz.chan // SUB, sz.blocks, SUB, sz.blk), BF16)
    args = [meta, cross, weight, tbase, sbase, psel, qsel, *got, *tiles, *fields]
    return call(
        functools.partial(output_kernel, sz),
        [SMEM] + [VMEM] * (len(args) - 1),
        [VMEM] * 2,
        [out, out],
        [pltpu.VMEM((sz.blocks, sz.chan, sz.blk), BF16)] * 2
        + [pltpu.VMEM((sz.pairs, sz.chan, sz.blk), F32)] * 2,
        16 * sz.blocks * sz.chan * sz.chan * sz.blk,
        10 << 20,
        16,
        "outputs",
    )(*args)


def add_kernel(mine, theirs, out):
    out[...] = mine[...] + theirs[...]


def add(mine, theirs):
    return call(
        add_kernel,
        [VMEM, VMEM],
        VMEM,
        shape(mine.shape, F32),
        [],
        mine.size,
        12 * mine.size,
        2,
        "add",
    )(mine, theirs)


def weight_kernel(chan, gram, out):
    top, low = pl.ds(0, chan), pl.ds(chan, chan)
    zeroth, first = gram[top, top], gram[low, top]
    out[0] = zeroth
    out[1] = first
    out[2] = 2.0 * gram[low, low] - zeroth
    out[3] = 2.0 * gram[top, low] - first


def weight_gradient(sz, gram):
    return call(
        functools.partial(weight_kernel, sz.chan),
        [VMEM],
        VMEM,
        shape((4, sz.chan, sz.chan), F32),
        [],
        gram.size,
        8 * gram.size,
        2,
        "weight",
    )(gram)


def from_partner(values, bit):
    count = lax.axis_size("dom")
    route = []
    for low in range(count):
        high = low | 1 << bit
        if high != low and high < count:
            route += [(low, high), (high, low)]
    return lax.ppermute(values, "dom", route)


def total_over_devices(gram):
    count = lax.axis_size("dom")
    if count & (count - 1):
        return lax.psum(gram, "dom")
    for bit in range(count.bit_length() - 1):
        gram = add(gram, from_partner(gram, bit))
    return gram


def local(
    features,
    cheb_weight,
    lap_tiles,
    col_index,
    cross_tiles,
    send_index,
    row_index,
    pair_on,
    blk_live,
    cotangent,
):
    sz = Sizes(features, lap_tiles, cross_tiles)
    split = (sz.chan // SUB, SUB, sz.blocks, sz.blk)
    x4 = features.reshape(split).transpose(0, 2, 1, 3)
    u4 = cotangent.reshape(split).transpose(0, 2, 1, 3)
    col = col_index.T

    packed = pack(sz, x4, u4, cross_tiles, send_index, row_index, pair_on, blk_live)
    t0, s0, meta = packed[:3]
    tiles = [from_partner(pay, bit) for bit, pay in enumerate(packed[3:])]
    t1, s1, psel, qsel = local_products(sz, meta, col, lap_tiles, t0, s0)
    t1, s1, pays, _ = join(sz, 1.0, meta, cross_tiles, t1, s1, psel, qsel, tiles, tiles)

    got = [from_partner(pay, bit) for bit, pay in enumerate(pays)]
    t2, s2, psel, qsel, gram = local_products(
        sz, meta, col, lap_tiles, t1, s1, t0, s0, grad=True
    )
    t2, s2, pays, tail = join(
        sz, 2.0, meta, cross_tiles, t2, s2, psel, qsel, got, tiles, gram, s1
    )

    got = [from_partner(pay, bit) for bit, pay in enumerate(pays)]
    grad_w = weight_gradient(sz, total_over_devices(tail[0]))
    t3, s3, psel, qsel = local_products(sz, meta, col, lap_tiles, t2, s2, t1, s1)
    out4, grad4 = outputs(
        sz, meta, cross_tiles, cheb_weight, t3, s3, psel, qsel, got, tiles, (t0, t1, t2, s0, s1, s2)
    )
    conv_out = out4.transpose(0, 2, 1, 3).reshape(features.shape)
    grad_x = grad4.transpose(0, 2, 1, 3).reshape(features.shape)
    return (conv_out, grad_x, grad_w)


def solution(mesh):
    in_specs = (
        P(None, "dom"),
        P(),
        P("dom", None, None, None),
        P("dom", None),
        P("dom", None, None, None, None),
        P("dom", None, None),
        P("dom", None, None),
        P("dom", None),
        P("dom"),
        P(None, "dom"),
    )
    out_specs = (P(None, "dom"), P(None, "dom"), P())
    return jax.shard_map(local, mesh=mesh, in_specs=in_specs, out_specs=out_specs, check_vma=False)
```

```python
import functools

import jax
import jax.numpy as jnp
from jax import lax
from jax.experimental import pallas as pl
from jax.experimental.pallas import tpu as pltpu
from jax.sharding import PartitionSpec as P

F32 = jnp.float32
BF16 = jnp.bfloat16
SUB = 8
LANES = 128
ROWS_FIRST = 8
ROWS = 16

VMEM = pl.BlockSpec(memory_space=pltpu.VMEM)
SMEM = pl.BlockSpec(memory_space=pltpu.SMEM)
HBM = pl.BlockSpec(memory_space=pltpu.HBM)
TOKEN = jax.ShapeDtypeStruct((SUB, LANES), F32)


def shape(dims, dtype):
    return jax.ShapeDtypeStruct(dims, dtype)


def nn(a, b):
    return lax.dot_general(a, b, (((1,), (0,)), ((), ())), preferred_element_type=F32)


class Sizes:
    def __init__(self, features, lap_tiles, cross_tiles):
        self.chan = features.shape[0]
        self.blocks, self.nz, self.blk = lap_tiles.shape[:3]
        self.rounds, self.hb = cross_tiles.shape[1:3]
        self.pairs = self.rounds * self.hb
        self.rows = 0
        self.sends = self.pairs
        self.first_row = 2 * self.pairs
        self.first_send = 3 * self.pairs
        self.flags = 4 * self.pairs
        self.live = self.flags + self.rounds
        self.meta = self.live + 1
        self.half = self.hb * self.chan
        self.field = shape((self.blocks, self.chan, self.blk), BF16)
        self.picked = shape((self.pairs, self.chan, self.blk), F32)
        self.pay = shape((2 * self.half, self.blk), BF16)

    def couplings(self):
        return [(r, h, r * self.hb + h) for r in range(self.rounds) for h in range(self.hb)]

    def forward_part(self, h):
        return pl.ds(h * self.chan, self.chan)

    def adjoint_part(self, h):
        return pl.ds(self.half + h * self.chan, self.chan)


def call(kernel, in_specs, out_specs, out_shape, scratch, flops, moved, limit, name, aliases=None):
    return pl.pallas_call(
        kernel,
        in_specs=in_specs,
        out_specs=out_specs,
        out_shape=out_shape,
        scratch_shapes=scratch,
        input_output_aliases=aliases or {},
        compiler_params=pltpu.CompilerParams(vmem_limit_bytes=limit << 20),
        cost_estimate=pl.CostEstimate(flops=flops, bytes_accessed=moved, transcendentals=0),
        name=name,
    )


def fill_pays(sz, meta, tnew, snew, cross, pays):
    for r, h, j in sz.couplings():
        pays[r][sz.forward_part(h), :] = tnew[meta[sz.sends + j]]
        term = nn(snew[meta[sz.rows + j]], cross[j])
        factor = meta[sz.flags + r].astype(F32)
        pays[r][sz.adjoint_part(h), :] = (factor * term).astype(BF16)


def pack_kernel(sz, *refs):
    x4, u4, coupling, send, row, pair, live, col = refs[:8]
    xb, ub, cross, meta, col_out = refs[8:13]
    pays = refs[13 : 13 + sz.rounds]
    send_s, row_s, pair_s, live_s, sem_x, sem_u, sem_t, sem_i = refs[13 + sz.rounds :]
    small = [
        pltpu.make_async_copy(send, send_s, sem_i.at[0]),
        pltpu.make_async_copy(row, row_s, sem_i.at[1]),
        pltpu.make_async_copy(pair, pair_s, sem_i.at[2]),
        pltpu.make_async_copy(live, live_s, sem_i.at[3]),
    ]
    copies = []
    for t in range(sz.chan // SUB):
        part = pl.ds(t * SUB, SUB)
        copies.append(pltpu.make_async_copy(x4.at[t], xb.at[:, part, :], sem_x.at[t]))
        copies.append(pltpu.make_async_copy(u4.at[t], ub.at[:, part, :], sem_u.at[t]))
    copies.append(pltpu.make_async_copy(coupling, cross, sem_t))
    copies.append(pltpu.make_async_copy(col, col_out, sem_i.at[4]))
    for copy in small + copies:
        copy.start()
    for copy in small:
        copy.wait()
    count = live_s[0]
    rows = [lax.rem(row_s[0, h, r], count) for r, h, _ in sz.couplings()]
    sends = [lax.rem(send_s[0, h, r], count) for r, h, _ in sz.couplings()]
    for values, spot, first in (
        (rows, sz.rows, sz.first_row),
        (sends, sz.sends, sz.first_send),
    ):
        for j, value in enumerate(values):
            earliest = jnp.int32(j)
            for q in reversed(range(j)):
                earliest = jnp.where(values[q] == value, q, earliest)
            meta[spot + j] = value
            meta[first + j] = earliest
    for r in range(sz.rounds):
        meta[sz.flags + r] = pair_s[0, r]
    meta[sz.live] = count
    for copy in copies:
        copy.wait()

    def clear(i, carry):
        xb[i] = jnp.zeros(xb.shape[1:], BF16)
        ub[i] = jnp.zeros(ub.shape[1:], BF16)
        return carry

    lax.fori_loop(count, sz.blocks, clear, 0)
    fill_pays(sz, meta, xb, ub, cross, pays)


def pack(sz, x4, u4, coupling, send, row, pair, live, col):
    groups = sz.chan // SUB
    cross = shape((sz.pairs, sz.blk, sz.blk), BF16)
    table = shape((sz.meta,), jnp.int32)
    return call(
        functools.partial(pack_kernel, sz),
        [HBM] * 8,
        [VMEM, VMEM, VMEM, SMEM, VMEM] + [VMEM] * sz.rounds,
        [sz.field, sz.field, cross, table, shape(col.shape, jnp.int32)] + [sz.pay] * sz.rounds,
        [
            pltpu.SMEM(send.shape, jnp.int32),
            pltpu.SMEM(row.shape, jnp.int32),
            pltpu.SMEM(pair.shape, jnp.int32),
            pltpu.SMEM(live.shape, jnp.int32),
            pltpu.SemaphoreType.DMA((groups,)),
            pltpu.SemaphoreType.DMA((groups,)),
            pltpu.SemaphoreType.DMA,
            pltpu.SemaphoreType.DMA((5,)),
        ],
        1000,
        4 << 20,
        8,
        "pack",
    )(x4, u4, coupling, send, row, pair, live, col)


def big_steps(count):
    return (count + ROWS - 1) // ROWS


def clear_sums(sz, summed):
    def clear(i, carry):
        summed[i] = jnp.zeros(summed.shape[1:], F32)
        return carry

    lax.fori_loop(0, sz.blocks, clear, 0, unroll=4)


def scatter_terms(sz, summed, cols, terms):
    for m in range(sz.nz):
        summed[cols[m]] = summed[cols[m]] + terms[:, m * sz.blk : (m + 1) * sz.blk]


def finish_local(sz, meta, held, adjoint, tnew, snew, psel, qsel):
    count = meta[sz.live]

    def finish(g, carry):
        for u in range(ROWS_FIRST):
            i = g * ROWS_FIRST + u
            snew[i] = adjoint(i).astype(BF16)
        return carry

    lax.fori_loop(0, (count + ROWS_FIRST - 1) // ROWS_FIRST, finish, 0)

    def dead(i, carry):
        tnew[i] = jnp.zeros(tnew.shape[1:], BF16)
        snew[i] = jnp.zeros(snew.shape[1:], BF16)
        return carry

    lax.fori_loop(count, sz.blocks, dead, 0)
    for j in range(sz.pairs):
        psel[j] = held[meta[sz.rows + j]]
        qsel[j] = adjoint(meta[sz.sends + j])


def first_kernel(
    sz, meta, col, tiles_hbm, t0, s0, tnew, snew, psel, qsel, tiles, turned, held, summed, sem
):
    count = meta[sz.live]
    steps = big_steps(count) * (ROWS // ROWS_FIRST)

    def fetch(g):
        part = pl.ds(g * ROWS_FIRST, ROWS_FIRST)
        return pltpu.make_async_copy(tiles_hbm.at[part], tiles.at[part], sem.at[g])

    def start(g, carry):
        fetch(g).start()
        return carry

    lax.fori_loop(0, steps, start, 0)
    clear_sums(sz, summed)

    def block_row(i):
        cols = [col[m, i] for m in range(sz.nz)]
        parts = [tiles[i, m] for m in range(sz.nz)]
        flipped = [part.T for part in parts]
        for m in range(sz.nz):
            turned[i, pl.ds(m * sz.blk, sz.blk), :] = flipped[m]
        gathered = jnp.concatenate([t0[c] for c in cols], axis=1)
        forward = nn(gathered, jnp.concatenate(flipped, axis=0))
        held[i] = forward
        tnew[i] = forward.astype(BF16)
        scatter_terms(sz, summed, cols, nn(s0[i], jnp.concatenate(parts, axis=1)))

    def step(g, carry):
        fetch(g).wait()
        for u in range(ROWS_FIRST):
            block_row(g * ROWS_FIRST + u)
        return carry

    lax.fori_loop(0, steps, step, 0)
    finish_local(sz, meta, held, lambda i: summed[i], tnew, snew, psel, qsel)


def first_products(sz, meta, col, tiles, t0, s0):
    turned = shape((sz.blocks, sz.nz * sz.blk, sz.blk), BF16)
    return call(
        functools.partial(first_kernel, sz),
        [SMEM, SMEM, HBM, VMEM, VMEM],
        [VMEM] * 6,
        [sz.field, sz.field, sz.picked, sz.picked, shape(tiles.shape, BF16), turned],
        [pltpu.VMEM((sz.blocks, sz.chan, sz.blk), F32)] * 2
        + [pltpu.SemaphoreType.DMA((sz.blocks // ROWS_FIRST,))],
        4 * sz.blocks * sz.nz * sz.chan * sz.blk * sz.blk,
        12 << 20,
        24,
        "first",
    )(meta, col, tiles, t0, s0)


def local_kernel(sz, grad, *refs):
    meta, col, tiles, turned, tcur, scur, tprev, sprev, _ = refs[:9]
    tnew, snew, psel, qsel, last = refs[9:14]
    held, summed = refs[-2:]
    count = meta[sz.live]
    clear_sums(sz, summed)

    def block_row(i):
        cols = [col[m, i] for m in range(sz.nz)]
        gathered = jnp.concatenate([tcur[c] for c in cols], axis=1)
        forward = 2.0 * nn(gathered, turned[i]) - tprev[i].astype(F32)
        held[i] = forward
        tnew[i] = forward.astype(BF16)
        wide = jnp.concatenate([tiles[i, m] for m in range(sz.nz)], axis=1)
        scatter_terms(sz, summed, cols, nn(scur[i], wide))

    def step(g, carry):
        for u in range(ROWS):
            block_row(g * ROWS + u)
        return carry

    lax.fori_loop(0, big_steps(count), step, 0)

    def adjoint(i):
        return 2.0 * summed[i] - sprev[i].astype(F32)

    finish_local(sz, meta, held, adjoint, tnew, snew, psel, qsel)
    if not grad:
        last[...] = jnp.zeros(last.shape, F32)
        return

    def products(g, total):
        left, right = [], []
        for u in range(ROWS_FIRST):
            i = g * ROWS_FIRST + u
            left.append(jnp.concatenate([tprev[i], tcur[i], tnew[i]], axis=0))
            right.append(jnp.concatenate([sprev[i], scur[i]], axis=0).T)
        return total + nn(jnp.concatenate(left, axis=1), jnp.concatenate(right, axis=0))

    steps = (count + ROWS_FIRST - 1) // ROWS_FIRST
    last[...] = lax.fori_loop(0, steps, products, jnp.zeros(last.shape, F32))


def local_products(sz, meta, col, tiles, turned, fields, token, grad):
    tail = shape((3 * sz.chan, 2 * sz.chan), F32) if grad else TOKEN
    return call(
        functools.partial(local_kernel, sz, grad),
        [SMEM, SMEM] + [VMEM] * 7,
        [VMEM] * 5,
        [sz.field, sz.field, sz.picked, sz.picked, tail],
        [pltpu.VMEM((sz.blocks, sz.chan, sz.blk), F32)] * 2,
        4 * sz.blocks * sz.nz * sz.chan * sz.blk * sz.blk,
        12 << 20,
        24,
        "local",
    )(meta, col, tiles, turned, *fields, token)


def add_coupled(sz, scale, meta, got, cross, psel, qsel, pacc, qacc):
    for j in range(sz.pairs):
        pacc[j] = psel[j]
        qacc[j] = qsel[j]
    terms = []
    for r, h, j in sz.couplings():
        factor = scale * meta[sz.flags + r].astype(F32)
        terms.append(factor * nn(got[r][sz.forward_part(h), :], cross[j].T))
        spot = meta[sz.first_row + j]
        pacc[spot] = pacc[spot] + terms[j]
        spot = meta[sz.first_send + j]
        qacc[spot] = qacc[spot] + scale * got[r][sz.adjoint_part(h), :].astype(F32)
    return terms


def join_kernel(sz, scale, grad, *refs):
    refs = list(refs)
    meta, cross, tbase, sbase, psel, qsel = refs[:6]
    got, refs = refs[6 : 6 + sz.rounds], refs[6 + sz.rounds :]
    if grad:
        gram, sold = refs[:2]
        refs = refs[2:]
    tnew, snew = refs[:2]
    pays, refs = refs[2 : 2 + sz.rounds], refs[2 + sz.rounds :]
    if grad:
        partial, refs = refs[0], refs[1:]
    pacc, qacc = refs
    terms = add_coupled(sz, scale, meta, got, cross, psel, qsel, pacc, qacc)

    def move(i, carry):
        tnew[i] = tbase[i]
        snew[i] = sbase[i]
        return carry

    lax.fori_loop(0, sz.blocks, move, 0, unroll=4)
    for j in range(sz.pairs):
        tnew[meta[sz.rows + j]] = pacc[meta[sz.first_row + j]].astype(BF16)
        snew[meta[sz.sends + j]] = qacc[meta[sz.first_send + j]].astype(BF16)
    fill_pays(sz, meta, tnew, snew, cross, pays)
    if grad:
        left = jnp.concatenate([term.astype(BF16) for term in terms], axis=1)
        right = [sold[meta[sz.rows + j]].T for j in range(sz.pairs)]
        extra = nn(left, jnp.concatenate(right, axis=0))
        one, two, three = (pl.ds(k * sz.chan, sz.chan) for k in range(3))
        partial[one, one] = gram[one, one]
        partial[two, :] = gram[two, :]
        partial[one, two] = gram[three, two] + extra


def join(sz, scale, meta, cross, base, got, gram=None, sold=None):
    outs = [sz.field, sz.field] + [sz.pay] * sz.rounds
    args = [meta, cross, *base, *got]
    if gram is not None:
        args += [gram, sold]
        outs.append(shape((2 * sz.chan, 2 * sz.chan), F32))
    outs = call(
        functools.partial(join_kernel, sz, scale, gram is not None),
        [SMEM] + [VMEM] * (len(args) - 1),
        [VMEM] * len(outs),
        outs,
        [pltpu.VMEM(sz.picked.shape, F32)] * 2,
        4 * sz.pairs * sz.chan * sz.blk * sz.blk,
        6 << 20,
        12,
        "join",
    )(*args)
    return outs[0], outs[1], outs[2 : 2 + sz.rounds], outs[2 + sz.rounds :]


def output_weights(weight):
    wide = [weight[k].astype(F32) for k in range(weight.shape[0])]
    ahead = jnp.concatenate([w.T for w in wide], axis=1).astype(BF16)
    back = jnp.concatenate(wide, axis=1).astype(BF16)
    return ahead, back


def output_kernel(sz, low, high, *refs):
    meta, weight = refs[:2]
    forward, adjoint = refs[2:6], refs[6:10]
    refs = refs[11:] if low == 0 else refs[13:]
    out4, grad4, token, held_out, held_grad, sem = refs
    count = meta[sz.live]
    ahead, back = output_weights(weight)
    groups = sz.chan // SUB

    def block(i):
        for left, fields, held in ((ahead, forward, held_out), (back, adjoint, held_grad)):
            value = nn(left, jnp.concatenate([f[i] for f in fields], axis=0)).astype(BF16)
            for t in range(groups):
                held[t, i - low] = value[t * SUB : (t + 1) * SUB]

    def step(g, carry):
        for u in range(ROWS_FIRST):
            block(g * ROWS_FIRST + u)
        return carry

    end = jnp.minimum((count + ROWS_FIRST - 1) // ROWS_FIRST, high // ROWS_FIRST)
    lax.fori_loop(low // ROWS_FIRST, end, step, 0)

    def dead(i, carry):
        for t in range(groups):
            held_out[t, i - low] = jnp.zeros((SUB, sz.blk), BF16)
            held_grad[t, i - low] = jnp.zeros((SUB, sz.blk), BF16)
        return carry

    lax.fori_loop(jnp.maximum(count, low), high, dead, 0)
    part = pl.ds(low, high - low)
    copies = [
        pltpu.make_async_copy(held_out, out4.at[:, part], sem.at[0]),
        pltpu.make_async_copy(held_grad, grad4.at[:, part], sem.at[1]),
    ]
    for copy in copies:
        copy.start()
    token[...] = jnp.zeros(token.shape, F32)
    for copy in copies:
        copy.wait()


def base_outputs(sz, low, high, meta, weight, forward, adjoint, token, before):
    out = shape((sz.chan // SUB, sz.blocks, SUB, sz.blk), BF16)
    args = [meta, weight, *forward, *adjoint, token]
    specs = [SMEM] + [VMEM] * (len(args) - 1)
    aliases = {}
    if low > 0:
        aliases = {len(args): 0, len(args) + 1: 1}
        args += before
        specs += [HBM] * 2
    held = pltpu.VMEM((sz.chan // SUB, high - low, SUB, sz.blk), BF16)
    return call(
        functools.partial(output_kernel, sz, low, high),
        specs,
        [HBM, HBM, VMEM],
        [out, out, TOKEN],
        [held, held, pltpu.SemaphoreType.DMA((2,))],
        16 * (high - low) * sz.chan * sz.chan * sz.blk,
        10 << 20,
        8,
        "outputs",
        aliases,
    )(*args)


def fix_kernel(sz, *refs):
    meta, cross, weight, psel, qsel = refs[:5]
    got, refs = refs[5 : 5 + sz.rounds], refs[5 + sz.rounds :]
    forward, adjoint = refs[:3], refs[3:6]
    mine, theirs = refs[6:8]
    out4, grad4, grad_w, pacc, qacc, held_out, held_grad, sem = refs[10:]
    add_coupled(sz, 2.0, meta, got, cross, psel, qsel, pacc, qacc)
    ahead, back = output_weights(weight)
    groups = sz.chan // SUB
    copies = []
    for j in range(sz.pairs):
        for left, fields, last, spot, first, held, out, s in (
            (ahead, forward, pacc, sz.rows, sz.first_row, held_out, out4, 0),
            (back, adjoint, qacc, sz.sends, sz.first_send, held_grad, grad4, 1),
        ):
            i, slot = meta[spot + j], meta[first + j]
            stack = [f[i] for f in fields] + [last[slot].astype(BF16)]
            value = nn(left, jnp.concatenate(stack, axis=0)).astype(BF16)
            for t in range(groups):
                held[j, t] = value[t * SUB : (t + 1) * SUB]
            copies.append((slot == j, pltpu.make_async_copy(held.at[j], out.at[:, i], sem.at[s, j])))
    for own, copy in copies:
        pl.when(own)(copy.start)
    one, two = pl.ds(0, sz.chan), pl.ds(sz.chan, sz.chan)

    def total(a, b):
        return mine[a, b] + theirs[a, b]

    zeroth, first = total(one, one), total(two, one)
    grad_w[0] = zeroth
    grad_w[1] = first
    grad_w[2] = 2.0 * total(two, two) - zeroth
    grad_w[3] = 2.0 * total(one, two) - first
    for own, copy in copies:
        pl.when(own)(copy.wait)


def fix_outputs(sz, meta, cross, weight, picked, got, forward, adjoint, mine, theirs, before):
    out = shape(before[0].shape, BF16)
    args = [meta, cross, weight, *picked, *got, *forward, *adjoint, mine, theirs]
    held = pltpu.VMEM((sz.pairs, sz.chan // SUB, SUB, sz.blk), BF16)
    return call(
        functools.partial(fix_kernel, sz),
        [SMEM] + [VMEM] * (len(args) - 1) + [HBM] * 2,
        [HBM, HBM, VMEM],
        [out, out, shape((4, sz.chan, sz.chan), F32)],
        [pltpu.VMEM(sz.picked.shape, F32)] * 2 + [held, held]
        + [pltpu.SemaphoreType.DMA((2, sz.pairs))],
        8 * sz.pairs * sz.chan * sz.blk * sz.blk,
        4 << 20,
        10,
        "fix",
        {len(args): 0, len(args) + 1: 1},
    )(*args, *before)


def add_kernel(gated, *refs):
    mine, theirs, _ = refs[:3]
    if gated:
        pay, out, token, pay_out = refs[3:]
        pay_out[...] = pay[...]
    else:
        out, token = refs[3:]
    out[...] = mine[...] + theirs[...]
    token[...] = jnp.zeros(token.shape, F32)


def add(mine, theirs, token, pay):
    outs = [shape(mine.shape, F32), TOKEN]
    args = [mine, theirs, token]
    if pay is not None:
        outs.append(shape(pay.shape, BF16))
        args.append(pay)
    return call(
        functools.partial(add_kernel, pay is not None),
        [VMEM] * len(args),
        [VMEM] * len(outs),
        outs,
        [],
        mine.size,
        12 * mine.size,
        2,
        "add",
    )(*args)


def from_partner(values, bit):
    count = lax.axis_size("dom")
    route = []
    for low in range(count):
        high = low | 1 << bit
        if high != low and high < count:
            route += [(low, high), (high, low)]
    return lax.ppermute(values, "dom", route)


def local(
    features,
    cheb_weight,
    lap_tiles,
    col_index,
    cross_tiles,
    send_index,
    row_index,
    pair_on,
    blk_live,
    cotangent,
):
    sz = Sizes(features, lap_tiles, cross_tiles)
    split = (sz.chan // SUB, SUB, sz.blocks, sz.blk)
    x4 = features.reshape(split).transpose(0, 2, 1, 3)
    u4 = cotangent.reshape(split).transpose(0, 2, 1, 3)
    coupling = cross_tiles.reshape(sz.pairs, sz.blk, sz.blk)
    send, row = send_index.transpose(0, 2, 1), row_index.transpose(0, 2, 1)

    packed = pack(sz, x4, u4, coupling, send, row, pair_on, blk_live, col_index.T)
    t0, s0, cross, meta, col = packed[:5]
    got = [from_partner(pay, bit) for bit, pay in enumerate(packed[5:])]
    *base, tiles, turned = first_products(sz, meta, col, lap_tiles, t0, s0)
    t1, s1, pays, _ = join(sz, 1.0, meta, cross, base, got)

    got = [from_partner(pay, bit) for bit, pay in enumerate(pays)]
    fields = (t1, s1, t0, s0)
    *base, gram = local_products(sz, meta, col, tiles, turned, fields, cross, True)
    t2, s2, pays, (mine,) = join(sz, 2.0, meta, cross, base, got, gram, s1)

    state = {}

    def window_products(token):
        fields = (t2, s2, t1, s1)
        *base, token = local_products(sz, meta, col, tiles, turned, fields, token, False)
        state["base"] = base
        return token

    def window_outputs(low, high):
        def window(token):
            forward = (t0, t1, t2, state["base"][0])
            adjoint = (s0, s1, s2, state["base"][1])
            out4, grad4, token = base_outputs(
                sz, low, high, meta, cheb_weight, forward, adjoint, token, state.get("outs", [])
            )
            state["outs"] = [out4, grad4]
            return token

        return window

    middle = sz.blocks // (2 * ROWS_FIRST) * ROWS_FIRST
    windows = [window_products, window_outputs(0, middle), window_outputs(middle, sz.blocks)]
    bits = list(reversed(range((lax.axis_size("dom") - 1).bit_length())))
    pays, got = list(pays), [None] * sz.rounds
    token = mine
    for at, bit in enumerate(bits):
        if bit < sz.rounds:
            got[bit] = from_partner(pays[bit], bit)
        theirs = from_partner(mine, bit)
        if at < len(windows):
            token = windows[at](token)
        if at + 1 < len(bits):
            later = bits[at + 1]
            gated = later < sz.rounds
            mine, token, *rest = add(mine, theirs, token, pays[later] if gated else None)
            if gated:
                pays[later] = rest[0]
    out4, grad4, grad_w = fix_outputs(
        sz,
        meta,
        cross,
        cheb_weight,
        state["base"][2:4],
        got,
        (t0, t1, t2),
        (s0, s1, s2),
        mine,
        theirs,
        state["outs"],
    )
    conv_out = out4.transpose(0, 2, 1, 3).reshape(features.shape)
    grad_x = grad4.transpose(0, 2, 1, 3).reshape(features.shape)
    return (conv_out, grad_x, grad_w)


def solution(mesh):
    in_specs = (
        P(None, "dom"),
        P(),
        P("dom", None, None, None),
        P("dom", None),
        P("dom", None, None, None, None),
        P("dom", None, None),
        P("dom", None, None),
        P("dom", None),
        P("dom"),
        P(None, "dom"),
    )
    out_specs = (P(None, "dom"), P(None, "dom"), P())
    return jax.shard_map(local, mesh=mesh, in_specs=in_specs, out_specs=out_specs, check_vma=False)
```

```python
import functools

import jax
import jax.numpy as jnp
from jax import lax
from jax.experimental import pallas as pl
from jax.experimental.pallas import tpu as pltpu
from jax.sharding import PartitionSpec as P

F32 = jnp.float32
BF16 = jnp.bfloat16
SUB = 8
LANES = 128
ROWS_FIRST = 8
ROWS = 16

VMEM = pl.BlockSpec(memory_space=pltpu.VMEM)
SMEM = pl.BlockSpec(memory_space=pltpu.SMEM)
HBM = pl.BlockSpec(memory_space=pltpu.HBM)
TOKEN = jax.ShapeDtypeStruct((SUB, LANES), F32)


def shape(dims, dtype):
    return jax.ShapeDtypeStruct(dims, dtype)


def nn(a, b):
    return lax.dot_general(a, b, (((1,), (0,)), ((), ())), preferred_element_type=F32)


class Sizes:
    def __init__(self, features, lap_tiles, cross_tiles):
        self.chan = features.shape[0]
        self.blocks, self.nz, self.blk = lap_tiles.shape[:3]
        self.rounds, self.hb = cross_tiles.shape[1:3]
        self.pairs = self.rounds * self.hb
        self.rows = 0
        self.sends = self.pairs
        self.first_row = 2 * self.pairs
        self.first_send = 3 * self.pairs
        self.flags = 4 * self.pairs
        self.live = self.flags + self.rounds
        self.meta = self.live + 1
        self.half = self.hb * self.chan
        self.field = shape((self.blocks, self.chan, self.blk), BF16)
        self.picked = shape((self.pairs, self.chan, self.blk), F32)
        self.pay = shape((2 * self.half, self.blk), BF16)

    def couplings(self):
        return [(r, h, r * self.hb + h) for r in range(self.rounds) for h in range(self.hb)]

    def forward_part(self, h):
        return pl.ds(h * self.chan, self.chan)

    def adjoint_part(self, h):
        return pl.ds(self.half + h * self.chan, self.chan)


def call(kernel, in_specs, out_specs, out_shape, scratch, flops, moved, limit, name, aliases=None):
    return pl.pallas_call(
        kernel,
        in_specs=in_specs,
        out_specs=out_specs,
        out_shape=out_shape,
        scratch_shapes=scratch,
        input_output_aliases=aliases or {},
        compiler_params=pltpu.CompilerParams(vmem_limit_bytes=limit << 20),
        cost_estimate=pl.CostEstimate(flops=flops, bytes_accessed=moved, transcendentals=0),
        name=name,
    )


def fill_pays(sz, meta, tnew, snew, cross, pays):
    for r, h, j in sz.couplings():
        pays[r][sz.forward_part(h), :] = tnew[meta[sz.sends + j]]
        term = nn(snew[meta[sz.rows + j]], cross[j])
        factor = meta[sz.flags + r].astype(F32)
        pays[r][sz.adjoint_part(h), :] = (factor * term).astype(BF16)


def pack_kernel(sz, *refs):
    x4, u4, coupling, send, row, pair, live_s, col = refs[:8]
    xb, ub, cross, meta, col_out = refs[8:13]
    pays = refs[13 : 13 + sz.rounds]
    send_s, row_s, pair_s, sem_x, sem_u, sem_t, sem_i = refs[13 + sz.rounds :]
    small = [
        pltpu.make_async_copy(send, send_s, sem_i.at[0]),
        pltpu.make_async_copy(row, row_s, sem_i.at[1]),
        pltpu.make_async_copy(pair, pair_s, sem_i.at[2]),
    ]
    copies = []
    for t in range(sz.chan // SUB):
        part = pl.ds(t * SUB, SUB)
        copies.append(pltpu.make_async_copy(x4.at[t], xb.at[:, part, :], sem_x.at[t]))
        copies.append(pltpu.make_async_copy(u4.at[t], ub.at[:, part, :], sem_u.at[t]))
    copies.append(pltpu.make_async_copy(coupling, cross, sem_t))
    copies.append(pltpu.make_async_copy(col, col_out, sem_i.at[3]))
    for copy in small + copies:
        copy.start()
    for copy in small:
        copy.wait()
    count = live_s[0]
    rows = [lax.rem(row_s[0, h, r], count) for r, h, _ in sz.couplings()]
    sends = [lax.rem(send_s[0, h, r], count) for r, h, _ in sz.couplings()]
    for values, spot, first in (
        (rows, sz.rows, sz.first_row),
        (sends, sz.sends, sz.first_send),
    ):
        for j, value in enumerate(values):
            earliest = jnp.int32(j)
            for q in reversed(range(j)):
                earliest = jnp.where(values[q] == value, q, earliest)
            meta[spot + j] = value
            meta[first + j] = earliest
    for r in range(sz.rounds):
        meta[sz.flags + r] = pair_s[0, r]
    meta[sz.live] = count
    for copy in copies:
        copy.wait()

    def clear(i, carry):
        xb[i] = jnp.zeros(xb.shape[1:], BF16)
        ub[i] = jnp.zeros(ub.shape[1:], BF16)
        return carry

    lax.fori_loop(count, sz.blocks, clear, 0)
    fill_pays(sz, meta, xb, ub, cross, pays)


def keep(array):
    return pltpu.with_memory_space_constraint(array, pltpu.HBM)


def pack(sz, *args):
    args = [array if array.size == 1 else keep(array) for array in args]
    _, _, _, send, row, pair, live, col = args
    groups = sz.chan // SUB
    cross = shape((sz.pairs, sz.blk, sz.blk), BF16)
    table = shape((sz.meta,), jnp.int32)
    return call(
        functools.partial(pack_kernel, sz),
        [HBM] * 6 + [SMEM, HBM],
        [VMEM, VMEM, VMEM, SMEM, VMEM] + [VMEM] * sz.rounds,
        [sz.field, sz.field, cross, table, shape(col.shape, jnp.int32)] + [sz.pay] * sz.rounds,
        [
            pltpu.SMEM(send.shape, jnp.int32),
            pltpu.SMEM(row.shape, jnp.int32),
            pltpu.SMEM(pair.shape, jnp.int32),
            pltpu.SemaphoreType.DMA((groups,)),
            pltpu.SemaphoreType.DMA((groups,)),
            pltpu.SemaphoreType.DMA,
            pltpu.SemaphoreType.DMA((4,)),
        ],
        1000,
        4 << 20,
        8,
        "pack",
    )(*args)


def big_steps(count):
    return (count + ROWS - 1) // ROWS


def clear_sums(sz, summed):
    def clear(i, carry):
        summed[i] = jnp.zeros(summed.shape[1:], F32)
        return carry

    lax.fori_loop(0, sz.blocks, clear, 0, unroll=4)


def scatter_terms(sz, summed, cols, terms):
    for m in range(sz.nz):
        summed[cols[m]] = summed[cols[m]] + terms[:, m * sz.blk : (m + 1) * sz.blk]


def finish_local(sz, meta, held, adjoint, tnew, snew, psel, qsel):
    count = meta[sz.live]

    def finish(g, carry):
        for u in range(ROWS_FIRST):
            i = g * ROWS_FIRST + u
            snew[i] = adjoint(i).astype(BF16)
        return carry

    lax.fori_loop(0, (count + ROWS_FIRST - 1) // ROWS_FIRST, finish, 0)

    def dead(i, carry):
        tnew[i] = jnp.zeros(tnew.shape[1:], BF16)
        snew[i] = jnp.zeros(snew.shape[1:], BF16)
        return carry

    lax.fori_loop(count, sz.blocks, dead, 0)
    for j in range(sz.pairs):
        psel[j] = held[meta[sz.rows + j]]
        qsel[j] = adjoint(meta[sz.sends + j])


def first_kernel(
    sz, meta, col, tiles_hbm, t0, s0, tnew, snew, psel, qsel, tiles, turned, held, summed, sem
):
    count = meta[sz.live]
    steps = big_steps(count) * (ROWS // ROWS_FIRST)

    def fetch(g):
        part = pl.ds(g * ROWS_FIRST, ROWS_FIRST)
        return pltpu.make_async_copy(tiles_hbm.at[part], tiles.at[part], sem.at[g])

    def start(g, carry):
        fetch(g).start()
        return carry

    lax.fori_loop(0, steps, start, 0)
    clear_sums(sz, summed)

    def block_row(i):
        cols = [col[m, i] for m in range(sz.nz)]
        parts = [tiles[i, m] for m in range(sz.nz)]
        flipped = [part.T for part in parts]
        for m in range(sz.nz):
            turned[i, pl.ds(m * sz.blk, sz.blk), :] = flipped[m]
        gathered = jnp.concatenate([t0[c] for c in cols], axis=1)
        forward = nn(gathered, jnp.concatenate(flipped, axis=0))
        held[i] = forward
        tnew[i] = forward.astype(BF16)
        scatter_terms(sz, summed, cols, nn(s0[i], jnp.concatenate(parts, axis=1)))

    def step(g, carry):
        fetch(g).wait()
        for u in range(ROWS_FIRST):
            block_row(g * ROWS_FIRST + u)
        return carry

    lax.fori_loop(0, steps, step, 0)
    finish_local(sz, meta, held, lambda i: summed[i], tnew, snew, psel, qsel)


def first_products(sz, meta, col, tiles, t0, s0):
    turned = shape((sz.blocks, sz.nz * sz.blk, sz.blk), BF16)
    return call(
        functools.partial(first_kernel, sz),
        [SMEM, SMEM, HBM, VMEM, VMEM],
        [VMEM] * 6,
        [sz.field, sz.field, sz.picked, sz.picked, shape(tiles.shape, BF16), turned],
        [pltpu.VMEM((sz.blocks, sz.chan, sz.blk), F32)] * 2
        + [pltpu.SemaphoreType.DMA((sz.blocks // ROWS_FIRST,))],
        4 * sz.blocks * sz.nz * sz.chan * sz.blk * sz.blk,
        12 << 20,
        24,
        "first",
    )(meta, col, keep(tiles), t0, s0)


def local_kernel(sz, grad, *refs):
    meta, col, tiles, turned, tcur, scur, tprev, sprev, _ = refs[:9]
    tnew, snew, psel, qsel, last = refs[9:14]
    held, summed = refs[-2:]
    count = meta[sz.live]
    clear_sums(sz, summed)

    def block_row(i):
        cols = [col[m, i] for m in range(sz.nz)]
        gathered = jnp.concatenate([tcur[c] for c in cols], axis=1)
        forward = 2.0 * nn(gathered, turned[i]) - tprev[i].astype(F32)
        held[i] = forward
        tnew[i] = forward.astype(BF16)
        wide = jnp.concatenate([tiles[i, m] for m in range(sz.nz)], axis=1)
        scatter_terms(sz, summed, cols, nn(scur[i], wide))

    def step(g, carry):
        for u in range(ROWS):
            block_row(g * ROWS + u)
        return carry

    lax.fori_loop(0, big_steps(count), step, 0)

    def adjoint(i):
        return 2.0 * summed[i] - sprev[i].astype(F32)

    finish_local(sz, meta, held, adjoint, tnew, snew, psel, qsel)
    if not grad:
        last[...] = jnp.zeros(last.shape, F32)
        return

    def products(g, total):
        left, right = [], []
        for u in range(ROWS_FIRST):
            i = g * ROWS_FIRST + u
            left.append(jnp.concatenate([tprev[i], tcur[i], tnew[i]], axis=0))
            right.append(jnp.concatenate([sprev[i], scur[i]], axis=0).T)
        return total + nn(jnp.concatenate(left, axis=1), jnp.concatenate(right, axis=0))

    steps = (count + ROWS_FIRST - 1) // ROWS_FIRST
    last[...] = lax.fori_loop(0, steps, products, jnp.zeros(last.shape, F32))


def local_products(sz, meta, col, tiles, turned, fields, token, grad):
    tail = shape((3 * sz.chan, 2 * sz.chan), F32) if grad else TOKEN
    return call(
        functools.partial(local_kernel, sz, grad),
        [SMEM, SMEM] + [VMEM] * 7,
        [VMEM] * 5,
        [sz.field, sz.field, sz.picked, sz.picked, tail],
        [pltpu.VMEM((sz.blocks, sz.chan, sz.blk), F32)] * 2,
        4 * sz.blocks * sz.nz * sz.chan * sz.blk * sz.blk,
        12 << 20,
        24,
        "local",
    )(meta, col, tiles, turned, *fields, token)


def add_coupled(sz, scale, meta, got, cross, psel, qsel, pacc, qacc):
    for j in range(sz.pairs):
        pacc[j] = psel[j]
        qacc[j] = qsel[j]
    terms = []
    for r, h, j in sz.couplings():
        factor = scale * meta[sz.flags + r].astype(F32)
        terms.append(factor * nn(got[r][sz.forward_part(h), :], cross[j].T))
        spot = meta[sz.first_row + j]
        pacc[spot] = pacc[spot] + terms[j]
        spot = meta[sz.first_send + j]
        qacc[spot] = qacc[spot] + scale * got[r][sz.adjoint_part(h), :].astype(F32)
    return terms


def join_kernel(sz, scale, grad, *refs):
    refs = list(refs)
    meta, cross, tbase, sbase, psel, qsel = refs[:6]
    got, refs = refs[6 : 6 + sz.rounds], refs[6 + sz.rounds :]
    if grad:
        gram, sold = refs[:2]
        refs = refs[2:]
    tnew, snew = refs[:2]
    pays, refs = refs[2 : 2 + sz.rounds], refs[2 + sz.rounds :]
    if grad:
        partial, refs = refs[0], refs[1:]
    pacc, qacc = refs
    terms = add_coupled(sz, scale, meta, got, cross, psel, qsel, pacc, qacc)

    def move(i, carry):
        tnew[i] = tbase[i]
        snew[i] = sbase[i]
        return carry

    lax.fori_loop(0, sz.blocks, move, 0, unroll=4)
    for j in range(sz.pairs):
        tnew[meta[sz.rows + j]] = pacc[meta[sz.first_row + j]].astype(BF16)
        snew[meta[sz.sends + j]] = qacc[meta[sz.first_send + j]].astype(BF16)
    fill_pays(sz, meta, tnew, snew, cross, pays)
    if grad:
        left = jnp.concatenate([term.astype(BF16) for term in terms], axis=1)
        right = [sold[meta[sz.rows + j]].T for j in range(sz.pairs)]
        extra = nn(left, jnp.concatenate(right, axis=0))
        one, two, three = (pl.ds(k * sz.chan, sz.chan) for k in range(3))
        partial[one, one] = gram[one, one]
        partial[two, :] = gram[two, :]
        partial[one, two] = gram[three, two] + extra


def join(sz, scale, meta, cross, base, got, gram=None, sold=None):
    outs = [sz.field, sz.field] + [sz.pay] * sz.rounds
    args = [meta, cross, *base, *got]
    if gram is not None:
        args += [gram, sold]
        outs.append(shape((2 * sz.chan, 2 * sz.chan), F32))
    outs = call(
        functools.partial(join_kernel, sz, scale, gram is not None),
        [SMEM] + [VMEM] * (len(args) - 1),
        [VMEM] * len(outs),
        outs,
        [pltpu.VMEM(sz.picked.shape, F32)] * 2,
        4 * sz.pairs * sz.chan * sz.blk * sz.blk,
        6 << 20,
        12,
        "join",
    )(*args)
    return outs[0], outs[1], outs[2 : 2 + sz.rounds], outs[2 + sz.rounds :]


def output_weights(weight):
    wide = [weight[k].astype(F32) for k in range(weight.shape[0])]
    ahead = jnp.concatenate([w.T for w in wide], axis=1).astype(BF16)
    back = jnp.concatenate(wide, axis=1).astype(BF16)
    return ahead, back


def output_kernel(sz, low, high, *refs):
    meta, weight = refs[:2]
    forward, adjoint = refs[2:6], refs[6:10]
    refs = refs[11:] if low == 0 else refs[13:]
    out4, grad4, token, held_out, held_grad, sem = refs
    count = meta[sz.live]
    ahead, back = output_weights(weight)
    groups = sz.chan // SUB

    def block(i):
        for left, fields, held in ((ahead, forward, held_out), (back, adjoint, held_grad)):
            value = nn(left, jnp.concatenate([f[i] for f in fields], axis=0)).astype(BF16)
            for t in range(groups):
                held[t, i - low] = value[t * SUB : (t + 1) * SUB]

    def step(g, carry):
        for u in range(ROWS_FIRST):
            block(g * ROWS_FIRST + u)
        return carry

    end = jnp.minimum((count + ROWS_FIRST - 1) // ROWS_FIRST, high // ROWS_FIRST)
    lax.fori_loop(low // ROWS_FIRST, end, step, 0)

    def dead(i, carry):
        for t in range(groups):
            held_out[t, i - low] = jnp.zeros((SUB, sz.blk), BF16)
            held_grad[t, i - low] = jnp.zeros((SUB, sz.blk), BF16)
        return carry

    lax.fori_loop(jnp.maximum(count, low), high, dead, 0)
    part = pl.ds(low, high - low)
    copies = [
        pltpu.make_async_copy(held_out, out4.at[:, part], sem.at[0]),
        pltpu.make_async_copy(held_grad, grad4.at[:, part], sem.at[1]),
    ]
    for copy in copies:
        copy.start()
    token[...] = jnp.zeros(token.shape, F32)
    for copy in copies:
        copy.wait()


def base_outputs(sz, low, high, meta, weight, forward, adjoint, token, before):
    out = shape((sz.chan // SUB, sz.blocks, SUB, sz.blk), BF16)
    args = [meta, weight, *forward, *adjoint, token]
    specs = [SMEM] + [VMEM] * (len(args) - 1)
    aliases = {}
    if low > 0:
        aliases = {len(args): 0, len(args) + 1: 1}
        args += before
        specs += [HBM] * 2
    held = pltpu.VMEM((sz.chan // SUB, high - low, SUB, sz.blk), BF16)
    return call(
        functools.partial(output_kernel, sz, low, high),
        specs,
        [HBM, HBM, VMEM],
        [out, out, TOKEN],
        [held, held, pltpu.SemaphoreType.DMA((2,))],
        16 * (high - low) * sz.chan * sz.chan * sz.blk,
        10 << 20,
        8,
        "outputs",
        aliases,
    )(*args)


def fix_kernel(sz, *refs):
    meta, cross, weight, psel, qsel = refs[:5]
    got, refs = refs[5 : 5 + sz.rounds], refs[5 + sz.rounds :]
    forward, adjoint = refs[:3], refs[3:6]
    mine, theirs = refs[6:8]
    out4, grad4, grad_w, pacc, qacc, held_out, held_grad, sem = refs[10:]
    add_coupled(sz, 2.0, meta, got, cross, psel, qsel, pacc, qacc)
    ahead, back = output_weights(weight)
    groups = sz.chan // SUB
    copies = []
    for j in range(sz.pairs):
        for left, fields, last, spot, first, held, out, s in (
            (ahead, forward, pacc, sz.rows, sz.first_row, held_out, out4, 0),
            (back, adjoint, qacc, sz.sends, sz.first_send, held_grad, grad4, 1),
        ):
            i, slot = meta[spot + j], meta[first + j]
            stack = [f[i] for f in fields] + [last[slot].astype(BF16)]
            value = nn(left, jnp.concatenate(stack, axis=0)).astype(BF16)
            for t in range(groups):
                held[j, t] = value[t * SUB : (t + 1) * SUB]
            copies.append((slot == j, pltpu.make_async_copy(held.at[j], out.at[:, i], sem.at[s, j])))
    for own, copy in copies:
        pl.when(own)(copy.start)
    one, two = pl.ds(0, sz.chan), pl.ds(sz.chan, sz.chan)

    def total(a, b):
        return mine[a, b] + theirs[a, b]

    zeroth, first = total(one, one), total(two, one)
    grad_w[0] = zeroth
    grad_w[1] = first
    grad_w[2] = 2.0 * total(two, two) - zeroth
    grad_w[3] = 2.0 * total(one, two) - first
    for own, copy in copies:
        pl.when(own)(copy.wait)


def fix_outputs(sz, meta, cross, weight, picked, got, forward, adjoint, mine, theirs, before):
    out = shape(before[0].shape, BF16)
    args = [meta, cross, weight, *picked, *got, *forward, *adjoint, mine, theirs]
    held = pltpu.VMEM((sz.pairs, sz.chan // SUB, SUB, sz.blk), BF16)
    return call(
        functools.partial(fix_kernel, sz),
        [SMEM] + [VMEM] * (len(args) - 1) + [HBM] * 2,
        [HBM, HBM, VMEM],
        [out, out, shape((4, sz.chan, sz.chan), F32)],
        [pltpu.VMEM(sz.picked.shape, F32)] * 2 + [held, held]
        + [pltpu.SemaphoreType.DMA((2, sz.pairs))],
        8 * sz.pairs * sz.chan * sz.blk * sz.blk,
        4 << 20,
        10,
        "fix",
        {len(args): 0, len(args) + 1: 1},
    )(*args, *before)


def add_kernel(gated, inputs, *refs):
    mine, theirs = refs[:2]
    out, token = refs[inputs : inputs + 2]
    if gated:
        refs[-1][...] = refs[2][...]
    out[...] = mine[...] + theirs[...]
    token[...] = jnp.zeros(token.shape, F32)


def add(mine, theirs, pay, after):
    outs = [shape(mine.shape, F32), TOKEN]
    args = [mine, theirs]
    if pay is not None:
        outs.append(shape(pay.shape, BF16))
        args.append(pay)
    args += after
    return call(
        functools.partial(add_kernel, pay is not None, len(args)),
        [VMEM] * len(args),
        [VMEM] * len(outs),
        outs,
        [],
        mine.size,
        12 * mine.size,
        2,
        "add",
    )(*args)


def from_partner(values, bit):
    count = lax.axis_size("dom")
    route = []
    for low in range(count):
        high = low | 1 << bit
        if high != low and high < count:
            route += [(low, high), (high, low)]
    return lax.ppermute(values, "dom", route)


def local(
    features,
    cheb_weight,
    lap_tiles,
    col_index,
    cross_tiles,
    send_index,
    row_index,
    pair_on,
    blk_live,
    cotangent,
):
    sz = Sizes(features, lap_tiles, cross_tiles)
    split = (sz.chan // SUB, SUB, sz.blocks, sz.blk)
    x4 = features.reshape(split).transpose(0, 2, 1, 3)
    u4 = cotangent.reshape(split).transpose(0, 2, 1, 3)
    coupling = cross_tiles.reshape(sz.pairs, sz.blk, sz.blk)
    send, row = send_index.transpose(0, 2, 1), row_index.transpose(0, 2, 1)

    packed = pack(sz, x4, u4, coupling, send, row, pair_on, blk_live, col_index.T)
    t0, s0, cross, meta, col = packed[:5]
    got = [from_partner(pay, bit) for bit, pay in enumerate(packed[5:])]
    *base, tiles, turned = first_products(sz, meta, col, lap_tiles, t0, s0)
    t1, s1, pays, _ = join(sz, 1.0, meta, cross, base, got)

    got = [from_partner(pay, bit) for bit, pay in enumerate(pays)]
    fields = (t1, s1, t0, s0)
    *base, gram = local_products(sz, meta, col, tiles, turned, fields, cross, True)
    t2, s2, pays, (mine,) = join(sz, 2.0, meta, cross, base, got, gram, s1)

    state = {}

    def window_products(token):
        fields = (t2, s2, t1, s1)
        *base, token = local_products(sz, meta, col, tiles, turned, fields, token, False)
        state["base"] = base
        return token

    def window_outputs(low, high):
        def window(token):
            forward = (t0, t1, t2, state["base"][0])
            adjoint = (s0, s1, s2, state["base"][1])
            out4, grad4, token = base_outputs(
                sz, low, high, meta, cheb_weight, forward, adjoint, token, state.get("outs", [])
            )
            state["outs"] = [out4, grad4]
            return token

        return window

    middle = sz.blocks // (2 * ROWS_FIRST) * ROWS_FIRST
    windows = [window_products, window_outputs(0, middle), window_outputs(middle, sz.blocks)]
    bits = list(reversed(range((lax.axis_size("dom") - 1).bit_length())))
    pays, got = list(pays), [None] * sz.rounds
    token = mine
    for at, bit in enumerate(bits):
        if bit < sz.rounds:
            got[bit] = from_partner(pays[bit], bit)
        theirs = from_partner(mine, bit)
        if at < len(windows):
            token = windows[at](token)
        if at + 1 < len(bits):
            later = bits[at + 1]
            gated = later < sz.rounds
            after = [token] + ([got[bit]] if bit < sz.rounds else [])
            mine, token, *rest = add(mine, theirs, pays[later] if gated else None, after)
            if gated:
                pays[later] = rest[0]
    out4, grad4, grad_w = fix_outputs(
        sz,
        meta,
        cross,
        cheb_weight,
        state["base"][2:4],
        got,
        (t0, t1, t2),
        (s0, s1, s2),
        mine,
        theirs,
        state["outs"],
    )
    conv_out = out4.transpose(0, 2, 1, 3).reshape(features.shape)
    grad_x = grad4.transpose(0, 2, 1, 3).reshape(features.shape)
    return (conv_out, grad_x, grad_w)


def solution(mesh):
    in_specs = (
        P(None, "dom"),
        P(),
        P("dom", None, None, None),
        P("dom", None),
        P("dom", None, None, None, None),
        P("dom", None, None),
        P("dom", None, None),
        P("dom", None),
        P("dom"),
        P(None, "dom"),
    )
    out_specs = (P(None, "dom"), P(None, "dom"), P())
    return jax.shard_map(local, mesh=mesh, in_specs=in_specs, out_specs=out_specs, check_vma=False)
```

```python
import functools

import jax
import jax.numpy as jnp
from jax import lax
from jax.experimental import pallas as pl
from jax.experimental.pallas import tpu as pltpu
from jax.sharding import PartitionSpec as P


F32 = jnp.float32
BF16 = jnp.bfloat16
SUB = 8
LANES = 128
ROWS_FIRST = 8
ROWS = 16

VMEM = pl.BlockSpec(memory_space=pltpu.VMEM)
SMEM = pl.BlockSpec(memory_space=pltpu.SMEM)
HBM = pl.BlockSpec(memory_space=pltpu.HBM)
TOKEN = jax.ShapeDtypeStruct((SUB, LANES), F32)


def shape(dims, dtype):
    return jax.ShapeDtypeStruct(dims, dtype)


def nn(a, b):
    return lax.dot_general(a, b, (((1,), (0,)), ((), ())), preferred_element_type=F32)


class Sizes:
    def __init__(self, features, lap_tiles, cross_tiles):
        self.chan = features.shape[0]
        self.blocks, self.nz, self.blk = lap_tiles.shape[:3]
        self.rounds, self.hb = cross_tiles.shape[1:3]
        self.pairs = self.rounds * self.hb
        self.rows = 0
        self.sends = self.pairs
        self.first_row = 2 * self.pairs
        self.first_send = 3 * self.pairs
        self.flags = 4 * self.pairs
        self.live = self.flags + self.rounds
        self.meta = self.live + 1
        self.half = self.hb * self.chan
        self.field = shape((self.blocks, self.chan, self.blk), BF16)
        self.picked = shape((self.pairs, self.chan, self.blk), F32)
        self.pay = shape((2 * self.half, self.blk), BF16)

    def couplings(self):
        return [(r, h, r * self.hb + h) for r in range(self.rounds) for h in range(self.hb)]

    def forward_part(self, h):
        return pl.ds(h * self.chan, self.chan)

    def adjoint_part(self, h):
        return pl.ds(self.half + h * self.chan, self.chan)


def call(kernel, in_specs, out_specs, out_shape, scratch, flops, moved, limit, aliases=None):
    return pl.pallas_call(
        kernel,
        in_specs=in_specs,
        out_specs=out_specs,
        out_shape=out_shape,
        scratch_shapes=scratch,
        input_output_aliases=aliases or {},
        compiler_params=pltpu.CompilerParams(vmem_limit_bytes=limit << 20),
        cost_estimate=pl.CostEstimate(flops=flops, bytes_accessed=moved, transcendentals=0),
    )


def fill_pays(sz, meta, tnew, snew, cross, pays):
    for r, h, j in sz.couplings():
        pays[r][sz.forward_part(h), :] = tnew[meta[sz.sends + j]]
        term = nn(snew[meta[sz.rows + j]], cross[j])
        factor = meta[sz.flags + r].astype(F32)
        pays[r][sz.adjoint_part(h), :] = (factor * term).astype(BF16)


def pack_kernel(sz, *refs):
    x4, u4, coupling, send, row, pair, live_s, col = refs[:8]
    xb, ub, cross, across, meta, col_out = refs[8:14]
    pays = refs[14 : 14 + sz.rounds]
    send_s, row_s, pair_s, sem_x, sem_u, sem_t, sem_i = refs[14 + sz.rounds :]
    small = [
        pltpu.make_async_copy(send, send_s, sem_i.at[0]),
        pltpu.make_async_copy(row, row_s, sem_i.at[1]),
        pltpu.make_async_copy(pair, pair_s, sem_i.at[2]),
    ]
    tiles = pltpu.make_async_copy(coupling, cross, sem_t)
    copies = []
    for t in range(sz.chan // SUB):
        part = pl.ds(t * SUB, SUB)
        copies.append(pltpu.make_async_copy(x4.at[t], xb.at[:, part, :], sem_x.at[t]))
        copies.append(pltpu.make_async_copy(u4.at[t], ub.at[:, part, :], sem_u.at[t]))
    copies.append(pltpu.make_async_copy(col, col_out, sem_i.at[3]))
    for copy in small + [tiles] + copies:
        copy.start()
    for copy in small:
        copy.wait()
    count = live_s[0]
    rows = [lax.rem(row_s[0, h, r], count) for r, h, _ in sz.couplings()]
    sends = [lax.rem(send_s[0, h, r], count) for r, h, _ in sz.couplings()]
    for values, spot, first in (
        (rows, sz.rows, sz.first_row),
        (sends, sz.sends, sz.first_send),
    ):
        for j, value in enumerate(values):
            earliest = jnp.int32(j)
            for q in reversed(range(j)):
                earliest = jnp.where(values[q] == value, q, earliest)
            meta[spot + j] = value
            meta[first + j] = earliest
    for r in range(sz.rounds):
        meta[sz.flags + r] = pair_s[0, r]
    meta[sz.live] = count
    tiles.wait()
    for j in range(sz.pairs):
        across[j] = cross[j].T
    for copy in copies:
        copy.wait()

    def clear(i, carry):
        xb[i] = jnp.zeros(xb.shape[1:], BF16)
        ub[i] = jnp.zeros(ub.shape[1:], BF16)
        return carry

    lax.fori_loop(count, sz.blocks, clear, 0)
    fill_pays(sz, meta, xb, ub, cross, pays)


def keep(array):
    return pltpu.with_memory_space_constraint(array, pltpu.HBM)


def pack(sz, *args):
    args = [array if array.size == 1 else keep(array) for array in args]
    _, _, _, send, row, pair, _, col = args
    groups = sz.chan // SUB
    cross = shape((sz.pairs, sz.blk, sz.blk), BF16)
    table = shape((sz.meta,), jnp.int32)
    return call(
        functools.partial(pack_kernel, sz),
        [HBM] * 6 + [SMEM, HBM],
        [VMEM] * 4 + [SMEM, VMEM] + [VMEM] * sz.rounds,
        [sz.field, sz.field, cross, cross, table, shape(col.shape, jnp.int32)]
        + [sz.pay] * sz.rounds,
        [
            pltpu.SMEM(send.shape, jnp.int32),
            pltpu.SMEM(row.shape, jnp.int32),
            pltpu.SMEM(pair.shape, jnp.int32),
            pltpu.SemaphoreType.DMA((groups,)),
            pltpu.SemaphoreType.DMA((groups,)),
            pltpu.SemaphoreType.DMA,
            pltpu.SemaphoreType.DMA((4,)),
        ],
        1000,
        4 << 20,
        8,
    )(*args)


def big_steps(count):
    return (count + ROWS - 1) // ROWS


def clear_sums(sz, summed):
    def clear(i, carry):
        summed[i] = jnp.zeros(summed.shape[1:], F32)
        return carry

    lax.fori_loop(0, sz.blocks, clear, 0, unroll=4)


def scatter_terms(sz, summed, cols, terms):
    for m in range(sz.nz):
        summed[cols[m]] = summed[cols[m]] + terms[:, m * sz.blk : (m + 1) * sz.blk]


def finish_local(sz, meta, held, adjoint, tnew, snew, psel, qsel):
    count = meta[sz.live]

    def finish(g, carry):
        for u in range(ROWS_FIRST):
            i = g * ROWS_FIRST + u
            snew[i] = adjoint(i).astype(BF16)
        return carry

    lax.fori_loop(0, (count + ROWS_FIRST - 1) // ROWS_FIRST, finish, 0)

    def dead(i, carry):
        tnew[i] = jnp.zeros(tnew.shape[1:], BF16)
        snew[i] = jnp.zeros(snew.shape[1:], BF16)
        return carry

    lax.fori_loop(count, sz.blocks, dead, 0)
    for j in range(sz.pairs):
        psel[j] = held[meta[sz.rows + j]]
        qsel[j] = adjoint(meta[sz.sends + j])


def first_kernel(
    sz, meta, col, tiles_hbm, t0, s0, tnew, snew, psel, qsel, tiles, turned, gram, held, summed, sem
):
    count = meta[sz.live]
    steps = big_steps(count)
    loads = steps * (ROWS // ROWS_FIRST)

    def fetch(g):
        part = pl.ds(g * ROWS_FIRST, ROWS_FIRST)
        return pltpu.make_async_copy(tiles_hbm.at[part], tiles.at[part], sem.at[g])

    def start(g, carry):
        fetch(g).start()
        return carry

    lax.fori_loop(0, loads, start, 0)
    clear_sums(sz, summed)

    def products(g, total):
        spots = [g * ROWS + u for u in range(ROWS)]
        left = jnp.concatenate([t0[i] for i in spots], axis=1)
        return total + nn(left, jnp.concatenate([s0[i].T for i in spots], axis=0))

    gram[...] = lax.fori_loop(0, steps, products, jnp.zeros(gram.shape, F32))

    def block_row(i):
        cols = [col[m, i] for m in range(sz.nz)]
        parts = [tiles[i, m] for m in range(sz.nz)]
        flipped = [part.T for part in parts]
        for m in range(sz.nz):
            turned[i, pl.ds(m * sz.blk, sz.blk), :] = flipped[m]
        gathered = jnp.concatenate([t0[c] for c in cols], axis=1)
        forward = nn(gathered, jnp.concatenate(flipped, axis=0))
        held[i] = forward
        tnew[i] = forward.astype(BF16)
        scatter_terms(sz, summed, cols, nn(s0[i], jnp.concatenate(parts, axis=1)))

    def step(g, carry):
        for part in range(ROWS // ROWS_FIRST):
            fetch(g * (ROWS // ROWS_FIRST) + part).wait()
        for u in range(ROWS):
            block_row(g * ROWS + u)
        return carry

    lax.fori_loop(0, steps, step, 0)
    finish_local(sz, meta, held, lambda i: summed[i], tnew, snew, psel, qsel)


def first_products(sz, meta, col, tiles, t0, s0):
    turned = shape((sz.blocks, sz.nz * sz.blk, sz.blk), BF16)
    return call(
        functools.partial(first_kernel, sz),
        [SMEM, SMEM, HBM, VMEM, VMEM],
        [VMEM] * 7,
        [sz.field, sz.field, sz.picked, sz.picked, shape(tiles.shape, BF16), turned]
        + [shape((sz.chan, sz.chan), F32)],
        [pltpu.VMEM((sz.blocks, sz.chan, sz.blk), F32)] * 2
        + [pltpu.SemaphoreType.DMA((sz.blocks // ROWS_FIRST,))],
        4 * sz.blocks * sz.nz * sz.chan * sz.blk * sz.blk,
        12 << 20,
        24,
    )(meta, col, keep(tiles), t0, s0)


def local_kernel(sz, grad, *refs):
    meta, col, tiles, turned, tcur, scur, tprev, sprev, _ = refs[:9]
    tnew, snew, psel, qsel, last = refs[9:14]
    held, summed = refs[-2:]
    count = meta[sz.live]
    clear_sums(sz, summed)

    def block_row(i):
        cols = [col[m, i] for m in range(sz.nz)]
        gathered = jnp.concatenate([tcur[c] for c in cols], axis=1)
        forward = 2.0 * nn(gathered, turned[i]) - tprev[i].astype(F32)
        held[i] = forward
        tnew[i] = forward.astype(BF16)
        wide = jnp.concatenate([tiles[i, m] for m in range(sz.nz)], axis=1)
        scatter_terms(sz, summed, cols, nn(scur[i], wide))

    def step(g, carry):
        for u in range(ROWS):
            block_row(g * ROWS + u)
        return carry

    lax.fori_loop(0, big_steps(count), step, 0)

    def adjoint(i):
        return 2.0 * summed[i] - sprev[i].astype(F32)

    finish_local(sz, meta, held, adjoint, tnew, snew, psel, qsel)
    if not grad:
        last[...] = jnp.zeros(last.shape, F32)
        return

    def products(g, total):
        left, right = [], []
        for u in range(ROWS):
            i = g * ROWS + u
            left.append(jnp.concatenate([tcur[i], tnew[i]], axis=0))
            right.append(jnp.concatenate([sprev[i], scur[i]], axis=0).T)
        return total + nn(jnp.concatenate(left, axis=1), jnp.concatenate(right, axis=0))

    last[...] = lax.fori_loop(0, big_steps(count), products, jnp.zeros(last.shape, F32))


def local_products(sz, meta, col, tiles, turned, fields, token, grad):
    tail = shape((2 * sz.chan, 2 * sz.chan), F32) if grad else TOKEN
    return call(
        functools.partial(local_kernel, sz, grad),
        [SMEM, SMEM] + [VMEM] * 7,
        [VMEM] * 5,
        [sz.field, sz.field, sz.picked, sz.picked, tail],
        [pltpu.VMEM((sz.blocks, sz.chan, sz.blk), F32)] * 2,
        4 * sz.blocks * sz.nz * sz.chan * sz.blk * sz.blk,
        12 << 20,
        24,
    )(meta, col, tiles, turned, *fields, token)


def add_coupled(sz, scale, meta, got, across, psel, qsel, pacc, qacc, which):
    for j in range(sz.pairs):
        pacc[j] = psel[j]
        qacc[j] = qsel[j]
    terms = {}
    for r, h, j in sz.couplings():
        if r in which:
            factor = scale * meta[sz.flags + r].astype(F32)
            terms[j] = factor * nn(got[r][sz.forward_part(h), :], across[j])
            spot = meta[sz.first_row + j]
            pacc[spot] = pacc[spot] + terms[j]
            spot = meta[sz.first_send + j]
            qacc[spot] = qacc[spot] + scale * got[r][sz.adjoint_part(h), :].astype(F32)
    return terms


def couple_kernel(sz, scale, which, *refs):
    meta, across, psel, qsel = refs[:4]
    got = dict(zip(which, refs[4 : 4 + len(which)]))
    pacc, qacc = refs[-2:]
    add_coupled(sz, scale, meta, got, across, psel, qsel, pacc, qacc, which)


def couple(sz, scale, meta, across, picked, got, which, after):
    args = [meta, across, *picked, *(got[r] for r in which), *after]
    return call(
        functools.partial(couple_kernel, sz, scale, which),
        [SMEM] + [VMEM] * (len(args) - 1),
        [VMEM] * 2,
        [sz.picked] * 2,
        [],
        2 * len(which) * sz.hb * sz.chan * sz.blk * sz.blk,
        2 << 20,
        6,
    )(*args)


def correct_kernel(sz, axis, *refs):
    meta, across, psel, qsel, gram0, gram, sold = refs[:7]
    got, refs = refs[7 : 7 + sz.rounds], refs[7 + sz.rounds :]
    pacc, qacc, keep_half, give_half, whole = refs
    which = range(sz.rounds)
    terms = add_coupled(sz, 2.0, meta, got, across, psel, qsel, pacc, qacc, which)
    left = jnp.concatenate([terms[j].astype(BF16) for j in range(sz.pairs)], axis=1)
    right = [sold[meta[sz.rows + j]].T for j in range(sz.pairs)]
    extra = nn(left, jnp.concatenate(right, axis=0))
    one, two = pl.ds(0, sz.chan), pl.ds(sz.chan, sz.chan)
    whole[one, one] = gram0[...]
    whole[two, one] = gram[one, one]
    whole[two, two] = gram[one, two]
    whole[one, two] = gram[two, two] + extra
    odd = lax.rem(lax.axis_index(axis), 2)
    keep_half[...] = whole[pl.ds(pl.multiple_of(odd * sz.chan, sz.chan), sz.chan), :]
    give_half[...] = whole[pl.ds(pl.multiple_of((1 - odd) * sz.chan, sz.chan), sz.chan), :]


def correct(sz, axis, meta, across, picked, got, gram0, gram, sold):
    args = [meta, across, *picked, gram0, gram, sold, *got]
    half = shape((sz.chan, 2 * sz.chan), F32)
    return call(
        functools.partial(correct_kernel, sz, axis),
        [SMEM] + [VMEM] * (len(args) - 1),
        [VMEM] * 4,
        [sz.picked, sz.picked, half, half],
        [pltpu.VMEM((2 * sz.chan, 2 * sz.chan), F32)],
        4 * sz.pairs * sz.chan * sz.blk * sz.blk,
        3 << 20,
        8,
    )(*args)


def join_kernel(sz, *refs):
    meta, cross, tbase, sbase, pacc, qacc, tnew, snew = refs[:8]
    pays = refs[8:]

    def move(i, carry):
        tnew[i] = tbase[i]
        snew[i] = sbase[i]
        return carry

    lax.fori_loop(0, sz.blocks, move, 0, unroll=4)
    for j in range(sz.pairs):
        tnew[meta[sz.rows + j]] = pacc[meta[sz.first_row + j]].astype(BF16)
        snew[meta[sz.sends + j]] = qacc[meta[sz.first_send + j]].astype(BF16)
    fill_pays(sz, meta, tnew, snew, cross, pays)


def join(sz, meta, cross, base, picked):
    args = [meta, cross, *base, *picked]
    outs = [sz.field, sz.field] + [sz.pay] * sz.rounds
    outs = call(
        functools.partial(join_kernel, sz),
        [SMEM] + [VMEM] * (len(args) - 1),
        [VMEM] * len(outs),
        outs,
        [],
        2 * sz.pairs * sz.chan * sz.blk * sz.blk,
        5 << 20,
        8,
    )(*args)
    return outs[0], outs[1], outs[2:]


def output_weights(weight):
    wide = [weight[k].astype(F32) for k in range(weight.shape[0])]
    ahead = jnp.concatenate([w.T for w in wide], axis=1).astype(BF16)
    back = jnp.concatenate(wide, axis=1).astype(BF16)
    return ahead, back


def output_kernel(sz, low, high, *refs):
    meta, weight = refs[:2]
    forward, adjoint = refs[2:6], refs[6:10]
    refs = refs[11:] if low == 0 else refs[13:]
    out4, grad4, token, held_out, held_grad, sem = refs
    count = meta[sz.live]
    ahead, back = output_weights(weight)
    groups = sz.chan // SUB

    def block(i):
        for left, fields, held in ((ahead, forward, held_out), (back, adjoint, held_grad)):
            value = nn(left, jnp.concatenate([f[i] for f in fields], axis=0)).astype(BF16)
            for t in range(groups):
                held[t, i - low] = value[t * SUB : (t + 1) * SUB]

    def step(g, carry):
        for u in range(ROWS_FIRST):
            block(g * ROWS_FIRST + u)
        return carry

    end = jnp.minimum((count + ROWS_FIRST - 1) // ROWS_FIRST, high // ROWS_FIRST)
    lax.fori_loop(low // ROWS_FIRST, end, step, 0)

    def dead(i, carry):
        for t in range(groups):
            held_out[t, i - low] = jnp.zeros((SUB, sz.blk), BF16)
            held_grad[t, i - low] = jnp.zeros((SUB, sz.blk), BF16)
        return carry

    lax.fori_loop(jnp.maximum(count, low), high, dead, 0)
    part = pl.ds(low, high - low)
    copies = [
        pltpu.make_async_copy(held_out, out4.at[:, part], sem.at[0]),
        pltpu.make_async_copy(held_grad, grad4.at[:, part], sem.at[1]),
    ]
    for copy in copies:
        copy.start()
    token[...] = jnp.zeros(token.shape, F32)
    for copy in copies:
        copy.wait()


def base_outputs(sz, low, high, meta, weight, forward, adjoint, token, before):
    out = shape((sz.chan // SUB, sz.blocks, SUB, sz.blk), BF16)
    args = [meta, weight, *forward, *adjoint, token]
    specs = [SMEM] + [VMEM] * (len(args) - 1)
    aliases = {}
    if low > 0:
        aliases = {len(args): 0, len(args) + 1: 1}
        args += before
        specs += [HBM] * 2
    held = pltpu.VMEM((sz.chan // SUB, high - low, SUB, sz.blk), BF16)
    return call(
        functools.partial(output_kernel, sz, low, high),
        specs,
        [HBM, HBM, VMEM],
        [out, out, TOKEN],
        [held, held, pltpu.SemaphoreType.DMA((2,))],
        16 * (high - low) * sz.chan * sz.chan * sz.blk,
        10 << 20,
        8,
        aliases,
    )(*args)


def fix_kernel(sz, axis, which, *refs):
    meta, across, weight, psel, qsel = refs[:5]
    got, refs = dict(zip(which, refs[5 : 5 + len(which)])), refs[5 + len(which) :]
    forward, adjoint = refs[:3], refs[3:6]
    mine, theirs = refs[6:8]
    out4, grad4, grad_w, pacc, qacc, held_out, held_grad, sem = refs[10:]
    add_coupled(sz, 2.0, meta, got, across, psel, qsel, pacc, qacc, which)
    ahead, back = output_weights(weight)
    groups = sz.chan // SUB
    copies = []
    for j in range(sz.pairs):
        for left, fields, last, spot, first, held, out, s in (
            (ahead, forward, pacc, sz.rows, sz.first_row, held_out, out4, 0),
            (back, adjoint, qacc, sz.sends, sz.first_send, held_grad, grad4, 1),
        ):
            i, slot = meta[spot + j], meta[first + j]
            stack = [f[i] for f in fields] + [last[slot].astype(BF16)]
            value = nn(left, jnp.concatenate(stack, axis=0)).astype(BF16)
            for t in range(groups):
                held[j, t] = value[t * SUB : (t + 1) * SUB]
            copies.append((slot == j, pltpu.make_async_copy(held.at[j], out.at[:, i], sem.at[s, j])))
    for own, copy in copies:
        pl.when(own)(copy.start)
    odd = lax.rem(lax.axis_index(axis), 2) == 1
    top = jnp.where(odd, theirs[...], mine[...])
    low = jnp.where(odd, mine[...], theirs[...])
    zeroth, first = top[:, : sz.chan], low[:, : sz.chan]
    grad_w[0] = zeroth
    grad_w[1] = first
    grad_w[2] = 2.0 * low[:, sz.chan :] - zeroth
    grad_w[3] = 2.0 * top[:, sz.chan :] - first
    for own, copy in copies:
        pl.when(own)(copy.wait)


def fix_outputs(
    sz, axis, meta, across, weight, picked, got, which, forward, adjoint, mine, theirs, before
):
    out = shape(before[0].shape, BF16)
    late = [got[r] for r in which]
    args = [meta, across, weight, *picked, *late, *forward, *adjoint, mine, theirs]
    held = pltpu.VMEM((sz.pairs, sz.chan // SUB, SUB, sz.blk), BF16)
    return call(
        functools.partial(fix_kernel, sz, axis, which),
        [SMEM] + [VMEM] * (len(args) - 1) + [HBM] * 2,
        [HBM, HBM, VMEM],
        [out, out, shape((4, sz.chan, sz.chan), F32)],
        [pltpu.VMEM(sz.picked.shape, F32)] * 2 + [held, held]
        + [pltpu.SemaphoreType.DMA((2, sz.pairs))],
        8 * sz.pairs * sz.chan * sz.blk * sz.blk,
        4 << 20,
        10,
        {len(args): 0, len(args) + 1: 1},
    )(*args, *before)


def add_kernel(gated, inputs, *refs):
    mine, theirs = refs[:2]
    out, token = refs[inputs : inputs + 2]
    if gated:
        refs[-1][...] = refs[2][...]
    out[...] = mine[...] + theirs[...]
    token[...] = jnp.zeros(token.shape, F32)


def add(mine, theirs, pay, after):
    outs = [shape(mine.shape, F32), TOKEN]
    args = [mine, theirs]
    if pay is not None:
        outs.append(shape(pay.shape, BF16))
        args.append(pay)
    args += after
    return call(
        functools.partial(add_kernel, pay is not None, len(args)),
        [VMEM] * len(args),
        [VMEM] * len(outs),
        outs,
        [],
        mine.size,
        12 * mine.size,
        2,
    )(*args)


def from_partner(values, bit):
    count = lax.axis_size("dom")
    route = []
    for low in range(count):
        high = low | 1 << bit
        if high != low and high < count:
            route += [(low, high), (high, low)]
    return lax.ppermute(values, "dom", route)


def local(
    features,
    cheb_weight,
    lap_tiles,
    col_index,
    cross_tiles,
    send_index,
    row_index,
    pair_on,
    blk_live,
    cotangent,
):
    sz = Sizes(features, lap_tiles, cross_tiles)
    split = (sz.chan // SUB, SUB, sz.blocks, sz.blk)
    x4 = features.reshape(split).transpose(0, 2, 1, 3)
    u4 = cotangent.reshape(split).transpose(0, 2, 1, 3)
    coupling = cross_tiles.reshape(sz.pairs, sz.blk, sz.blk)
    send, row = send_index.transpose(0, 2, 1), row_index.transpose(0, 2, 1)

    packed = pack(sz, x4, u4, coupling, send, row, pair_on, blk_live, col_index.T)
    t0, s0, cross, across, meta, col = packed[:6]
    everyone = range(sz.rounds)
    got = [from_partner(pay, bit) for bit, pay in enumerate(packed[6:])]
    *base, psel, qsel, tiles, turned, gram0 = first_products(sz, meta, col, lap_tiles, t0, s0)
    picked = couple(sz, 1.0, meta, across, (psel, qsel), got, everyone, [])
    t1, s1, pays = join(sz, meta, cross, base, picked)

    got = [from_partner(pay, bit) for bit, pay in enumerate(pays)]
    fields = (t1, s1, t0, s0)
    *base, psel, qsel, gram = local_products(sz, meta, col, tiles, turned, fields, cross, True)
    *picked, mine, given = correct(
        sz, "dom", meta, across, (psel, qsel), got, gram0, gram, s1
    )
    theirs = from_partner(given, 0)
    t2, s2, pays = join(sz, meta, cross, base, picked)

    state = {}

    def window_products(token):
        fields = (t2, s2, t1, s1)
        *state["base"], token = local_products(sz, meta, col, tiles, turned, fields, token, False)
        return token

    def window_outputs(low, high):
        def window(token):
            forward = (t0, t1, t2, state["base"][0])
            adjoint = (s0, s1, s2, state["base"][1])
            out4, grad4, token = base_outputs(
                sz, low, high, meta, cheb_weight, forward, adjoint, token, state.get("outs", [])
            )
            state["outs"] = [out4, grad4]
            return token

        return window

    middle = sz.blocks // (2 * ROWS_FIRST) * ROWS_FIRST
    windows = [window_products, window_outputs(0, middle), window_outputs(middle, sz.blocks)]
    bits = list(reversed(range(1, (lax.axis_size("dom") - 1).bit_length())))
    pays, got = list(pays), [None] * sz.rounds
    got[0] = from_partner(pays[0], 0)
    early = [bit for bit in bits[:-1] if bit < sz.rounds]
    late = [bit for bit in everyone if bit not in early]
    mine, token, *rest = add(mine, theirs, pays[bits[0]] if bits[0] < sz.rounds else None, [])
    for at, bit in enumerate(bits):
        if bit < sz.rounds:
            pays[bit] = rest[0]
        theirs = from_partner(mine, bit)
        if bit < sz.rounds:
            got[bit] = from_partner(pays[bit], bit)
        if at < len(windows):
            token = windows[at](token)
        last = at + 1 == len(bits)
        if last:
            picked = couple(sz, 2.0, meta, across, state["base"][2:4], got, early, [token])
            token = picked[0]
        gated = not last and bits[at + 1] < sz.rounds
        after = [token] + ([got[bit]] if bit < sz.rounds and not last else [])
        if at == 0:
            after.append(got[0])
        mine, token, *rest = add(mine, theirs, pays[bits[at + 1]] if gated else None, after)
    theirs = from_partner(mine, 0)
    out4, grad4, grad_w = fix_outputs(
        sz,
        "dom",
        meta,
        across,
        cheb_weight,
        picked,
        got,
        late,
        (t0, t1, t2),
        (s0, s1, s2),
        mine,
        theirs,
        state["outs"],
    )
    conv_out = out4.transpose(0, 2, 1, 3).reshape(features.shape)
    grad_x = grad4.transpose(0, 2, 1, 3).reshape(features.shape)
    return (conv_out, grad_x, grad_w)


def solution(mesh):
    in_specs = (
        P(None, "dom"),
        P(),
        P("dom", None, None, None),
        P("dom", None),
        P("dom", None, None, None, None),
        P("dom", None, None),
        P("dom", None, None),
        P("dom", None),
        P("dom"),
        P(None, "dom"),
    )
    out_specs = (P(None, "dom"), P(None, "dom"), P())
    return jax.shard_map(local, mesh=mesh, in_specs=in_specs, out_specs=out_specs, check_vma=False)
```

```python
import functools

import jax
import jax.numpy as jnp
from jax import lax
from jax.experimental import pallas as pl
from jax.experimental.pallas import tpu as pltpu
from jax.sharding import PartitionSpec as P


F32 = jnp.float32
BF16 = jnp.bfloat16
SUB = 8
LANES = 128
ROWS_FIRST = 8
ROWS = 16

VMEM = pl.BlockSpec(memory_space=pltpu.VMEM)
SMEM = pl.BlockSpec(memory_space=pltpu.SMEM)
HBM = pl.BlockSpec(memory_space=pltpu.HBM)
TOKEN = jax.ShapeDtypeStruct((SUB, LANES), F32)


def shape(dims, dtype):
    return jax.ShapeDtypeStruct(dims, dtype)


def nn(a, b):
    return lax.dot_general(a, b, (((1,), (0,)), ((), ())), preferred_element_type=F32)


class Sizes:
    def __init__(self, features, lap_tiles, cross_tiles):
        self.chan = features.shape[0]
        self.blocks, self.nz, self.blk = lap_tiles.shape[:3]
        self.rounds, self.hb = cross_tiles.shape[1:3]
        self.pairs = self.rounds * self.hb
        self.rows = 0
        self.sends = self.pairs
        self.first_row = 2 * self.pairs
        self.first_send = 3 * self.pairs
        self.flags = 4 * self.pairs
        self.live = self.flags + self.rounds
        self.meta = self.live + 1
        self.half = self.hb * self.chan
        self.field = shape((self.blocks, self.chan, self.blk), BF16)
        self.picked = shape((self.pairs, self.chan, self.blk), F32)
        self.pay = shape((2 * self.half, self.blk), BF16)

    def couplings(self):
        return [(r, h, r * self.hb + h) for r in range(self.rounds) for h in range(self.hb)]

    def forward_part(self, h):
        return pl.ds(h * self.chan, self.chan)

    def adjoint_part(self, h):
        return pl.ds(self.half + h * self.chan, self.chan)


def call(kernel, in_specs, out_specs, out_shape, scratch, flops, moved, limit, aliases=None):
    return pl.pallas_call(
        kernel,
        in_specs=in_specs,
        out_specs=out_specs,
        out_shape=out_shape,
        scratch_shapes=scratch,
        input_output_aliases=aliases or {},
        compiler_params=pltpu.CompilerParams(vmem_limit_bytes=limit << 20),
        cost_estimate=pl.CostEstimate(flops=flops, bytes_accessed=moved, transcendentals=0),
    )


def fill_pays(sz, meta, tnew, snew, cross, pays):
    for r, h, j in sz.couplings():
        pays[r][sz.forward_part(h), :] = tnew[meta[sz.sends + j]]
        term = nn(snew[meta[sz.rows + j]], cross[j])
        factor = meta[sz.flags + r].astype(F32)
        pays[r][sz.adjoint_part(h), :] = (factor * term).astype(BF16)


def pack_kernel(sz, *refs):
    x4, u4, coupling, send, row, pair, live_s, col = refs[:8]
    xb, ub, cross, across, meta, col_out = refs[8:14]
    pays = refs[14 : 14 + sz.rounds]
    send_s, row_s, pair_s, sem_x, sem_u, sem_t, sem_i = refs[14 + sz.rounds :]
    small = [
        pltpu.make_async_copy(send, send_s, sem_i.at[0]),
        pltpu.make_async_copy(row, row_s, sem_i.at[1]),
        pltpu.make_async_copy(pair, pair_s, sem_i.at[2]),
    ]
    tiles = pltpu.make_async_copy(coupling, cross, sem_t)
    copies = []
    for t in range(sz.chan // SUB):
        part = pl.ds(t * SUB, SUB)
        copies.append(pltpu.make_async_copy(x4.at[t], xb.at[:, part, :], sem_x.at[t]))
        copies.append(pltpu.make_async_copy(u4.at[t], ub.at[:, part, :], sem_u.at[t]))
    copies.append(pltpu.make_async_copy(col, col_out, sem_i.at[3]))
    for copy in small + [tiles] + copies:
        copy.start()
    for copy in small:
        copy.wait()
    count = live_s[0]
    rows = [lax.rem(row_s[0, h, r], count) for r, h, _ in sz.couplings()]
    sends = [lax.rem(send_s[0, h, r], count) for r, h, _ in sz.couplings()]
    for values, spot, first in (
        (rows, sz.rows, sz.first_row),
        (sends, sz.sends, sz.first_send),
    ):
        for j, value in enumerate(values):
            earliest = jnp.int32(j)
            for q in reversed(range(j)):
                earliest = jnp.where(values[q] == value, q, earliest)
            meta[spot + j] = value
            meta[first + j] = earliest
    for r in range(sz.rounds):
        meta[sz.flags + r] = pair_s[0, r]
    meta[sz.live] = count
    tiles.wait()
    for j in range(sz.pairs):
        across[j] = cross[j].T
    for copy in copies:
        copy.wait()

    def clear(i, carry):
        xb[i] = jnp.zeros(xb.shape[1:], BF16)
        ub[i] = jnp.zeros(ub.shape[1:], BF16)
        return carry

    lax.fori_loop(count, sz.blocks, clear, 0)
    fill_pays(sz, meta, xb, ub, cross, pays)


def keep(array):
    return pltpu.with_memory_space_constraint(array, pltpu.HBM)


def pack(sz, *args):
    args = [array if array.size == 1 else keep(array) for array in args]
    _, _, _, send, row, pair, _, col = args
    groups = sz.chan // SUB
    cross = shape((sz.pairs, sz.blk, sz.blk), BF16)
    table = shape((sz.meta,), jnp.int32)
    return call(
        functools.partial(pack_kernel, sz),
        [HBM] * 6 + [SMEM, HBM],
        [VMEM] * 4 + [SMEM, VMEM] + [VMEM] * sz.rounds,
        [sz.field, sz.field, cross, cross, table, shape(col.shape, jnp.int32)]
        + [sz.pay] * sz.rounds,
        [
            pltpu.SMEM(send.shape, jnp.int32),
            pltpu.SMEM(row.shape, jnp.int32),
            pltpu.SMEM(pair.shape, jnp.int32),
            pltpu.SemaphoreType.DMA((groups,)),
            pltpu.SemaphoreType.DMA((groups,)),
            pltpu.SemaphoreType.DMA,
            pltpu.SemaphoreType.DMA((4,)),
        ],
        1000,
        4 << 20,
        8,
    )(*args)


def big_steps(count):
    return (count + ROWS - 1) // ROWS


def clear_sums(sz, summed):
    def clear(i, carry):
        summed[i] = jnp.zeros(summed.shape[1:], F32)
        return carry

    lax.fori_loop(0, sz.blocks, clear, 0, unroll=4)


def scatter_terms(sz, summed, cols, terms):
    for m in range(sz.nz):
        summed[cols[m]] = summed[cols[m]] + terms[:, m * sz.blk : (m + 1) * sz.blk]


def finish_local(sz, meta, held, adjoint, tnew, snew, psel, qsel):
    count = meta[sz.live]

    def finish(g, carry):
        for u in range(ROWS_FIRST):
            i = g * ROWS_FIRST + u
            snew[i] = adjoint(i).astype(BF16)
        return carry

    lax.fori_loop(0, (count + ROWS_FIRST - 1) // ROWS_FIRST, finish, 0)

    def dead(i, carry):
        tnew[i] = jnp.zeros(tnew.shape[1:], BF16)
        snew[i] = jnp.zeros(snew.shape[1:], BF16)
        return carry

    lax.fori_loop(count, sz.blocks, dead, 0)
    for j in range(sz.pairs):
        psel[j] = held[meta[sz.rows + j]]
        qsel[j] = adjoint(meta[sz.sends + j])


def first_kernel(
    sz, meta, col, tiles_hbm, t0, s0, tnew, snew, psel, qsel, tiles, turned, gram, held, summed, sem
):
    count = meta[sz.live]
    steps = big_steps(count)
    loads = steps * (ROWS // ROWS_FIRST)

    def fetch(g):
        part = pl.ds(g * ROWS_FIRST, ROWS_FIRST)
        return pltpu.make_async_copy(tiles_hbm.at[part], tiles.at[part], sem.at[g])

    def start(g, carry):
        fetch(g).start()
        return carry

    lax.fori_loop(0, loads, start, 0)
    clear_sums(sz, summed)

    def products(g, total):
        spots = [g * ROWS + u for u in range(ROWS)]
        left = jnp.concatenate([t0[i] for i in spots], axis=1)
        return total + nn(left, jnp.concatenate([s0[i].T for i in spots], axis=0))

    gram[...] = lax.fori_loop(0, steps, products, jnp.zeros(gram.shape, F32))

    def block_row(i):
        cols = [col[m, i] for m in range(sz.nz)]
        parts = [tiles[i, m] for m in range(sz.nz)]
        flipped = [part.T for part in parts]
        for m in range(sz.nz):
            turned[i, pl.ds(m * sz.blk, sz.blk), :] = flipped[m]
        gathered = jnp.concatenate([t0[c] for c in cols], axis=1)
        forward = nn(gathered, jnp.concatenate(flipped, axis=0))
        held[i] = forward
        tnew[i] = forward.astype(BF16)
        scatter_terms(sz, summed, cols, nn(s0[i], jnp.concatenate(parts, axis=1)))

    def step(g, carry):
        for part in range(ROWS // ROWS_FIRST):
            fetch(g * (ROWS // ROWS_FIRST) + part).wait()
        for u in range(ROWS):
            block_row(g * ROWS + u)
        return carry

    lax.fori_loop(0, steps, step, 0)
    finish_local(sz, meta, held, lambda i: summed[i], tnew, snew, psel, qsel)


def first_products(sz, meta, col, tiles, t0, s0):
    turned = shape((sz.blocks, sz.nz * sz.blk, sz.blk), BF16)
    return call(
        functools.partial(first_kernel, sz),
        [SMEM, SMEM, HBM, VMEM, VMEM],
        [VMEM] * 7,
        [sz.field, sz.field, sz.picked, sz.picked, shape(tiles.shape, BF16), turned]
        + [shape((sz.chan, sz.chan), F32)],
        [pltpu.VMEM((sz.blocks, sz.chan, sz.blk), F32)] * 2
        + [pltpu.SemaphoreType.DMA((sz.blocks // ROWS_FIRST,))],
        4 * sz.blocks * sz.nz * sz.chan * sz.blk * sz.blk,
        12 << 20,
        24,
    )(meta, col, keep(tiles), t0, s0)


def local_kernel(sz, grad, *refs):
    meta, col, tiles, turned, tcur, scur, tprev, sprev, _ = refs[:9]
    tnew, snew, psel, qsel, last = refs[9:14]
    held, summed = refs[-2:]
    count = meta[sz.live]
    clear_sums(sz, summed)

    def block_row(i):
        cols = [col[m, i] for m in range(sz.nz)]
        gathered = jnp.concatenate([tcur[c] for c in cols], axis=1)
        forward = 2.0 * nn(gathered, turned[i]) - tprev[i].astype(F32)
        held[i] = forward
        tnew[i] = forward.astype(BF16)
        wide = jnp.concatenate([tiles[i, m] for m in range(sz.nz)], axis=1)
        scatter_terms(sz, summed, cols, nn(scur[i], wide))

    def step(g, carry):
        for u in range(ROWS):
            block_row(g * ROWS + u)
        return carry

    lax.fori_loop(0, big_steps(count), step, 0)

    def adjoint(i):
        return 2.0 * summed[i] - sprev[i].astype(F32)

    finish_local(sz, meta, held, adjoint, tnew, snew, psel, qsel)
    if not grad:
        last[...] = jnp.zeros(last.shape, F32)
        return

    def products(g, total):
        left, right = [], []
        for u in range(ROWS):
            i = g * ROWS + u
            left.append(jnp.concatenate([tcur[i], tnew[i]], axis=0))
            right.append(jnp.concatenate([sprev[i], scur[i]], axis=0).T)
        return total + nn(jnp.concatenate(left, axis=1), jnp.concatenate(right, axis=0))

    last[...] = lax.fori_loop(0, big_steps(count), products, jnp.zeros(last.shape, F32))


def local_products(sz, meta, col, tiles, turned, fields, token, grad):
    tail = shape((2 * sz.chan, 2 * sz.chan), F32) if grad else TOKEN
    return call(
        functools.partial(local_kernel, sz, grad),
        [SMEM, SMEM] + [VMEM] * 7,
        [VMEM] * 5,
        [sz.field, sz.field, sz.picked, sz.picked, tail],
        [pltpu.VMEM((sz.blocks, sz.chan, sz.blk), F32)] * 2,
        4 * sz.blocks * sz.nz * sz.chan * sz.blk * sz.blk,
        12 << 20,
        24,
    )(meta, col, tiles, turned, *fields, token)


def add_coupled(sz, scale, meta, got, across, psel, qsel, pacc, qacc, which):
    for j in range(sz.pairs):
        pacc[j] = psel[j]
        qacc[j] = qsel[j]
    terms = {}
    for r, h, j in sz.couplings():
        if r in which:
            factor = scale * meta[sz.flags + r].astype(F32)
            terms[j] = factor * nn(got[r][sz.forward_part(h), :], across[j])
            spot = meta[sz.first_row + j]
            pacc[spot] = pacc[spot] + terms[j]
            spot = meta[sz.first_send + j]
            qacc[spot] = qacc[spot] + scale * got[r][sz.adjoint_part(h), :].astype(F32)
    return terms


def couple_kernel(sz, scale, which, *refs):
    meta, across, psel, qsel = refs[:4]
    got = dict(zip(which, refs[4 : 4 + len(which)]))
    pacc, qacc = refs[-2:]
    add_coupled(sz, scale, meta, got, across, psel, qsel, pacc, qacc, which)


def couple(sz, scale, meta, across, picked, got, which, after):
    args = [meta, across, *picked, *(got[r] for r in which), *after]
    return call(
        functools.partial(couple_kernel, sz, scale, which),
        [SMEM] + [VMEM] * (len(args) - 1),
        [VMEM] * 2,
        [sz.picked] * 2,
        [],
        2 * len(which) * sz.hb * sz.chan * sz.blk * sz.blk,
        2 << 20,
        6,
    )(*args)


def correct_kernel(sz, axis, *refs):
    meta, across, psel, qsel, gram0, gram, sold = refs[:7]
    got, refs = refs[7 : 7 + sz.rounds], refs[7 + sz.rounds :]
    pacc, qacc, keep_half, give_half, whole = refs
    which = range(sz.rounds)
    terms = add_coupled(sz, 2.0, meta, got, across, psel, qsel, pacc, qacc, which)
    left = jnp.concatenate([terms[j].astype(BF16) for j in range(sz.pairs)], axis=1)
    right = [sold[meta[sz.rows + j]].T for j in range(sz.pairs)]
    extra = nn(left, jnp.concatenate(right, axis=0))
    one, two = pl.ds(0, sz.chan), pl.ds(sz.chan, sz.chan)
    whole[one, one] = gram0[...]
    whole[two, one] = gram[one, one]
    whole[two, two] = gram[one, two]
    whole[one, two] = gram[two, two] + extra
    odd = lax.rem(lax.axis_index(axis), 2)
    keep_half[...] = whole[pl.ds(pl.multiple_of(odd * sz.chan, sz.chan), sz.chan), :]
    give_half[...] = whole[pl.ds(pl.multiple_of((1 - odd) * sz.chan, sz.chan), sz.chan), :]


def correct(sz, axis, meta, across, picked, got, gram0, gram, sold):
    args = [meta, across, *picked, gram0, gram, sold, *got]
    half = shape((sz.chan, 2 * sz.chan), F32)
    return call(
        functools.partial(correct_kernel, sz, axis),
        [SMEM] + [VMEM] * (len(args) - 1),
        [VMEM] * 4,
        [sz.picked, sz.picked, half, half],
        [pltpu.VMEM((2 * sz.chan, 2 * sz.chan), F32)],
        4 * sz.pairs * sz.chan * sz.blk * sz.blk,
        3 << 20,
        8,
    )(*args)


def join_kernel(sz, *refs):
    meta, cross, tbase, sbase, pacc, qacc, tnew, snew = refs[:8]
    pays = refs[8:]

    def move(i, carry):
        tnew[i] = tbase[i]
        snew[i] = sbase[i]
        return carry

    lax.fori_loop(0, sz.blocks, move, 0, unroll=4)
    for j in range(sz.pairs):
        tnew[meta[sz.rows + j]] = pacc[meta[sz.first_row + j]].astype(BF16)
        snew[meta[sz.sends + j]] = qacc[meta[sz.first_send + j]].astype(BF16)
    fill_pays(sz, meta, tnew, snew, cross, pays)


def join(sz, meta, cross, base, picked):
    args = [meta, cross, *base, *picked]
    outs = [sz.field, sz.field] + [sz.pay] * sz.rounds
    outs = call(
        functools.partial(join_kernel, sz),
        [SMEM] + [VMEM] * (len(args) - 1),
        [VMEM] * len(outs),
        outs,
        [],
        2 * sz.pairs * sz.chan * sz.blk * sz.blk,
        5 << 20,
        8,
    )(*args)
    return outs[0], outs[1], outs[2:]


def output_weights(weight):
    wide = [weight[k].astype(F32) for k in range(weight.shape[0])]
    ahead = jnp.concatenate([w.T for w in wide], axis=1).astype(BF16)
    back = jnp.concatenate(wide, axis=1).astype(BF16)
    return ahead, back


def output_kernel(sz, low, high, *refs):
    meta, weight = refs[:2]
    forward, adjoint = refs[2:6], refs[6:10]
    refs = refs[11:] if low == 0 else refs[13:]
    out4, grad4, token, held_out, held_grad, sem = refs
    count = meta[sz.live]
    ahead, back = output_weights(weight)
    groups = sz.chan // SUB

    def block(i):
        for left, fields, held in ((ahead, forward, held_out), (back, adjoint, held_grad)):
            value = nn(left, jnp.concatenate([f[i] for f in fields], axis=0)).astype(BF16)
            for t in range(groups):
                held[t, i - low] = value[t * SUB : (t + 1) * SUB]

    def step(g, carry):
        for u in range(ROWS_FIRST):
            block(g * ROWS_FIRST + u)
        return carry

    end = jnp.minimum((count + ROWS_FIRST - 1) // ROWS_FIRST, high // ROWS_FIRST)
    lax.fori_loop(low // ROWS_FIRST, end, step, 0)

    def dead(i, carry):
        for t in range(groups):
            held_out[t, i - low] = jnp.zeros((SUB, sz.blk), BF16)
            held_grad[t, i - low] = jnp.zeros((SUB, sz.blk), BF16)
        return carry

    lax.fori_loop(jnp.maximum(count, low), high, dead, 0)
    part = pl.ds(low, high - low)
    copies = [
        pltpu.make_async_copy(held_out, out4.at[:, part], sem.at[0]),
        pltpu.make_async_copy(held_grad, grad4.at[:, part], sem.at[1]),
    ]
    for copy in copies:
        copy.start()
    token[...] = jnp.zeros(token.shape, F32)
    for copy in copies:
        copy.wait()


def base_outputs(sz, low, high, meta, weight, forward, adjoint, token, before):
    out = shape((sz.chan // SUB, sz.blocks, SUB, sz.blk), BF16)
    args = [meta, weight, *forward, *adjoint, token]
    specs = [SMEM] + [VMEM] * (len(args) - 1)
    aliases = {}
    if low > 0:
        aliases = {len(args): 0, len(args) + 1: 1}
        args += before
        specs += [HBM] * 2
    held = pltpu.VMEM((sz.chan // SUB, high - low, SUB, sz.blk), BF16)
    return call(
        functools.partial(output_kernel, sz, low, high),
        specs,
        [HBM, HBM, VMEM],
        [out, out, TOKEN],
        [held, held, pltpu.SemaphoreType.DMA((2,))],
        16 * (high - low) * sz.chan * sz.chan * sz.blk,
        10 << 20,
        8,
        aliases,
    )(*args)


def fix_kernel(sz, axis, which, *refs):
    meta, across, weight, psel, qsel = refs[:5]
    got, refs = dict(zip(which, refs[5 : 5 + len(which)])), refs[5 + len(which) :]
    forward, adjoint = refs[:3], refs[3:6]
    mine, theirs = refs[6:8]
    out4, grad4, grad_w, pacc, qacc, held_out, held_grad, sem = refs[10:]
    add_coupled(sz, 2.0, meta, got, across, psel, qsel, pacc, qacc, which)
    ahead, back = output_weights(weight)
    groups = sz.chan // SUB
    copies = []
    for j in range(sz.pairs):
        for left, fields, last, spot, first, held, out, s in (
            (ahead, forward, pacc, sz.rows, sz.first_row, held_out, out4, 0),
            (back, adjoint, qacc, sz.sends, sz.first_send, held_grad, grad4, 1),
        ):
            i, slot = meta[spot + j], meta[first + j]
            stack = [f[i] for f in fields] + [last[slot].astype(BF16)]
            value = nn(left, jnp.concatenate(stack, axis=0)).astype(BF16)
            for t in range(groups):
                held[j, t] = value[t * SUB : (t + 1) * SUB]
            copies.append((slot == j, pltpu.make_async_copy(held.at[j], out.at[:, i], sem.at[s, j])))
    for own, copy in copies:
        pl.when(own)(copy.start)
    odd = lax.rem(lax.axis_index(axis), 2) == 1
    top = jnp.where(odd, theirs[...], mine[...])
    low = jnp.where(odd, mine[...], theirs[...])
    zeroth, first = top[:, : sz.chan], low[:, : sz.chan]
    grad_w[0] = zeroth
    grad_w[1] = first
    grad_w[2] = 2.0 * low[:, sz.chan :] - zeroth
    grad_w[3] = 2.0 * top[:, sz.chan :] - first
    for own, copy in copies:
        pl.when(own)(copy.wait)


def fix_outputs(
    sz, axis, meta, across, weight, picked, got, which, forward, adjoint, mine, theirs, before
):
    out = shape(before[0].shape, BF16)
    late = [got[r] for r in which]
    args = [meta, across, weight, *picked, *late, *forward, *adjoint, mine, theirs]
    held = pltpu.VMEM((sz.pairs, sz.chan // SUB, SUB, sz.blk), BF16)
    return call(
        functools.partial(fix_kernel, sz, axis, which),
        [SMEM] + [VMEM] * (len(args) - 1) + [HBM] * 2,
        [HBM, HBM, VMEM],
        [out, out, shape((4, sz.chan, sz.chan), F32)],
        [pltpu.VMEM(sz.picked.shape, F32)] * 2 + [held, held]
        + [pltpu.SemaphoreType.DMA((2, sz.pairs))],
        8 * sz.pairs * sz.chan * sz.blk * sz.blk,
        4 << 20,
        10,
        {len(args): 0, len(args) + 1: 1},
    )(*args, *before)


def add_kernel(gated, inputs, *refs):
    mine, theirs = refs[:2]
    outs = refs[inputs:]
    if gated:
        outs[2][...] = refs[2][...]
    outs[0][...] = mine[...] + theirs[...]
    if len(outs) > 1:
        outs[1][...] = jnp.zeros(outs[1].shape, F32)


def add(mine, theirs, pay, after, last=False):
    outs = [shape(mine.shape, F32)] + ([] if last else [TOKEN])
    args = [mine, theirs]
    if pay is not None:
        outs.append(shape(pay.shape, BF16))
        args.append(pay)
    args += after
    return call(
        functools.partial(add_kernel, pay is not None, len(args)),
        [VMEM] * len(args),
        [VMEM] * len(outs),
        outs,
        [],
        mine.size,
        12 * mine.size,
        2,
    )(*args)


def from_partner(values, bit):
    count = lax.axis_size("dom")
    route = []
    for low in range(count):
        high = low | 1 << bit
        if high != low and high < count:
            route += [(low, high), (high, low)]
    return lax.ppermute(values, "dom", route)


def local(
    features,
    cheb_weight,
    lap_tiles,
    col_index,
    cross_tiles,
    send_index,
    row_index,
    pair_on,
    blk_live,
    cotangent,
):
    sz = Sizes(features, lap_tiles, cross_tiles)
    split = (sz.chan // SUB, SUB, sz.blocks, sz.blk)
    x4 = features.reshape(split).transpose(0, 2, 1, 3)
    u4 = cotangent.reshape(split).transpose(0, 2, 1, 3)
    coupling = cross_tiles.reshape(sz.pairs, sz.blk, sz.blk)
    send, row = send_index.transpose(0, 2, 1), row_index.transpose(0, 2, 1)

    packed = pack(sz, x4, u4, coupling, send, row, pair_on, blk_live, col_index.T)
    t0, s0, cross, across, meta, col = packed[:6]
    everyone = range(sz.rounds)
    got = [from_partner(pay, bit) for bit, pay in enumerate(packed[6:])]
    *base, psel, qsel, tiles, turned, gram0 = first_products(sz, meta, col, lap_tiles, t0, s0)
    picked = couple(sz, 1.0, meta, across, (psel, qsel), got, everyone, [])
    t1, s1, pays = join(sz, meta, cross, base, picked)

    got = [from_partner(pay, bit) for bit, pay in enumerate(pays)]
    fields = (t1, s1, t0, s0)
    *base, psel, qsel, gram = local_products(sz, meta, col, tiles, turned, fields, cross, True)
    *picked, mine, given = correct(
        sz, "dom", meta, across, (psel, qsel), got, gram0, gram, s1
    )
    theirs = from_partner(given, 0)
    t2, s2, pays = join(sz, meta, cross, base, picked)

    state = {}

    def window_products(token):
        fields = (t2, s2, t1, s1)
        *state["base"], token = local_products(sz, meta, col, tiles, turned, fields, token, False)
        return token

    def window_outputs(low, high):
        def window(token):
            forward = (t0, t1, t2, state["base"][0])
            adjoint = (s0, s1, s2, state["base"][1])
            out4, grad4, token = base_outputs(
                sz, low, high, meta, cheb_weight, forward, adjoint, token, state.get("outs", [])
            )
            state["outs"] = [out4, grad4]
            return token

        return window

    middle = sz.blocks // (2 * ROWS_FIRST) * ROWS_FIRST
    windows = [window_products, window_outputs(0, middle), window_outputs(middle, sz.blocks)]
    bits = list(reversed(range(1, (lax.axis_size("dom") - 1).bit_length())))
    pays, got = list(pays), [None] * sz.rounds
    got[0] = from_partner(pays[0], 0)
    early = [bit for bit in bits[:-1] if bit < sz.rounds]
    late = [bit for bit in everyone if bit not in early]
    mine, token, *rest = add(mine, theirs, pays[bits[0]] if bits[0] < sz.rounds else None, [])
    held = [got[0]]
    for at, bit in enumerate(bits):
        if bit < sz.rounds:
            pays[bit] = rest[0]
        theirs = from_partner(mine, bit)
        if bit < sz.rounds:
            got[bit] = from_partner(pays[bit], bit)
        if at < len(windows):
            token = windows[at](token)
        last = at + 1 == len(bits)
        if last:
            picked = couple(sz, 2.0, meta, across, state["base"][2:4], got, early, [token])
            token = picked[0]
        gated = not last and bits[at + 1] < sz.rounds
        after = [token] + held
        held = [got[bit]] if bit < sz.rounds else []
        if last:
            (mine,) = add(mine, theirs, None, after, True)
        else:
            mine, token, *rest = add(mine, theirs, pays[bits[at + 1]] if gated else None, after)
    theirs = from_partner(mine, 0)
    out4, grad4, grad_w = fix_outputs(
        sz,
        "dom",
        meta,
        across,
        cheb_weight,
        picked,
        got,
        late,
        (t0, t1, t2),
        (s0, s1, s2),
        mine,
        theirs,
        state["outs"],
    )
    conv_out = out4.transpose(0, 2, 1, 3).reshape(features.shape)
    grad_x = grad4.transpose(0, 2, 1, 3).reshape(features.shape)
    return (conv_out, grad_x, grad_w)


def solution(mesh):
    in_specs = (
        P(None, "dom"),
        P(),
        P("dom", None, None, None),
        P("dom", None),
        P("dom", None, None, None, None),
        P("dom", None, None),
        P("dom", None, None),
        P("dom", None),
        P("dom"),
        P(None, "dom"),
    )
    out_specs = (P(None, "dom"), P(None, "dom"), P())
    return jax.shard_map(local, mesh=mesh, in_specs=in_specs, out_specs=out_specs, check_vma=False)
```

```python
import functools

import jax
import jax.numpy as jnp
from jax import lax
from jax.experimental import pallas as pl
from jax.experimental.pallas import tpu as pltpu
from jax.sharding import PartitionSpec as P


F32 = jnp.float32
BF16 = jnp.bfloat16
SUB = 8
LANES = 128
ROWS_FIRST = 8
ROWS = 16

VMEM = pl.BlockSpec(memory_space=pltpu.VMEM)
SMEM = pl.BlockSpec(memory_space=pltpu.SMEM)
HBM = pl.BlockSpec(memory_space=pltpu.HBM)
TOKEN = jax.ShapeDtypeStruct((SUB, LANES), F32)


def shape(dims, dtype):
    return jax.ShapeDtypeStruct(dims, dtype)


def nn(a, b):
    return lax.dot_general(a, b, (((1,), (0,)), ((), ())), preferred_element_type=F32)


class Sizes:
    def __init__(self, features, lap_tiles, cross_tiles):
        self.chan = features.shape[0]
        self.blocks, self.nz, self.blk = lap_tiles.shape[:3]
        self.rounds, self.hb = cross_tiles.shape[1:3]
        self.pairs = self.rounds * self.hb
        self.rows = 0
        self.sends = self.pairs
        self.first_row = 2 * self.pairs
        self.first_send = 3 * self.pairs
        self.flags = 4 * self.pairs
        self.live = self.flags + self.rounds
        self.meta = self.live + 1
        self.half = self.hb * self.chan
        self.field = shape((self.blocks, self.chan, self.blk), BF16)
        self.picked = shape((self.pairs, self.chan, self.blk), F32)
        self.pay = shape((2 * self.half, self.blk), BF16)

    def couplings(self):
        return [(r, h, r * self.hb + h) for r in range(self.rounds) for h in range(self.hb)]

    def forward_part(self, h):
        return pl.ds(h * self.chan, self.chan)

    def adjoint_part(self, h):
        return pl.ds(self.half + h * self.chan, self.chan)


def call(kernel, in_specs, out_specs, out_shape, scratch, flops, moved, limit, aliases=None):
    return pl.pallas_call(
        kernel,
        in_specs=in_specs,
        out_specs=out_specs,
        out_shape=out_shape,
        scratch_shapes=scratch,
        input_output_aliases=aliases or {},
        compiler_params=pltpu.CompilerParams(vmem_limit_bytes=limit << 20),
        cost_estimate=pl.CostEstimate(flops=flops, bytes_accessed=moved, transcendentals=0),
    )


def fill_pays(sz, meta, tnew, snew, cross, pays):
    for r, h, j in sz.couplings():
        pays[r][sz.forward_part(h), :] = tnew[meta[sz.sends + j]]
        term = nn(snew[meta[sz.rows + j]], cross[j])
        factor = meta[sz.flags + r].astype(F32)
        pays[r][sz.adjoint_part(h), :] = (factor * term).astype(BF16)


def pack_kernel(sz, *refs):
    x4, u4, coupling, send, row, pair, live_s, col = refs[:8]
    xb, ub, cross, across, meta, col_out = refs[8:14]
    pays = refs[14 : 14 + sz.rounds]
    send_s, row_s, pair_s, sem_x, sem_u, sem_t, sem_i = refs[14 + sz.rounds :]
    small = [
        pltpu.make_async_copy(send, send_s, sem_i.at[0]),
        pltpu.make_async_copy(row, row_s, sem_i.at[1]),
        pltpu.make_async_copy(pair, pair_s, sem_i.at[2]),
    ]
    tiles = pltpu.make_async_copy(coupling, cross, sem_t)
    copies = []
    for t in range(sz.chan // SUB):
        part = pl.ds(t * SUB, SUB)
        copies.append(pltpu.make_async_copy(x4.at[t], xb.at[:, part, :], sem_x.at[t]))
        copies.append(pltpu.make_async_copy(u4.at[t], ub.at[:, part, :], sem_u.at[t]))
    copies.append(pltpu.make_async_copy(col, col_out, sem_i.at[3]))
    for copy in small + [tiles] + copies:
        copy.start()
    for copy in small:
        copy.wait()
    count = live_s[0]
    rows = [lax.rem(row_s[0, h, r], count) for r, h, _ in sz.couplings()]
    sends = [lax.rem(send_s[0, h, r], count) for r, h, _ in sz.couplings()]
    for values, spot, first in (
        (rows, sz.rows, sz.first_row),
        (sends, sz.sends, sz.first_send),
    ):
        for j, value in enumerate(values):
            earliest = jnp.int32(j)
            for q in reversed(range(j)):
                earliest = jnp.where(values[q] == value, q, earliest)
            meta[spot + j] = value
            meta[first + j] = earliest
    for r in range(sz.rounds):
        meta[sz.flags + r] = pair_s[0, r]
    meta[sz.live] = count
    tiles.wait()
    for j in range(sz.pairs):
        across[j] = cross[j].T
    for copy in copies:
        copy.wait()

    def clear(i, carry):
        xb[i] = jnp.zeros(xb.shape[1:], BF16)
        ub[i] = jnp.zeros(ub.shape[1:], BF16)
        return carry

    lax.fori_loop(count, sz.blocks, clear, 0)
    fill_pays(sz, meta, xb, ub, cross, pays)


def keep(array):
    return pltpu.with_memory_space_constraint(array, pltpu.HBM)


def pack(sz, *args):
    args = [array if array.size == 1 else keep(array) for array in args]
    _, _, _, send, row, pair, _, col = args
    groups = sz.chan // SUB
    cross = shape((sz.pairs, sz.blk, sz.blk), BF16)
    table = shape((sz.meta,), jnp.int32)
    return call(
        functools.partial(pack_kernel, sz),
        [HBM] * 6 + [SMEM, HBM],
        [VMEM] * 4 + [SMEM, VMEM] + [VMEM] * sz.rounds,
        [sz.field, sz.field, cross, cross, table, shape(col.shape, jnp.int32)]
        + [sz.pay] * sz.rounds,
        [
            pltpu.SMEM(send.shape, jnp.int32),
            pltpu.SMEM(row.shape, jnp.int32),
            pltpu.SMEM(pair.shape, jnp.int32),
            pltpu.SemaphoreType.DMA((groups,)),
            pltpu.SemaphoreType.DMA((groups,)),
            pltpu.SemaphoreType.DMA,
            pltpu.SemaphoreType.DMA((4,)),
        ],
        1000,
        4 << 20,
        8,
    )(*args)


def big_steps(count):
    return (count + ROWS - 1) // ROWS


def table_scratch(sz, col):
    return [pltpu.SMEM((sz.meta,), jnp.int32), pltpu.SMEM(col.shape, jnp.int32)]


def clear_sums(sz, summed):
    def clear(i, carry):
        summed[i] = jnp.zeros(summed.shape[1:], F32)
        return carry

    lax.fori_loop(0, sz.blocks, clear, 0, unroll=4)


def scatter_terms(sz, summed, cols, terms):
    for m in range(sz.nz):
        summed[cols[m]] = summed[cols[m]] + terms[:, m * sz.blk : (m + 1) * sz.blk]


def finish_local(sz, meta, held, adjoint, tnew, snew, psel, qsel):
    count = meta[sz.live]

    def finish(g, carry):
        for u in range(ROWS):
            i = g * ROWS + u
            snew[i] = adjoint(i).astype(BF16)
        return carry

    lax.fori_loop(0, big_steps(count), finish, 0)

    def dead(i, carry):
        tnew[i] = jnp.zeros(tnew.shape[1:], BF16)
        snew[i] = jnp.zeros(snew.shape[1:], BF16)
        return carry

    lax.fori_loop(count, sz.blocks, dead, 0)
    for j in range(sz.pairs):
        psel[j] = held[meta[sz.rows + j]]
        qsel[j] = adjoint(meta[sz.sends + j])


def first_kernel(sz, *refs):
    meta_in, col_in, tiles_hbm, t0, s0 = refs[:5]
    tnew, snew, psel, qsel, tiles, turned, gram, held, summed, meta, col, sem, sem_i = refs[5:]
    small = [
        pltpu.make_async_copy(meta_in, meta, sem_i.at[0]),
        pltpu.make_async_copy(col_in, col, sem_i.at[1]),
    ]
    for copy in small:
        copy.start()
    for copy in small:
        copy.wait()
    count = meta[sz.live]
    steps = big_steps(count)
    loads = steps * (ROWS // ROWS_FIRST)

    def fetch(g):
        part = pl.ds(g * ROWS_FIRST, ROWS_FIRST)
        return pltpu.make_async_copy(tiles_hbm.at[part], tiles.at[part], sem.at[g])

    def start(g, carry):
        fetch(g).start()
        return carry

    lax.fori_loop(0, loads, start, 0)
    clear_sums(sz, summed)

    def products(g, total):
        spots = [g * ROWS + u for u in range(ROWS)]
        left = jnp.concatenate([t0[i] for i in spots], axis=1)
        return total + nn(left, jnp.concatenate([s0[i].T for i in spots], axis=0))

    gram[...] = lax.fori_loop(0, steps, products, jnp.zeros(gram.shape, F32))

    def block_row(i):
        cols = [col[m, i] for m in range(sz.nz)]
        parts = [tiles[i, m] for m in range(sz.nz)]
        flipped = [part.T for part in parts]
        for m in range(sz.nz):
            turned[i, pl.ds(m * sz.blk, sz.blk), :] = flipped[m]
        gathered = jnp.concatenate([t0[c] for c in cols], axis=1)
        forward = nn(gathered, jnp.concatenate(flipped, axis=0))
        held[i] = forward
        tnew[i] = forward.astype(BF16)
        scatter_terms(sz, summed, cols, nn(s0[i], jnp.concatenate(parts, axis=1)))

    def step(g, carry):
        for part in range(ROWS // ROWS_FIRST):
            fetch(g * (ROWS // ROWS_FIRST) + part).wait()
        for u in range(ROWS):
            block_row(g * ROWS + u)
        return carry

    lax.fori_loop(0, steps, step, 0)
    finish_local(sz, meta, held, lambda i: summed[i], tnew, snew, psel, qsel)


def first_products(sz, meta, col, tiles, t0, s0):
    turned = shape((sz.blocks, sz.nz * sz.blk, sz.blk), BF16)
    return call(
        functools.partial(first_kernel, sz),
        [VMEM, VMEM, HBM, VMEM, VMEM],
        [VMEM] * 7,
        [sz.field, sz.field, sz.picked, sz.picked, shape(tiles.shape, BF16), turned]
        + [shape((sz.chan, sz.chan), F32)],
        [pltpu.VMEM((sz.blocks, sz.chan, sz.blk), F32)] * 2
        + table_scratch(sz, col)
        + [pltpu.SemaphoreType.DMA((sz.blocks // ROWS_FIRST,)), pltpu.SemaphoreType.DMA((2,))],
        4 * sz.blocks * sz.nz * sz.chan * sz.blk * sz.blk,
        12 << 20,
        24,
    )(meta, col, keep(tiles), t0, s0)


def local_kernel(sz, grad, *refs):
    meta_in, col_in, tiles, turned, tcur, scur, tprev, sprev, _ = refs[:9]
    tnew, snew, psel, qsel, last = refs[9:14]
    held, summed, meta, col, sem = refs[14:]
    small = [
        pltpu.make_async_copy(meta_in, meta, sem.at[0]),
        pltpu.make_async_copy(col_in, col, sem.at[1]),
    ]
    for copy in small:
        copy.start()
    clear_sums(sz, summed)
    for copy in small:
        copy.wait()
    count = meta[sz.live]

    def block_row(i):
        cols = [col[m, i] for m in range(sz.nz)]
        gathered = jnp.concatenate([tcur[c] for c in cols], axis=1)
        forward = 2.0 * nn(gathered, turned[i]) - tprev[i].astype(F32)
        held[i] = forward
        tnew[i] = forward.astype(BF16)
        wide = jnp.concatenate([tiles[i, m] for m in range(sz.nz)], axis=1)
        scatter_terms(sz, summed, cols, nn(scur[i], wide))

    def step(g, carry):
        for u in range(ROWS):
            block_row(g * ROWS + u)
        return carry

    lax.fori_loop(0, big_steps(count), step, 0)

    def adjoint(i):
        return 2.0 * summed[i] - sprev[i].astype(F32)

    finish_local(sz, meta, held, adjoint, tnew, snew, psel, qsel)
    if not grad:
        last[...] = jnp.zeros(last.shape, F32)
        return

    def products(g, total):
        left, right = [], []
        for u in range(ROWS):
            i = g * ROWS + u
            left.append(jnp.concatenate([tcur[i], tnew[i]], axis=0))
            right.append(jnp.concatenate([sprev[i], scur[i]], axis=0).T)
        return total + nn(jnp.concatenate(left, axis=1), jnp.concatenate(right, axis=0))

    last[...] = lax.fori_loop(0, big_steps(count), products, jnp.zeros(last.shape, F32))


def local_products(sz, meta, col, tiles, turned, fields, token, grad):
    tail = shape((2 * sz.chan, 2 * sz.chan), F32) if grad else TOKEN
    return call(
        functools.partial(local_kernel, sz, grad),
        [VMEM] * 9,
        [VMEM] * 5,
        [sz.field, sz.field, sz.picked, sz.picked, tail],
        [pltpu.VMEM((sz.blocks, sz.chan, sz.blk), F32)] * 2
        + table_scratch(sz, col)
        + [pltpu.SemaphoreType.DMA((2,))],
        4 * sz.blocks * sz.nz * sz.chan * sz.blk * sz.blk,
        12 << 20,
        24,
    )(meta, col, tiles, turned, *fields, token)


def add_coupled(sz, scale, meta, got, across, psel, qsel, pacc, qacc, which):
    for j in range(sz.pairs):
        pacc[j] = psel[j]
        qacc[j] = qsel[j]
    terms = {}
    for r, h, j in sz.couplings():
        if r in which:
            factor = scale * meta[sz.flags + r].astype(F32)
            terms[j] = factor * nn(got[r][sz.forward_part(h), :], across[j])
            spot = meta[sz.first_row + j]
            pacc[spot] = pacc[spot] + terms[j]
            spot = meta[sz.first_send + j]
            qacc[spot] = qacc[spot] + scale * got[r][sz.adjoint_part(h), :].astype(F32)
    return terms


def correct_kernel(sz, axis, *refs):
    meta, across, psel, qsel, gram0, gram, sold = refs[:7]
    got, refs = refs[7 : 7 + sz.rounds], refs[7 + sz.rounds :]
    pacc, qacc, keep_half, give_half, whole = refs
    which = range(sz.rounds)
    terms = add_coupled(sz, 2.0, meta, got, across, psel, qsel, pacc, qacc, which)
    left = jnp.concatenate([terms[j].astype(BF16) for j in range(sz.pairs)], axis=1)
    right = [sold[meta[sz.rows + j]].T for j in range(sz.pairs)]
    extra = nn(left, jnp.concatenate(right, axis=0))
    one, two = pl.ds(0, sz.chan), pl.ds(sz.chan, sz.chan)
    whole[one, one] = gram0[...]
    whole[two, one] = gram[one, one]
    whole[two, two] = gram[one, two]
    whole[one, two] = gram[two, two] + extra
    odd = lax.rem(lax.axis_index(axis), 2)
    keep_half[...] = whole[pl.ds(pl.multiple_of(odd * sz.chan, sz.chan), sz.chan), :]
    give_half[...] = whole[pl.ds(pl.multiple_of((1 - odd) * sz.chan, sz.chan), sz.chan), :]


def correct(sz, axis, meta, across, picked, got, gram0, gram, sold):
    args = [meta, across, *picked, gram0, gram, sold, *got]
    half = shape((sz.chan, 2 * sz.chan), F32)
    return call(
        functools.partial(correct_kernel, sz, axis),
        [SMEM] + [VMEM] * (len(args) - 1),
        [VMEM] * 4,
        [sz.picked, sz.picked, half, half],
        [pltpu.VMEM((2 * sz.chan, 2 * sz.chan), F32)],
        4 * sz.pairs * sz.chan * sz.blk * sz.blk,
        3 << 20,
        8,
    )(*args)


def patch(sz, meta, cross, tnew, snew, pacc, qacc, pays):
    for j in range(sz.pairs):
        tnew[meta[sz.rows + j]] = pacc[meta[sz.first_row + j]].astype(BF16)
        snew[meta[sz.sends + j]] = qacc[meta[sz.first_send + j]].astype(BF16)
    fill_pays(sz, meta, tnew, snew, cross, pays)


def start_kernel(sz, *refs):
    meta, cross, _, _, across, psel, qsel = refs[:7]
    got, refs = refs[7 : 7 + sz.rounds], refs[7 + sz.rounds :]
    tnew, snew = refs[:2]
    pacc, qacc = refs[-2:]
    add_coupled(sz, 1.0, meta, got, across, psel, qsel, pacc, qacc, range(sz.rounds))
    patch(sz, meta, cross, tnew, snew, pacc, qacc, refs[2:-2])


def join_kernel(sz, *refs):
    meta, cross, _, _, pacc, qacc, tnew, snew = refs[:8]
    patch(sz, meta, cross, tnew, snew, pacc, qacc, refs[8:])


def join(sz, meta, cross, base, rest, first):
    args = [meta, cross, *base, *rest]
    outs = [sz.field, sz.field] + [sz.pay] * sz.rounds
    outs = call(
        functools.partial(start_kernel if first else join_kernel, sz),
        [SMEM] + [VMEM] * (len(args) - 1),
        [VMEM] * len(outs),
        outs,
        [pltpu.VMEM(sz.picked.shape, F32)] * 2 if first else [],
        2 * sz.pairs * sz.chan * sz.blk * sz.blk,
        5 << 20,
        8,
        {2: 0, 3: 1},
    )(*args)
    return outs[0], outs[1], outs[2:]


def output_weights(weight):
    wide = [weight[k].astype(F32) for k in range(weight.shape[0])]
    ahead = jnp.concatenate([w.T for w in wide], axis=1).astype(BF16)
    back = jnp.concatenate(wide, axis=1).astype(BF16)
    return ahead, back


def output_block(sz, left, fields, held, spot):
    value = nn(left[...], jnp.concatenate(fields, axis=0)).astype(BF16)
    for t in range(sz.chan // SUB):
        held[(t,) + spot if len(spot) == 1 else (spot[1], t)] = value[t * SUB : (t + 1) * SUB]


def output_kernel(sz, low, *refs):
    forward, adjoint = refs[:4], refs[4:8]
    if low == 0:
        weight, ahead, back, held_out, held_grad = refs[8], *refs[10:]
        wide_ahead, wide_back = output_weights(weight)
        ahead[...] = wide_ahead
        back[...] = wide_back
        copies = []
    else:
        ahead, back, before_out, before_grad = refs[8:12]
        held_out, held_grad, out4, grad4, sem = refs[13:]
        part = pl.ds(0, low)
        copies = [
            pltpu.make_async_copy(before_out, out4.at[:, part], sem.at[0]),
            pltpu.make_async_copy(before_grad, grad4.at[:, part], sem.at[1]),
        ]
    for copy in copies:
        copy.start()

    def step(g, carry):
        for u in range(ROWS):
            n = g * ROWS + u
            output_block(sz, ahead, [f[low + n] for f in forward], held_out, (n,))
            output_block(sz, back, [f[low + n] for f in adjoint], held_grad, (n,))
        return carry

    lax.fori_loop(0, held_out.shape[1] // ROWS, step, 0)
    for copy in copies:
        copy.wait()


def output_weight_shape(sz, orders):
    return shape((sz.chan, orders * sz.chan), BF16)


def base_outputs(sz, low, high, forward, adjoint, rest, token, orders):
    groups = sz.chan // SUB
    held = shape((groups, high - low, SUB, sz.blk), BF16)
    whole = shape((groups, sz.blocks, SUB, sz.blk), BF16)
    args = [*forward, *adjoint, *rest, token]
    if low == 0:
        outs = [output_weight_shape(sz, orders)] * 2 + [held, held]
        specs = [VMEM] * 4
    else:
        outs = [held, held, whole, whole]
        specs = [VMEM] * 2 + [HBM] * 2
    return call(
        functools.partial(output_kernel, sz, low),
        [VMEM] * len(args),
        specs,
        outs,
        [pltpu.SemaphoreType.DMA((2,))] if low else [],
        16 * (high - low) * sz.chan * sz.chan * sz.blk,
        6 << 20,
        8,
    )(*args)


def fixed_blocks(sz, meta, which, ahead, back, forward, adjoint, pacc, qacc, held, outs, sem):
    copies, seen = [], ([], [])
    for r, h, j in sz.couplings():
        if r not in which:
            continue
        for side, (left, fields, last, spot, first) in enumerate(
            (
                (ahead, forward, pacc, sz.rows, sz.first_row),
                (back, adjoint, qacc, sz.sends, sz.first_send),
            )
        ):
            i, slot = meta[spot + j], meta[first + j]
            stack = [f[i] for f in fields] + [last[slot].astype(BF16)]
            output_block(sz, left, stack, held[side], (None, j))
            fresh = jnp.bool_(True)
            for other in seen[side]:
                fresh = jnp.logical_and(fresh, other != i)
            seen[side].append(i)
            copy = pltpu.make_async_copy(
                held[side].at[j], outs[side].at[:, i], sem.at[side, j]
            )
            copies.append((fresh, copy))
    return copies


def run_copies(copies):
    for fresh, copy in copies:
        pl.when(fresh)(copy.start)


def end_copies(copies):
    for fresh, copy in copies:
        pl.when(fresh)(copy.wait)


def early_kernel(sz, which, low, *refs):
    meta, across, psel, qsel, ahead, back = refs[:6]
    got, refs = dict(zip(which, refs[6 : 6 + len(which)])), refs[6 + len(which) :]
    forward, adjoint = refs[:3], refs[3:6]
    before_out, before_grad = refs[6:8]
    pacc, qacc, out4, grad4, held_out, held_grad, sem, sem_base = refs[11:]
    part = pl.ds(low, before_out.shape[1])
    base = [
        pltpu.make_async_copy(before_out, out4.at[:, part], sem_base.at[0]),
        pltpu.make_async_copy(before_grad, grad4.at[:, part], sem_base.at[1]),
    ]
    for copy in base:
        copy.start()
    add_coupled(sz, 2.0, meta, got, across, psel, qsel, pacc, qacc, which)
    held, outs = (held_out, held_grad), (out4, grad4)
    copies = fixed_blocks(
        sz, meta, which, ahead, back, forward, adjoint, pacc, qacc, held, outs, sem
    )
    for copy in base:
        copy.wait()
    run_copies(copies)
    end_copies(copies)


def fix_kernel(sz, axis, which, *refs):
    meta, across, psel, qsel, ahead, back = refs[:6]
    got, refs = dict(zip(which, refs[6 : 6 + len(which)])), refs[6 + len(which) :]
    forward, adjoint = refs[:3], refs[3:6]
    mine, theirs = refs[6:8]
    out4, grad4, grad_w, pacc, qacc, held_out, held_grad, sem = refs[10:]
    add_coupled(sz, 2.0, meta, got, across, psel, qsel, pacc, qacc, which)
    held, outs = (held_out, held_grad), (out4, grad4)
    copies = fixed_blocks(
        sz, meta, which, ahead, back, forward, adjoint, pacc, qacc, held, outs, sem
    )
    run_copies(copies)
    odd = lax.rem(lax.axis_index(axis), 2) == 1
    top = jnp.where(odd, theirs[...], mine[...])
    low = jnp.where(odd, mine[...], theirs[...])
    zeroth, first = top[:, : sz.chan], low[:, : sz.chan]
    grad_w[0] = zeroth
    grad_w[1] = first
    grad_w[2] = 2.0 * low[:, sz.chan :] - zeroth
    grad_w[3] = 2.0 * top[:, sz.chan :] - first
    end_copies(copies)


def fix_outputs(sz, kernel, meta, across, picked, weights, got, which, fields, rest, token, outs, limit):
    late = [got[r] for r in which]
    args = [meta, across, *picked, *weights, *late, *fields, *rest, *token]
    whole = [shape(out.shape, BF16) for out in outs]
    held = pltpu.VMEM((sz.pairs, sz.chan // SUB, SUB, sz.blk), BF16)
    scratch = [held, held, pltpu.SemaphoreType.DMA((2, sz.pairs))]
    if token:
        results = [sz.picked, sz.picked] + whole
        specs, at = [VMEM] * 2 + [HBM] * 2, 2
        scratch.append(pltpu.SemaphoreType.DMA((2,)))
    else:
        results = whole + [shape((4, sz.chan, sz.chan), F32)]
        specs, at = [HBM] * 2 + [VMEM], 0
        scratch = [pltpu.VMEM(sz.picked.shape, F32)] * 2 + scratch
    return call(
        kernel,
        [SMEM] + [VMEM] * (len(args) - 1) + [HBM] * 2,
        specs,
        results,
        scratch,
        8 * sz.pairs * sz.chan * sz.blk * sz.blk,
        4 << 20,
        limit,
        {len(args): at, len(args) + 1: at + 1},
    )(*args, *outs)


def add_kernel(gated, inputs, *refs):
    mine, theirs = refs[:2]
    outs = refs[inputs:]
    if gated:
        outs[2][...] = refs[2][...]
    outs[0][...] = mine[...] + theirs[...]
    if len(outs) > 1:
        outs[1][...] = jnp.zeros(outs[1].shape, F32)


def add(mine, theirs, pay, after, last=False):
    outs = [shape(mine.shape, F32)] + ([] if last else [TOKEN])
    args = [mine, theirs]
    if pay is not None:
        outs.append(shape(pay.shape, BF16))
        args.append(pay)
    args += after
    return call(
        functools.partial(add_kernel, pay is not None, len(args)),
        [VMEM] * len(args),
        [VMEM] * len(outs),
        outs,
        [],
        mine.size,
        12 * mine.size,
        2,
    )(*args)


def from_partner(values, bit):
    count = lax.axis_size("dom")
    route = []
    for low in range(count):
        high = low | 1 << bit
        if high != low and high < count:
            route += [(low, high), (high, low)]
    return lax.ppermute(values, "dom", route)


def local(
    features,
    cheb_weight,
    lap_tiles,
    col_index,
    cross_tiles,
    send_index,
    row_index,
    pair_on,
    blk_live,
    cotangent,
):
    sz = Sizes(features, lap_tiles, cross_tiles)
    split = (sz.chan // SUB, SUB, sz.blocks, sz.blk)
    x4 = features.reshape(split).transpose(0, 2, 1, 3)
    u4 = cotangent.reshape(split).transpose(0, 2, 1, 3)
    coupling = cross_tiles.reshape(sz.pairs, sz.blk, sz.blk)
    send, row = send_index.transpose(0, 2, 1), row_index.transpose(0, 2, 1)

    packed = pack(sz, x4, u4, coupling, send, row, pair_on, blk_live, col_index.T)
    t0, s0, cross, across, meta, col = packed[:6]
    everyone = range(sz.rounds)
    got = [from_partner(pay, bit) for bit, pay in enumerate(packed[6:])]
    *base, psel, qsel, tiles, turned, gram0 = first_products(sz, meta, col, lap_tiles, t0, s0)
    t1, s1, pays = join(sz, meta, cross, base, [across, psel, qsel, *got], True)

    got = [from_partner(pay, bit) for bit, pay in enumerate(pays)]
    fields = (t1, s1, t0, s0)
    *base, psel, qsel, gram = local_products(sz, meta, col, tiles, turned, fields, cross, True)
    *picked, mine, given = correct(
        sz, "dom", meta, across, (psel, qsel), got, gram0, gram, s1
    )
    theirs = from_partner(given, 0)
    t2, s2, pays = join(sz, meta, cross, base, picked, False)

    state = {}

    def window_products(token):
        fields = (t2, s2, t1, s1)
        *state["base"], token = local_products(sz, meta, col, tiles, turned, fields, token, False)
        return token

    middle = sz.blocks // (2 * ROWS) * ROWS
    orders = cheb_weight.shape[0]

    def window_low(token):
        forward, adjoint = (t0, t1, t2, state["base"][0]), (s0, s1, s2, state["base"][1])
        *state["weights"], left, right = base_outputs(
            sz, 0, middle, forward, adjoint, [cheb_weight], token, orders
        )
        state["low"] = [left, right]
        return state["weights"][0]

    def window_high(token):
        forward, adjoint = (t0, t1, t2, state["base"][0]), (s0, s1, s2, state["base"][1])
        rest = state["weights"] + state["low"]
        left, right, out4, grad4 = base_outputs(
            sz, middle, sz.blocks, forward, adjoint, rest, token, orders
        )
        state["high"], state["outs"] = [left, right], [out4, grad4]
        return left

    windows = [window_products, window_low, window_high]
    bits = list(reversed(range(1, (lax.axis_size("dom") - 1).bit_length())))
    pays, got = list(pays), [None] * sz.rounds
    got[0] = from_partner(pays[0], 0)
    early = [0] + [bit for bit in bits[:-1] if bit < sz.rounds]
    late = [bit for bit in everyone if bit not in early]
    mine, token, *rest = add(mine, theirs, pays[bits[0]] if bits[0] < sz.rounds else None, [])
    held = [got[0]]
    for at, bit in enumerate(bits):
        if bit < sz.rounds:
            pays[bit] = rest[0]
        theirs = from_partner(mine, bit)
        if bit < sz.rounds:
            got[bit] = from_partner(pays[bit], bit)
        if at < len(windows):
            token = windows[at](token)
        last = at + 1 == len(bits)
        if last:
            *picked, out4, grad4 = fix_outputs(
                sz,
                functools.partial(early_kernel, sz, early, middle),
                meta,
                across,
                state["base"][2:4],
                state["weights"],
                got,
                early,
                (t0, t1, t2, s0, s1, s2),
                state["high"],
                [token],
                state["outs"],
                10,
            )
            token = picked[0]
        gated = not last and bits[at + 1] < sz.rounds
        after = [token] + held
        held = [got[bit]] if bit < sz.rounds else []
        if last:
            (mine,) = add(mine, theirs, None, after, True)
        else:
            mine, token, *rest = add(mine, theirs, pays[bits[at + 1]] if gated else None, after)
    theirs = from_partner(mine, 0)
    out4, grad4, grad_w = fix_outputs(
        sz,
        functools.partial(fix_kernel, sz, "dom", late),
        meta,
        across,
        picked,
        state["weights"],
        got,
        late,
        (t0, t1, t2, s0, s1, s2),
        [mine, theirs],
        [],
        [out4, grad4],
        10,
    )
    conv_out = out4.transpose(0, 2, 1, 3).reshape(features.shape)
    grad_x = grad4.transpose(0, 2, 1, 3).reshape(features.shape)
    return (conv_out, grad_x, grad_w)


def solution(mesh):
    in_specs = (
        P(None, "dom"),
        P(),
        P("dom", None, None, None),
        P("dom", None),
        P("dom", None, None, None, None),
        P("dom", None, None),
        P("dom", None, None),
        P("dom", None),
        P("dom"),
        P(None, "dom"),
    )
    out_specs = (P(None, "dom"), P(None, "dom"), P())
    return jax.shard_map(local, mesh=mesh, in_specs=in_specs, out_specs=out_specs, check_vma=False)
```

```python
import functools

import jax
import jax.numpy as jnp
from jax import lax
from jax.experimental import pallas as pl
from jax.experimental.pallas import tpu as pltpu
from jax.sharding import PartitionSpec as P


F32 = jnp.float32
BF16 = jnp.bfloat16
SUB = 8
LANES = 128
ROWS_FIRST = 8
ROWS = 16

VMEM = pl.BlockSpec(memory_space=pltpu.VMEM)
SMEM = pl.BlockSpec(memory_space=pltpu.SMEM)
HBM = pl.BlockSpec(memory_space=pltpu.HBM)
TOKEN = jax.ShapeDtypeStruct((SUB, LANES), F32)


def shape(dims, dtype):
    return jax.ShapeDtypeStruct(dims, dtype)


def nn(a, b):
    return lax.dot_general(a, b, (((1,), (0,)), ((), ())), preferred_element_type=F32)


class Sizes:
    def __init__(self, features, lap_tiles, cross_tiles):
        self.chan = features.shape[0]
        self.blocks, self.nz, self.blk = lap_tiles.shape[:3]
        self.rounds, self.hb = cross_tiles.shape[1:3]
        self.pairs = self.rounds * self.hb
        self.rows = 0
        self.sends = self.pairs
        self.first_row = 2 * self.pairs
        self.first_send = 3 * self.pairs
        self.flags = 4 * self.pairs
        self.live = self.flags + self.rounds
        self.meta = self.live + 1
        self.half = self.hb * self.chan
        self.field = shape((self.blocks, self.chan, self.blk), BF16)
        self.picked = shape((self.pairs, self.chan, self.blk), F32)
        self.pay = shape((2 * self.half, self.blk), BF16)

    def couplings(self):
        return [(r, h, r * self.hb + h) for r in range(self.rounds) for h in range(self.hb)]

    def forward_part(self, h):
        return pl.ds(h * self.chan, self.chan)

    def adjoint_part(self, h):
        return pl.ds(self.half + h * self.chan, self.chan)


def call(kernel, in_specs, out_specs, out_shape, scratch, flops, moved, limit, aliases=None):
    return pl.pallas_call(
        kernel,
        in_specs=in_specs,
        out_specs=out_specs,
        out_shape=out_shape,
        scratch_shapes=scratch,
        input_output_aliases=aliases or {},
        compiler_params=pltpu.CompilerParams(vmem_limit_bytes=limit << 20),
        cost_estimate=pl.CostEstimate(flops=flops, bytes_accessed=moved, transcendentals=0),
    )


def fill_pays(sz, meta, tnew, snew, cross, pays):
    for r, h, j in sz.couplings():
        pays[r][sz.forward_part(h), :] = tnew[meta[sz.sends + j]]
        term = nn(snew[meta[sz.rows + j]], cross[j])
        factor = meta[sz.flags + r].astype(F32)
        pays[r][sz.adjoint_part(h), :] = (factor * term).astype(BF16)


def pack_kernel(sz, *refs):
    x4, u4, coupling, send, row, pair, live_s, col = refs[:8]
    xb, ub, cross, across, meta, col_out = refs[8:14]
    pays = refs[14 : 14 + sz.rounds]
    send_s, row_s, pair_s, sem_x, sem_u, sem_t, sem_i = refs[14 + sz.rounds :]
    small = [
        pltpu.make_async_copy(send, send_s, sem_i.at[0]),
        pltpu.make_async_copy(row, row_s, sem_i.at[1]),
        pltpu.make_async_copy(pair, pair_s, sem_i.at[2]),
    ]
    tiles = pltpu.make_async_copy(coupling, cross, sem_t)
    copies = []
    for t in range(sz.chan // SUB):
        part = pl.ds(t * SUB, SUB)
        copies.append(pltpu.make_async_copy(x4.at[t], xb.at[:, part, :], sem_x.at[t]))
        copies.append(pltpu.make_async_copy(u4.at[t], ub.at[:, part, :], sem_u.at[t]))
    copies.append(pltpu.make_async_copy(col, col_out, sem_i.at[3]))
    for copy in small + [tiles] + copies:
        copy.start()
    for copy in small:
        copy.wait()
    count = live_s[0]
    rows = [lax.rem(row_s[0, h, r], count) for r, h, _ in sz.couplings()]
    sends = [lax.rem(send_s[0, h, r], count) for r, h, _ in sz.couplings()]
    for values, spot, first in (
        (rows, sz.rows, sz.first_row),
        (sends, sz.sends, sz.first_send),
    ):
        for j, value in enumerate(values):
            earliest = jnp.int32(j)
            for q in reversed(range(j)):
                earliest = jnp.where(values[q] == value, q, earliest)
            meta[spot + j] = value
            meta[first + j] = earliest
    for r in range(sz.rounds):
        meta[sz.flags + r] = pair_s[0, r]
    meta[sz.live] = count
    tiles.wait()
    for j in range(sz.pairs):
        across[j] = cross[j].T
    for copy in copies:
        copy.wait()

    def clear(i, carry):
        xb[i] = jnp.zeros(xb.shape[1:], BF16)
        ub[i] = jnp.zeros(ub.shape[1:], BF16)
        return carry

    lax.fori_loop(count, sz.blocks, clear, 0)
    fill_pays(sz, meta, xb, ub, cross, pays)


def keep(array):
    return pltpu.with_memory_space_constraint(array, pltpu.HBM)


def pack(sz, *args):
    args = [array if array.size == 1 else keep(array) for array in args]
    _, _, _, send, row, pair, _, col = args
    groups = sz.chan // SUB
    cross = shape((sz.pairs, sz.blk, sz.blk), BF16)
    table = shape((sz.meta,), jnp.int32)
    return call(
        functools.partial(pack_kernel, sz),
        [HBM] * 6 + [SMEM, HBM],
        [VMEM] * 4 + [SMEM, VMEM] + [VMEM] * sz.rounds,
        [sz.field, sz.field, cross, cross, table, shape(col.shape, jnp.int32)]
        + [sz.pay] * sz.rounds,
        [
            pltpu.SMEM(send.shape, jnp.int32),
            pltpu.SMEM(row.shape, jnp.int32),
            pltpu.SMEM(pair.shape, jnp.int32),
            pltpu.SemaphoreType.DMA((groups,)),
            pltpu.SemaphoreType.DMA((groups,)),
            pltpu.SemaphoreType.DMA,
            pltpu.SemaphoreType.DMA((4,)),
        ],
        1000,
        4 << 20,
        8,
    )(*args)


def big_steps(count):
    return (count + ROWS - 1) // ROWS


def table_scratch(sz, col):
    return [pltpu.SMEM((sz.meta,), jnp.int32), pltpu.SMEM(col.shape, jnp.int32)]


def clear_sums(sz, summed):
    def clear(i, carry):
        summed[i] = jnp.zeros(summed.shape[1:], F32)
        return carry

    lax.fori_loop(0, sz.blocks, clear, 0, unroll=4)


def scatter_terms(sz, summed, cols, terms):
    for m in range(sz.nz):
        summed[cols[m]] = summed[cols[m]] + terms[:, m * sz.blk : (m + 1) * sz.blk]


def finish_local(sz, meta, held, adjoint, tnew, snew, psel, qsel):
    count = meta[sz.live]

    def finish(g, carry):
        for u in range(ROWS):
            i = g * ROWS + u
            snew[i] = adjoint(i).astype(BF16)
        return carry

    lax.fori_loop(0, big_steps(count), finish, 0)

    def dead(i, carry):
        tnew[i] = jnp.zeros(tnew.shape[1:], BF16)
        snew[i] = jnp.zeros(snew.shape[1:], BF16)
        return carry

    lax.fori_loop(count, sz.blocks, dead, 0)
    for j in range(sz.pairs):
        psel[j] = held[meta[sz.rows + j]]
        qsel[j] = adjoint(meta[sz.sends + j])


def first_kernel(sz, *refs):
    meta_in, col_in, tiles_hbm, t0, s0 = refs[:5]
    tnew, snew, psel, qsel, tiles, turned, gram, held, summed, meta, col, sem, sem_i = refs[5:]
    small = [
        pltpu.make_async_copy(meta_in, meta, sem_i.at[0]),
        pltpu.make_async_copy(col_in, col, sem_i.at[1]),
    ]
    for copy in small:
        copy.start()
    for copy in small:
        copy.wait()
    count = meta[sz.live]
    steps = big_steps(count)
    loads = steps * (ROWS // ROWS_FIRST)

    def fetch(g):
        part = pl.ds(g * ROWS_FIRST, ROWS_FIRST)
        return pltpu.make_async_copy(tiles_hbm.at[part], tiles.at[part], sem.at[g])

    def start(g, carry):
        fetch(g).start()
        return carry

    lax.fori_loop(0, loads, start, 0)
    clear_sums(sz, summed)

    def products(g, total):
        spots = [g * ROWS + u for u in range(ROWS)]
        left = jnp.concatenate([t0[i] for i in spots], axis=1)
        return total + nn(left, jnp.concatenate([s0[i].T for i in spots], axis=0))

    gram[...] = lax.fori_loop(0, steps, products, jnp.zeros(gram.shape, F32))

    def block_row(i):
        cols = [col[m, i] for m in range(sz.nz)]
        parts = [tiles[i, m] for m in range(sz.nz)]
        flipped = [part.T for part in parts]
        for m in range(sz.nz):
            turned[i, pl.ds(m * sz.blk, sz.blk), :] = flipped[m]
        gathered = jnp.concatenate([t0[c] for c in cols], axis=1)
        forward = nn(gathered, jnp.concatenate(flipped, axis=0))
        held[i] = forward
        tnew[i] = forward.astype(BF16)
        scatter_terms(sz, summed, cols, nn(s0[i], jnp.concatenate(parts, axis=1)))

    def step(g, carry):
        for part in range(ROWS // ROWS_FIRST):
            fetch(g * (ROWS // ROWS_FIRST) + part).wait()
        for u in range(ROWS):
            block_row(g * ROWS + u)
        return carry

    lax.fori_loop(0, steps, step, 0)
    finish_local(sz, meta, held, lambda i: summed[i], tnew, snew, psel, qsel)


def first_products(sz, meta, col, tiles, t0, s0):
    turned = shape((sz.blocks, sz.nz * sz.blk, sz.blk), BF16)
    return call(
        functools.partial(first_kernel, sz),
        [VMEM, VMEM, HBM, VMEM, VMEM],
        [VMEM] * 7,
        [sz.field, sz.field, sz.picked, sz.picked, shape(tiles.shape, BF16), turned]
        + [shape((sz.chan, sz.chan), F32)],
        [pltpu.VMEM((sz.blocks, sz.chan, sz.blk), F32)] * 2
        + table_scratch(sz, col)
        + [pltpu.SemaphoreType.DMA((sz.blocks // ROWS_FIRST,)), pltpu.SemaphoreType.DMA((2,))],
        4 * sz.blocks * sz.nz * sz.chan * sz.blk * sz.blk,
        12 << 20,
        24,
    )(meta, col, keep(tiles), t0, s0)


def row_products(sz, col, low, high, arrays, tnew, held, summed):
    tiles, turned, tcur, scur, tprev = arrays

    def block_row(i):
        cols = [col[m, i] for m in range(sz.nz)]
        gathered = jnp.concatenate([tcur[c] for c in cols], axis=1)
        forward = 2.0 * nn(gathered, turned[i]) - tprev[i].astype(F32)
        held[i] = forward
        tnew[i] = forward.astype(BF16)
        wide = jnp.concatenate([tiles[i, m] for m in range(sz.nz)], axis=1)
        scatter_terms(sz, summed, cols, nn(scur[i], wide))

    def step(g, carry):
        for u in range(ROWS):
            block_row(g * ROWS + u)
        return carry

    lax.fori_loop(low, high, step, 0)


def start_table(meta_in, col_in, meta, col, sem):
    small = [
        pltpu.make_async_copy(meta_in, meta, sem.at[0]),
        pltpu.make_async_copy(col_in, col, sem.at[1]),
    ]
    for copy in small:
        copy.start()
    return small


def local_kernel(sz, *refs):
    meta_in, col_in, tiles, turned, tcur, scur, tprev, sprev = refs[:8]
    tnew, snew, psel, qsel, gram, held, summed, meta, col, sem = refs[8:]
    small = start_table(meta_in, col_in, meta, col, sem)
    clear_sums(sz, summed)
    for copy in small:
        copy.wait()
    steps = big_steps(meta[sz.live])
    arrays = (tiles, turned, tcur, scur, tprev)
    row_products(sz, col, 0, steps, arrays, tnew, held, summed)

    def adjoint(i):
        return 2.0 * summed[i] - sprev[i].astype(F32)

    finish_local(sz, meta, held, adjoint, tnew, snew, psel, qsel)

    def products(g, total):
        left, right = [], []
        for u in range(ROWS):
            i = g * ROWS + u
            left.append(jnp.concatenate([tcur[i], tnew[i]], axis=0))
            right.append(jnp.concatenate([sprev[i], scur[i]], axis=0).T)
        return total + nn(jnp.concatenate(left, axis=1), jnp.concatenate(right, axis=0))

    gram[...] = lax.fori_loop(0, steps, products, jnp.zeros(gram.shape, F32))


def local_products(sz, meta, col, tiles, turned, fields):
    gram = shape((2 * sz.chan, 2 * sz.chan), F32)
    return call(
        functools.partial(local_kernel, sz),
        [VMEM] * 8,
        [VMEM] * 5,
        [sz.field, sz.field, sz.picked, sz.picked, gram],
        [pltpu.VMEM((sz.blocks, sz.chan, sz.blk), F32)] * 2
        + table_scratch(sz, col)
        + [pltpu.SemaphoreType.DMA((2,))],
        4 * sz.blocks * sz.nz * sz.chan * sz.blk * sz.blk,
        12 << 20,
        24,
    )(meta, col, tiles, turned, *fields)


def early_rows_kernel(sz, *refs):
    meta_in, col_in, tiles, turned, tcur, scur, tprev, _ = refs[:8]
    tnew, held, summed, meta, col, sem = refs[8:]
    small = start_table(meta_in, col_in, meta, col, sem)
    clear_sums(sz, summed)
    for copy in small:
        copy.wait()
    cut = (3 * big_steps(meta[sz.live])) // 4
    arrays = (tiles, turned, tcur, scur, tprev)
    row_products(sz, col, 0, cut, arrays, tnew, held, summed)


def late_rows_kernel(sz, *refs):
    meta_in, col_in, tiles, turned, tcur, scur, tprev, sprev = refs[:8]
    tnew, held, summed, snew, psel, qsel, meta, col, sem = refs[12:]
    for copy in start_table(meta_in, col_in, meta, col, sem):
        copy.wait()
    steps = big_steps(meta[sz.live])
    arrays = (tiles, turned, tcur, scur, tprev)
    row_products(sz, col, (3 * steps) // 4, steps, arrays, tnew, held, summed)

    def adjoint(i):
        return 2.0 * summed[i] - sprev[i].astype(F32)

    finish_local(sz, meta, held, adjoint, tnew, snew, psel, qsel)


def part_products(sz, meta, col, tiles, turned, fields, before, token):
    sums = shape((sz.blocks, sz.chan, sz.blk), F32)
    args = [meta, col, tiles, turned, *fields]
    outs, aliases = [sz.field, sums, sums], {}
    if before is None:
        args[-1] = token
    else:
        aliases = {len(args) + k: k for k in range(3)}
        args += [*before, token]
        outs += [sz.field, sz.picked, sz.picked]
    return call(
        functools.partial(early_rows_kernel if before is None else late_rows_kernel, sz),
        [VMEM] * len(args),
        [VMEM] * len(outs),
        outs,
        table_scratch(sz, col) + [pltpu.SemaphoreType.DMA((2,))],
        2 * sz.blocks * sz.nz * sz.chan * sz.blk * sz.blk,
        6 << 20,
        8,
        aliases,
    )(*args)


def add_coupled(sz, scale, table, got, across, psel, qsel, pacc, qacc, which):
    meta_in, meta, sem = table
    copy = pltpu.make_async_copy(meta_in, meta, sem)
    copy.start()
    for j in range(sz.pairs):
        pacc[j] = psel[j]
        qacc[j] = qsel[j]
    some = [(r, h, j) for r, h, j in sz.couplings() if r in which]
    terms = {j: nn(got[r][sz.forward_part(h), :], across[j]) for r, h, j in some}
    copy.wait()
    for r, h, j in some:
        terms[j] = (scale * meta[sz.flags + r].astype(F32)) * terms[j]
        spot = meta[sz.first_row + j]
        pacc[spot] = pacc[spot] + terms[j]
        spot = meta[sz.first_send + j]
        qacc[spot] = qacc[spot] + scale * got[r][sz.adjoint_part(h), :].astype(F32)
    return terms


def table_copy(sz):
    return [pltpu.SMEM((sz.meta,), jnp.int32), pltpu.SemaphoreType.DMA]


def correct_kernel(sz, axis, *refs):
    meta_in, across, psel, qsel, gram0, gram, sold = refs[:7]
    got, refs = refs[7 : 7 + sz.rounds], refs[7 + sz.rounds :]
    pacc, qacc, keep_half, give_half, whole, meta, sem = refs
    which, table = range(sz.rounds), (meta_in, meta, sem)
    terms = add_coupled(sz, 2.0, table, got, across, psel, qsel, pacc, qacc, which)
    left = jnp.concatenate([terms[j].astype(BF16) for j in range(sz.pairs)], axis=1)
    right = [sold[meta[sz.rows + j]].T for j in range(sz.pairs)]
    extra = nn(left, jnp.concatenate(right, axis=0))
    one, two = pl.ds(0, sz.chan), pl.ds(sz.chan, sz.chan)
    whole[one, one] = gram0[...]
    whole[two, one] = gram[one, one]
    whole[two, two] = gram[one, two]
    whole[one, two] = gram[two, two] + extra
    odd = lax.rem(lax.axis_index(axis), 2)
    keep_half[...] = whole[pl.ds(pl.multiple_of(odd * sz.chan, sz.chan), sz.chan), :]
    give_half[...] = whole[pl.ds(pl.multiple_of((1 - odd) * sz.chan, sz.chan), sz.chan), :]


def correct(sz, axis, meta, across, picked, got, gram0, gram, sold):
    args = [meta, across, *picked, gram0, gram, sold, *got]
    half = shape((sz.chan, 2 * sz.chan), F32)
    return call(
        functools.partial(correct_kernel, sz, axis),
        [VMEM] * len(args),
        [VMEM] * 4,
        [sz.picked, sz.picked, half, half],
        [pltpu.VMEM((2 * sz.chan, 2 * sz.chan), F32)] + table_copy(sz),
        4 * sz.pairs * sz.chan * sz.blk * sz.blk,
        3 << 20,
        8,
    )(*args)


def patch(sz, meta, cross, tnew, snew, pacc, qacc, pays):
    for j in range(sz.pairs):
        tnew[meta[sz.rows + j]] = pacc[meta[sz.first_row + j]].astype(BF16)
        snew[meta[sz.sends + j]] = qacc[meta[sz.first_send + j]].astype(BF16)
    fill_pays(sz, meta, tnew, snew, cross, pays)


def start_kernel(sz, *refs):
    meta_in, cross, _, _, across, psel, qsel = refs[:7]
    got, refs = refs[7 : 7 + sz.rounds], refs[7 + sz.rounds :]
    tnew, snew = refs[:2]
    pacc, qacc, meta, sem = refs[-4:]
    table = (meta_in, meta, sem)
    add_coupled(sz, 1.0, table, got, across, psel, qsel, pacc, qacc, range(sz.rounds))
    patch(sz, meta, cross, tnew, snew, pacc, qacc, refs[2:-4])


def join_kernel(sz, *refs):
    meta, cross, _, _, pacc, qacc, tnew, snew = refs[:8]
    patch(sz, meta, cross, tnew, snew, pacc, qacc, refs[8:])


def join(sz, meta, cross, base, rest, first):
    args = [meta, cross, *base, *rest]
    outs = [sz.field, sz.field] + [sz.pay] * sz.rounds
    outs = call(
        functools.partial(start_kernel if first else join_kernel, sz),
        [VMEM if first else SMEM] + [VMEM] * (len(args) - 1),
        [VMEM] * len(outs),
        outs,
        [pltpu.VMEM(sz.picked.shape, F32)] * 2 + table_copy(sz) if first else [],
        2 * sz.pairs * sz.chan * sz.blk * sz.blk,
        5 << 20,
        8,
        {2: 0, 3: 1},
    )(*args)
    return outs[0], outs[1], outs[2:]


def output_weights(weight):
    wide = [weight[k].astype(F32) for k in range(weight.shape[0])]
    ahead = jnp.concatenate([w.T for w in wide], axis=1).astype(BF16)
    back = jnp.concatenate(wide, axis=1).astype(BF16)
    return ahead, back


def output_block(sz, left, fields, held, spot):
    value = nn(left[...], jnp.concatenate(fields, axis=0)).astype(BF16)
    for t in range(sz.chan // SUB):
        held[(t,) + spot if len(spot) == 1 else (spot[1], t)] = value[t * SUB : (t + 1) * SUB]


def output_kernel(sz, middle, *refs):
    forward, adjoint, weight = refs[:4], refs[4:8], refs[8]
    ahead, back, high_out, high_grad, out4, grad4, low_out, low_grad, sem = refs[10:]
    wide_ahead, wide_back = output_weights(weight)
    ahead[...] = wide_ahead
    back[...] = wide_back

    def half(low, count, held_out, held_grad):
        def step(g, carry):
            for u in range(ROWS):
                n = g * ROWS + u
                output_block(sz, ahead, [f[low + n] for f in forward], held_out, (n,))
                output_block(sz, back, [f[low + n] for f in adjoint], held_grad, (n,))
            return carry

        lax.fori_loop(0, count // ROWS, step, 0)

    half(0, middle, low_out, low_grad)
    part = pl.ds(0, middle)
    copies = [
        pltpu.make_async_copy(low_out, out4.at[:, part], sem.at[0]),
        pltpu.make_async_copy(low_grad, grad4.at[:, part], sem.at[1]),
    ]
    for copy in copies:
        copy.start()
    half(middle, sz.blocks - middle, high_out, high_grad)
    for copy in copies:
        copy.wait()


def base_outputs(sz, middle, forward, adjoint, weight, token):
    groups = sz.chan // SUB
    high = shape((groups, sz.blocks - middle, SUB, sz.blk), BF16)
    whole = shape((groups, sz.blocks, SUB, sz.blk), BF16)
    wide = shape((sz.chan, weight.shape[0] * sz.chan), BF16)
    args = [*forward, *adjoint, weight, token]
    return call(
        functools.partial(output_kernel, sz, middle),
        [VMEM] * len(args),
        [VMEM] * 4 + [HBM] * 2,
        [wide, wide, high, high, whole, whole],
        [pltpu.VMEM((groups, middle, SUB, sz.blk), BF16)] * 2 + [pltpu.SemaphoreType.DMA((2,))],
        16 * sz.blocks * sz.chan * sz.chan * sz.blk,
        6 << 20,
        10,
    )(*args)


def fixed_blocks(sz, meta, which, weights, fields, last, held):
    for r, h, j in sz.couplings():
        if r in which:
            for side, spot, first in ((0, sz.rows, sz.first_row), (1, sz.sends, sz.first_send)):
                i = meta[spot + j]
                stack = [f[i] for f in fields[3 * side : 3 * side + 3]]
                stack.append(last[side][meta[first + j]].astype(BF16))
                output_block(sz, weights[side], stack, held[side], (None, j))


def fixed_copies(sz, meta, which, over, held, outs, sem):
    copies = []
    for side, spot in ((0, sz.rows), (1, sz.sends)):
        seen = [meta[spot + j] for r, h, j in sz.couplings() if r in over]
        for r, h, j in sz.couplings():
            if r in which:
                i = meta[spot + j]
                fresh = jnp.bool_(True)
                for other in seen:
                    fresh = jnp.logical_and(fresh, other != i)
                seen.append(i)
                copy = pltpu.make_async_copy(
                    held[side].at[j], outs[side].at[:, i], sem.at[side, j]
                )
                copies.append((fresh, copy))
    return copies


def early_kernel(sz, which, low, *refs):
    meta_in, across, psel, qsel = refs[:4]
    got, refs = dict(zip(which, refs[4 : 4 + len(which)])), refs[4 + len(which) :]
    weights, fields, high = refs[:2], refs[2:8], refs[8:10]
    pacc, qacc, held_out, held_grad, out4, grad4, meta, sem, sem_base = refs[13:]
    part = pl.ds(low, high[0].shape[1])
    base = [
        pltpu.make_async_copy(high[0], out4.at[:, part], sem_base.at[0]),
        pltpu.make_async_copy(high[1], grad4.at[:, part], sem_base.at[1]),
    ]
    for copy in base:
        copy.start()
    add_coupled(sz, 2.0, (meta_in, meta, sem), got, across, psel, qsel, pacc, qacc, which)
    fixed_blocks(sz, meta, which, weights, fields, (pacc, qacc), (held_out, held_grad))
    for copy in base:
        copy.wait()


def early_outputs(sz, low, meta, across, picked, got, which, weights, fields, high, token, outs):
    args = [meta, across, *picked, *(got[r] for r in which), *weights, *fields, *high, token]
    whole = [shape(out.shape, BF16) for out in outs]
    held = shape((sz.pairs, sz.chan // SUB, SUB, sz.blk), BF16)
    return call(
        functools.partial(early_kernel, sz, which, low),
        [VMEM] * len(args) + [HBM] * 2,
        [VMEM] * 4 + [HBM] * 2,
        [sz.picked, sz.picked, held, held] + whole,
        table_copy(sz) + [pltpu.SemaphoreType.DMA((2,))],
        8 * sz.pairs * sz.chan * sz.blk * sz.blk,
        4 << 20,
        8,
        {len(args): 4, len(args) + 1: 5},
    )(*args, *outs)


def fix_kernel(sz, axis, early, late, *refs):
    meta_in, across, psel, qsel = refs[:4]
    got, refs = dict(zip(late, refs[4 : 4 + len(late)])), refs[4 + len(late) :]
    weights, fields, fixed = refs[:2], refs[2:8], refs[8:10]
    mine, theirs = refs[10:12]
    out4, grad4, grad_w, pacc, qacc, held_out, held_grad, total, meta, sem, sem_out, sem_w = refs[14:]
    held, outs = (held_out, held_grad), (out4, grad4)
    odd = lax.rem(lax.axis_index(axis), 2) == 1
    top = jnp.where(odd, theirs[...], mine[...])
    low = jnp.where(odd, mine[...], theirs[...])
    zeroth, first = top[:, : sz.chan], low[:, : sz.chan]
    total[0] = zeroth
    total[1] = first
    total[2] = 2.0 * low[:, sz.chan :] - zeroth
    total[3] = 2.0 * top[:, sz.chan :] - first
    weight_copy = pltpu.make_async_copy(total, grad_w, sem_w)
    weight_copy.start()
    add_coupled(sz, 2.0, (meta_in, meta, sem), got, across, psel, qsel, pacc, qacc, late)
    copies = fixed_copies(sz, meta, early, late, fixed, outs, sem_out)
    for fresh, copy in copies:
        pl.when(fresh)(copy.start)
    fixed_blocks(sz, meta, late, weights, fields, (pacc, qacc), held)
    last = fixed_copies(sz, meta, late, [], held, outs, sem_out)
    for fresh, copy in last:
        pl.when(fresh)(copy.start)
    for fresh, copy in copies + last:
        pl.when(fresh)(copy.wait)
    weight_copy.wait()


def fix_outputs(
    sz, axis, meta, across, picked, got, early, late, weights, fields, fixed, mine, theirs, outs
):
    args = [meta, across, *picked, *(got[r] for r in late), *weights, *fields, *fixed]
    args += [mine, theirs]
    whole = [shape(out.shape, BF16) for out in outs]
    held = pltpu.VMEM((sz.pairs, sz.chan // SUB, SUB, sz.blk), BF16)
    total = (4, sz.chan, sz.chan)
    return call(
        functools.partial(fix_kernel, sz, axis, early, late),
        [VMEM] * len(args) + [HBM] * 2,
        [HBM] * 3,
        whole + [shape(total, F32)],
        [pltpu.VMEM(sz.picked.shape, F32)] * 2
        + [held, held, pltpu.VMEM(total, F32)]
        + table_copy(sz)
        + [pltpu.SemaphoreType.DMA((2, sz.pairs)), pltpu.SemaphoreType.DMA],
        8 * len(late) * sz.hb * sz.chan * sz.blk * sz.blk,
        2 << 20,
        8,
        {len(args): 0, len(args) + 1: 1},
    )(*args, *outs)


def add_kernel(gated, inputs, *refs):
    mine, theirs = refs[:2]
    outs = refs[inputs:]
    if gated:
        outs[2][...] = refs[2][...]
    outs[0][...] = mine[...] + theirs[...]
    if len(outs) > 1:
        outs[1][...] = jnp.zeros(outs[1].shape, F32)


def add(mine, theirs, pay, after, last=False):
    outs = [shape(mine.shape, F32)] + ([] if last else [TOKEN])
    args = [mine, theirs]
    if pay is not None:
        outs.append(shape(pay.shape, BF16))
        args.append(pay)
    args += after
    return call(
        functools.partial(add_kernel, pay is not None, len(args)),
        [VMEM] * len(args),
        [VMEM] * len(outs),
        outs,
        [],
        mine.size,
        12 * mine.size,
        2,
    )(*args)


def from_partner(values, bit):
    count = lax.axis_size("dom")
    route = []
    for low in range(count):
        high = low | 1 << bit
        if high != low and high < count:
            route += [(low, high), (high, low)]
    return lax.ppermute(values, "dom", route)


def local(
    features,
    cheb_weight,
    lap_tiles,
    col_index,
    cross_tiles,
    send_index,
    row_index,
    pair_on,
    blk_live,
    cotangent,
):
    sz = Sizes(features, lap_tiles, cross_tiles)
    split = (sz.chan // SUB, SUB, sz.blocks, sz.blk)
    x4 = features.reshape(split).transpose(0, 2, 1, 3)
    u4 = cotangent.reshape(split).transpose(0, 2, 1, 3)
    coupling = cross_tiles.reshape(sz.pairs, sz.blk, sz.blk)
    send, row = send_index.transpose(0, 2, 1), row_index.transpose(0, 2, 1)

    packed = pack(sz, x4, u4, coupling, send, row, pair_on, blk_live, col_index.T)
    t0, s0, cross, across, meta, col = packed[:6]
    everyone = range(sz.rounds)
    got = [from_partner(pay, bit) for bit, pay in enumerate(packed[6:])]
    *base, psel, qsel, tiles, turned, gram0 = first_products(sz, meta, col, lap_tiles, t0, s0)
    t1, s1, pays = join(sz, meta, cross, base, [across, psel, qsel, *got], True)

    got = [from_partner(pay, bit) for bit, pay in enumerate(pays)]
    fields = (t1, s1, t0, s0)
    *base, psel, qsel, gram = local_products(sz, meta, col, tiles, turned, fields)
    *picked, mine, given = correct(
        sz, "dom", meta, across, (psel, qsel), got, gram0, gram, s1
    )
    theirs = from_partner(given, 0)
    t2, s2, pays = join(sz, meta, cross, base, picked, False)

    state = {}

    middle = sz.blocks // (2 * ROWS) * ROWS

    def window_early_rows(token):
        fields = (t2, s2, t1, s1)
        state["part"] = part_products(sz, meta, col, tiles, turned, fields, None, token)
        return None

    def window_late_rows(token):
        fields = (t2, s2, t1, s1)
        t3, _, _, s3, *state["picked"] = part_products(
            sz, meta, col, tiles, turned, fields, state["part"], token
        )
        state["last"] = (t3, s3)
        return state["picked"][0]

    def window_outputs(token):
        t3, s3 = state["last"]
        *state["weights"], left, right, out4, grad4 = base_outputs(
            sz, middle, (t0, t1, t2, t3), (s0, s1, s2, s3), cheb_weight, token
        )
        state["high"], state["outs"] = [left, right], [out4, grad4]
        return state["weights"][0]

    windows = [window_early_rows, window_late_rows, window_outputs]
    bits = list(reversed(range(1, (lax.axis_size("dom") - 1).bit_length())))
    pays, got = list(pays), [None] * sz.rounds
    history = (t0, t1, t2, s0, s1, s2)
    got[0] = from_partner(pays[0], 0)
    early = [0] + [bit for bit in bits[:-1] if bit < sz.rounds]
    late = [bit for bit in everyone if bit not in early]
    mine, token, *rest = add(mine, theirs, pays[bits[0]] if bits[0] < sz.rounds else None, [])
    held = [got[0]]
    for at, bit in enumerate(bits):
        if bit < sz.rounds:
            pays[bit] = rest[0]
        theirs = from_partner(mine, bit)
        if bit < sz.rounds:
            got[bit] = from_partner(pays[bit], bit)
        if at < len(windows):
            token = windows[at](token)
        last = at + 1 == len(bits)
        if last:
            *picked, left, right, out4, grad4 = early_outputs(
                sz,
                middle,
                meta,
                across,
                state["picked"],
                got,
                early,
                state["weights"],
                history,
                state["high"],
                token,
                state["outs"],
            )
            token = picked[0]
        gated = not last and bits[at + 1] < sz.rounds
        after = ([] if token is None else [token]) + held
        held = [got[bit]] if bit < sz.rounds else []
        if last:
            (mine,) = add(mine, theirs, None, after, True)
        else:
            mine, token, *rest = add(mine, theirs, pays[bits[at + 1]] if gated else None, after)
    theirs = from_partner(mine, 0)
    out4, grad4, grad_w = fix_outputs(
        sz,
        "dom",
        meta,
        across,
        picked,
        got,
        early,
        late,
        state["weights"],
        history,
        [left, right],
        mine,
        theirs,
        [out4, grad4],
    )
    conv_out = out4.transpose(0, 2, 1, 3).reshape(features.shape)
    grad_x = grad4.transpose(0, 2, 1, 3).reshape(features.shape)
    return (conv_out, grad_x, grad_w)


def solution(mesh):
    in_specs = (
        P(None, "dom"),
        P(),
        P("dom", None, None, None),
        P("dom", None),
        P("dom", None, None, None, None),
        P("dom", None, None),
        P("dom", None, None),
        P("dom", None),
        P("dom"),
        P(None, "dom"),
    )
    out_specs = (P(None, "dom"), P(None, "dom"), P())
    return jax.shard_map(local, mesh=mesh, in_specs=in_specs, out_specs=out_specs, check_vma=False)
```

```python
import functools

import jax
import jax.numpy as jnp
from jax import lax
from jax.experimental import pallas as pl
from jax.experimental.pallas import tpu as pltpu
from jax.sharding import PartitionSpec as P


F32 = jnp.float32
BF16 = jnp.bfloat16
SUB = 8
LANES = 128
ROWS_FIRST = 8
ROWS_PART = 16
ROWS = 32

VMEM = pl.BlockSpec(memory_space=pltpu.VMEM)
SMEM = pl.BlockSpec(memory_space=pltpu.SMEM)
HBM = pl.BlockSpec(memory_space=pltpu.HBM)
TOKEN = jax.ShapeDtypeStruct((SUB, LANES), F32)


def shape(dims, dtype):
    return jax.ShapeDtypeStruct(dims, dtype)


def nn(a, b):
    return lax.dot_general(a, b, (((1,), (0,)), ((), ())), preferred_element_type=F32)


class Sizes:
    def __init__(self, features, lap_tiles, cross_tiles):
        self.chan = features.shape[0]
        self.blocks, self.nz, self.blk = lap_tiles.shape[:3]
        self.rounds, self.hb = cross_tiles.shape[1:3]
        self.pairs = self.rounds * self.hb
        self.rows = 0
        self.sends = self.pairs
        self.first_row = 2 * self.pairs
        self.first_send = 3 * self.pairs
        self.flags = 4 * self.pairs
        self.live = self.flags + self.rounds
        self.meta = self.live + 1
        self.half = self.hb * self.chan
        self.field = shape((self.blocks, self.chan, self.blk), BF16)
        self.picked = shape((self.pairs, self.chan, self.blk), F32)
        self.pay = shape((2 * self.half, self.blk), BF16)

    def couplings(self):
        return [(r, h, r * self.hb + h) for r in range(self.rounds) for h in range(self.hb)]

    def forward_part(self, h):
        return pl.ds(h * self.chan, self.chan)

    def adjoint_part(self, h):
        return pl.ds(self.half + h * self.chan, self.chan)


def call(kernel, in_specs, out_specs, out_shape, scratch, flops, moved, limit, aliases=None):
    return pl.pallas_call(
        kernel,
        in_specs=in_specs,
        out_specs=out_specs,
        out_shape=out_shape,
        scratch_shapes=scratch,
        input_output_aliases=aliases or {},
        compiler_params=pltpu.CompilerParams(vmem_limit_bytes=limit << 20),
        cost_estimate=pl.CostEstimate(flops=flops, bytes_accessed=moved, transcendentals=0),
    )


def fill_pays(sz, meta, tnew, snew, cross, pays):
    for r, h, j in sz.couplings():
        pays[r][sz.forward_part(h), :] = tnew[meta[sz.sends + j]]
        term = nn(snew[meta[sz.rows + j]], cross[j])
        factor = meta[sz.flags + r].astype(F32)
        pays[r][sz.adjoint_part(h), :] = (factor * term).astype(BF16)


def pack_kernel(sz, *refs):
    x4, u4, coupling, send, row, pair, live_s, col = refs[:8]
    xb, ub, cross, across, meta, col_out = refs[8:14]
    pays = refs[14 : 14 + sz.rounds]
    send_s, row_s, pair_s, sem_x, sem_u, sem_t, sem_i = refs[14 + sz.rounds :]
    small = [
        pltpu.make_async_copy(send, send_s, sem_i.at[0]),
        pltpu.make_async_copy(row, row_s, sem_i.at[1]),
        pltpu.make_async_copy(pair, pair_s, sem_i.at[2]),
    ]
    tiles = pltpu.make_async_copy(coupling, cross, sem_t)
    copies = []
    for t in range(sz.chan // SUB):
        part = pl.ds(t * SUB, SUB)
        copies.append(pltpu.make_async_copy(x4.at[t], xb.at[:, part, :], sem_x.at[t]))
        copies.append(pltpu.make_async_copy(u4.at[t], ub.at[:, part, :], sem_u.at[t]))
    copies.append(pltpu.make_async_copy(col, col_out, sem_i.at[3]))
    for copy in small + [tiles] + copies:
        copy.start()
    for copy in small:
        copy.wait()
    count = live_s[0]
    rows = [lax.rem(row_s[0, h, r], count) for r, h, _ in sz.couplings()]
    sends = [lax.rem(send_s[0, h, r], count) for r, h, _ in sz.couplings()]
    for values, spot, first in (
        (rows, sz.rows, sz.first_row),
        (sends, sz.sends, sz.first_send),
    ):
        for j, value in enumerate(values):
            earliest = jnp.int32(j)
            for q in reversed(range(j)):
                earliest = jnp.where(values[q] == value, q, earliest)
            meta[spot + j] = value
            meta[first + j] = earliest
    for r in range(sz.rounds):
        meta[sz.flags + r] = pair_s[0, r]
    meta[sz.live] = count
    tiles.wait()
    for j in range(sz.pairs):
        across[j] = cross[j].T
    for copy in copies:
        copy.wait()

    def clear(i, carry):
        xb[i] = jnp.zeros(xb.shape[1:], BF16)
        ub[i] = jnp.zeros(ub.shape[1:], BF16)
        return carry

    lax.fori_loop(count, sz.blocks, clear, 0)
    fill_pays(sz, meta, xb, ub, cross, pays)


def keep(array):
    return pltpu.with_memory_space_constraint(array, pltpu.HBM)


def pack(sz, *args):
    args = [array if array.size == 1 else keep(array) for array in args]
    _, _, _, send, row, pair, _, col = args
    groups = sz.chan // SUB
    cross = shape((sz.pairs, sz.blk, sz.blk), BF16)
    table = shape((sz.meta,), jnp.int32)
    return call(
        functools.partial(pack_kernel, sz),
        [HBM] * 6 + [SMEM, HBM],
        [VMEM] * 4 + [SMEM, VMEM] + [VMEM] * sz.rounds,
        [sz.field, sz.field, cross, cross, table, shape(col.shape, jnp.int32)]
        + [sz.pay] * sz.rounds,
        [
            pltpu.SMEM(send.shape, jnp.int32),
            pltpu.SMEM(row.shape, jnp.int32),
            pltpu.SMEM(pair.shape, jnp.int32),
            pltpu.SemaphoreType.DMA((groups,)),
            pltpu.SemaphoreType.DMA((groups,)),
            pltpu.SemaphoreType.DMA,
            pltpu.SemaphoreType.DMA((4,)),
        ],
        1000,
        4 << 20,
        8,
    )(*args)


def big_steps(count):
    return (count + ROWS - 1) // ROWS


def part_steps(count):
    return (count + ROWS_PART - 1) // ROWS_PART


def table_scratch(sz, col):
    return [pltpu.SMEM((sz.meta,), jnp.int32), pltpu.SMEM(col.shape, jnp.int32)]


def clear_sums(sz, summed):
    def clear(i, carry):
        summed[i] = jnp.zeros(summed.shape[1:], F32)
        return carry

    lax.fori_loop(0, sz.blocks, clear, 0, unroll=4)


def scatter_terms(sz, summed, cols, terms):
    for m in range(sz.nz):
        summed[cols[m]] = summed[cols[m]] + terms[:, m * sz.blk : (m + 1) * sz.blk]


def finish_local(sz, meta, held, adjoint, tnew, snew, psel, qsel):
    count = meta[sz.live]

    def finish(g, carry):
        for u in range(ROWS):
            i = g * ROWS + u
            snew[i] = adjoint(i).astype(BF16)
        return carry

    lax.fori_loop(0, big_steps(count), finish, 0)

    def dead(i, carry):
        tnew[i] = jnp.zeros(tnew.shape[1:], BF16)
        snew[i] = jnp.zeros(snew.shape[1:], BF16)
        return carry

    lax.fori_loop(count, sz.blocks, dead, 0)
    for j in range(sz.pairs):
        psel[j] = held[meta[sz.rows + j]]
        qsel[j] = adjoint(meta[sz.sends + j])


def first_kernel(sz, *refs):
    meta_in, col_in, tiles_hbm, t0, s0 = refs[:5]
    tnew, snew, psel, qsel, tiles, turned, gram, held, summed, meta, col, sem, sem_i = refs[5:]
    small = [
        pltpu.make_async_copy(meta_in, meta, sem_i.at[0]),
        pltpu.make_async_copy(col_in, col, sem_i.at[1]),
    ]
    for copy in small:
        copy.start()
    for copy in small:
        copy.wait()
    count = meta[sz.live]
    steps = big_steps(count)
    loads = steps * (ROWS // ROWS_FIRST)

    def fetch(g):
        part = pl.ds(g * ROWS_FIRST, ROWS_FIRST)
        return pltpu.make_async_copy(tiles_hbm.at[part], tiles.at[part], sem.at[g])

    def start(g, carry):
        fetch(g).start()
        return carry

    lax.fori_loop(0, loads, start, 0)
    clear_sums(sz, summed)

    def products(g, total):
        spots = [g * ROWS + u for u in range(ROWS)]
        left = jnp.concatenate([t0[i] for i in spots], axis=1)
        return total + nn(left, jnp.concatenate([s0[i].T for i in spots], axis=0))

    gram[...] = lax.fori_loop(0, steps, products, jnp.zeros(gram.shape, F32))

    def block_row(i):
        cols = [col[m, i] for m in range(sz.nz)]
        parts = [tiles[i, m] for m in range(sz.nz)]
        flipped = [part.T for part in parts]
        for m in range(sz.nz):
            turned[i, pl.ds(m * sz.blk, sz.blk), :] = flipped[m]
        gathered = jnp.concatenate([t0[c] for c in cols], axis=1)
        forward = nn(gathered, jnp.concatenate(flipped, axis=0))
        held[i] = forward
        tnew[i] = forward.astype(BF16)
        scatter_terms(sz, summed, cols, nn(s0[i], jnp.concatenate(parts, axis=1)))

    def step(g, carry):
        for part in range(ROWS // ROWS_FIRST):
            fetch(g * (ROWS // ROWS_FIRST) + part).wait()
        for u in range(ROWS):
            block_row(g * ROWS + u)
        return carry

    lax.fori_loop(0, steps, step, 0)
    finish_local(sz, meta, held, lambda i: summed[i], tnew, snew, psel, qsel)


def first_products(sz, meta, col, tiles, t0, s0):
    turned = shape((sz.blocks, sz.nz * sz.blk, sz.blk), BF16)
    return call(
        functools.partial(first_kernel, sz),
        [VMEM, VMEM, HBM, VMEM, VMEM],
        [VMEM] * 7,
        [sz.field, sz.field, sz.picked, sz.picked, shape(tiles.shape, BF16), turned]
        + [shape((sz.chan, sz.chan), F32)],
        [pltpu.VMEM((sz.blocks, sz.chan, sz.blk), F32)] * 2
        + table_scratch(sz, col)
        + [pltpu.SemaphoreType.DMA((sz.blocks // ROWS_FIRST,)), pltpu.SemaphoreType.DMA((2,))],
        4 * sz.blocks * sz.nz * sz.chan * sz.blk * sz.blk,
        12 << 20,
        24,
    )(meta, col, keep(tiles), t0, s0)


def row_products(sz, col, low, high, rows, arrays, tnew, held, summed):
    tiles, turned, tcur, scur, tprev = arrays

    def block_row(i):
        cols = [col[m, i] for m in range(sz.nz)]
        gathered = jnp.concatenate([tcur[c] for c in cols], axis=1)
        forward = 2.0 * nn(gathered, turned[i]) - tprev[i].astype(F32)
        held[i] = forward
        tnew[i] = forward.astype(BF16)
        wide = jnp.concatenate([tiles[i, m] for m in range(sz.nz)], axis=1)
        scatter_terms(sz, summed, cols, nn(scur[i], wide))

    def step(g, carry):
        for u in range(rows):
            block_row(g * rows + u)
        return carry

    lax.fori_loop(low, high, step, 0)


def start_table(meta_in, col_in, meta, col, sem):
    small = [
        pltpu.make_async_copy(meta_in, meta, sem.at[0]),
        pltpu.make_async_copy(col_in, col, sem.at[1]),
    ]
    for copy in small:
        copy.start()
    return small


def local_kernel(sz, *refs):
    meta_in, col_in, tiles, turned, tcur, scur, tprev, sprev = refs[:8]
    tnew, snew, psel, qsel, gram, held, summed, meta, col, sem = refs[8:]
    small = start_table(meta_in, col_in, meta, col, sem)
    clear_sums(sz, summed)
    for copy in small:
        copy.wait()
    steps = big_steps(meta[sz.live])
    arrays = (tiles, turned, tcur, scur, tprev)
    row_products(sz, col, 0, steps, ROWS, arrays, tnew, held, summed)

    def adjoint(i):
        return 2.0 * summed[i] - sprev[i].astype(F32)

    finish_local(sz, meta, held, adjoint, tnew, snew, psel, qsel)

    def products(g, total):
        left, right = [], []
        for u in range(ROWS):
            i = g * ROWS + u
            left.append(jnp.concatenate([tcur[i], tnew[i]], axis=0))
            right.append(jnp.concatenate([sprev[i], scur[i]], axis=0).T)
        return total + nn(jnp.concatenate(left, axis=1), jnp.concatenate(right, axis=0))

    gram[...] = lax.fori_loop(0, steps, products, jnp.zeros(gram.shape, F32))


def local_products(sz, meta, col, tiles, turned, fields):
    gram = shape((2 * sz.chan, 2 * sz.chan), F32)
    return call(
        functools.partial(local_kernel, sz),
        [VMEM] * 8,
        [VMEM] * 5,
        [sz.field, sz.field, sz.picked, sz.picked, gram],
        [pltpu.VMEM((sz.blocks, sz.chan, sz.blk), F32)] * 2
        + table_scratch(sz, col)
        + [pltpu.SemaphoreType.DMA((2,))],
        4 * sz.blocks * sz.nz * sz.chan * sz.blk * sz.blk,
        12 << 20,
        24,
    )(meta, col, tiles, turned, *fields)


def early_rows_kernel(sz, *refs):
    meta_in, col_in, tiles, turned, tcur, scur, tprev, _ = refs[:8]
    tnew, held, summed, meta, col, sem = refs[8:]
    small = start_table(meta_in, col_in, meta, col, sem)
    clear_sums(sz, summed)
    for copy in small:
        copy.wait()
    cut = (3 * part_steps(meta[sz.live])) // 4
    arrays = (tiles, turned, tcur, scur, tprev)
    row_products(sz, col, 0, cut, ROWS_PART, arrays, tnew, held, summed)


def late_rows_kernel(sz, *refs):
    meta_in, col_in, tiles, turned, tcur, scur, tprev, sprev = refs[:8]
    tnew, held, summed, snew, psel, qsel, meta, col, sem = refs[12:]
    for copy in start_table(meta_in, col_in, meta, col, sem):
        copy.wait()
    steps = part_steps(meta[sz.live])
    arrays = (tiles, turned, tcur, scur, tprev)
    row_products(sz, col, (3 * steps) // 4, steps, ROWS_PART, arrays, tnew, held, summed)

    def adjoint(i):
        return 2.0 * summed[i] - sprev[i].astype(F32)

    finish_local(sz, meta, held, adjoint, tnew, snew, psel, qsel)


def part_products(sz, meta, col, tiles, turned, fields, before, token):
    sums = shape((sz.blocks, sz.chan, sz.blk), F32)
    args = [meta, col, tiles, turned, *fields]
    outs, aliases = [sz.field, sums, sums], {}
    if before is None:
        args[-1] = token
    else:
        aliases = {len(args) + k: k for k in range(3)}
        args += [*before, token]
        outs += [sz.field, sz.picked, sz.picked]
    return call(
        functools.partial(early_rows_kernel if before is None else late_rows_kernel, sz),
        [VMEM] * len(args),
        [VMEM] * len(outs),
        outs,
        table_scratch(sz, col) + [pltpu.SemaphoreType.DMA((2,))],
        2 * sz.blocks * sz.nz * sz.chan * sz.blk * sz.blk,
        6 << 20,
        8,
        aliases,
    )(*args)


def add_coupled(sz, scale, table, got, across, psel, qsel, pacc, qacc, which):
    meta_in, meta, sem = table
    copy = pltpu.make_async_copy(meta_in, meta, sem)
    copy.start()
    for j in range(sz.pairs):
        pacc[j] = psel[j]
        qacc[j] = qsel[j]
    some = [(r, h, j) for r, h, j in sz.couplings() if r in which]
    terms = {j: nn(got[r][sz.forward_part(h), :], across[j]) for r, h, j in some}
    copy.wait()
    for r, h, j in some:
        terms[j] = (scale * meta[sz.flags + r].astype(F32)) * terms[j]
        spot = meta[sz.first_row + j]
        pacc[spot] = pacc[spot] + terms[j]
        spot = meta[sz.first_send + j]
        qacc[spot] = qacc[spot] + scale * got[r][sz.adjoint_part(h), :].astype(F32)
    return terms


def table_copy(sz):
    return [pltpu.SMEM((sz.meta,), jnp.int32), pltpu.SemaphoreType.DMA]


def correct_kernel(sz, axis, *refs):
    meta_in, across, psel, qsel, gram0, gram, sold = refs[:7]
    got, refs = refs[7 : 7 + sz.rounds], refs[7 + sz.rounds :]
    pacc, qacc, keep_half, give_half, whole, meta, sem = refs
    which, table = range(sz.rounds), (meta_in, meta, sem)
    terms = add_coupled(sz, 2.0, table, got, across, psel, qsel, pacc, qacc, which)
    left = jnp.concatenate([terms[j].astype(BF16) for j in range(sz.pairs)], axis=1)
    right = [sold[meta[sz.rows + j]].T for j in range(sz.pairs)]
    extra = nn(left, jnp.concatenate(right, axis=0))
    one, two = pl.ds(0, sz.chan), pl.ds(sz.chan, sz.chan)
    whole[one, one] = gram0[...]
    whole[two, one] = gram[one, one]
    whole[two, two] = gram[one, two]
    whole[one, two] = gram[two, two] + extra
    odd = lax.rem(lax.axis_index(axis), 2)
    keep_half[...] = whole[pl.ds(pl.multiple_of(odd * sz.chan, sz.chan), sz.chan), :]
    give_half[...] = whole[pl.ds(pl.multiple_of((1 - odd) * sz.chan, sz.chan), sz.chan), :]


def correct(sz, axis, meta, across, picked, got, gram0, gram, sold):
    args = [meta, across, *picked, gram0, gram, sold, *got]
    half = shape((sz.chan, 2 * sz.chan), F32)
    return call(
        functools.partial(correct_kernel, sz, axis),
        [VMEM] * len(args),
        [VMEM] * 4,
        [sz.picked, sz.picked, half, half],
        [pltpu.VMEM((2 * sz.chan, 2 * sz.chan), F32)] + table_copy(sz),
        4 * sz.pairs * sz.chan * sz.blk * sz.blk,
        3 << 20,
        8,
    )(*args)


def patch(sz, meta, cross, tnew, snew, pacc, qacc, pays):
    for j in range(sz.pairs):
        tnew[meta[sz.rows + j]] = pacc[meta[sz.first_row + j]].astype(BF16)
        snew[meta[sz.sends + j]] = qacc[meta[sz.first_send + j]].astype(BF16)
    fill_pays(sz, meta, tnew, snew, cross, pays)


def start_kernel(sz, *refs):
    meta_in, cross, _, _, across, psel, qsel = refs[:7]
    got, refs = refs[7 : 7 + sz.rounds], refs[7 + sz.rounds :]
    tnew, snew = refs[:2]
    pacc, qacc, meta, sem = refs[-4:]
    table = (meta_in, meta, sem)
    add_coupled(sz, 1.0, table, got, across, psel, qsel, pacc, qacc, range(sz.rounds))
    patch(sz, meta, cross, tnew, snew, pacc, qacc, refs[2:-4])


def join_kernel(sz, *refs):
    meta, cross, _, _, pacc, qacc, tnew, snew = refs[:8]
    patch(sz, meta, cross, tnew, snew, pacc, qacc, refs[8:])


def join(sz, meta, cross, base, rest, first):
    args = [meta, cross, *base, *rest]
    outs = [sz.field, sz.field] + [sz.pay] * sz.rounds
    outs = call(
        functools.partial(start_kernel if first else join_kernel, sz),
        [VMEM if first else SMEM] + [VMEM] * (len(args) - 1),
        [VMEM] * len(outs),
        outs,
        [pltpu.VMEM(sz.picked.shape, F32)] * 2 + table_copy(sz) if first else [],
        2 * sz.pairs * sz.chan * sz.blk * sz.blk,
        5 << 20,
        8,
        {2: 0, 3: 1},
    )(*args)
    return outs[0], outs[1], outs[2:]


def output_weights(weight):
    wide = [weight[k].astype(F32) for k in range(weight.shape[0])]
    ahead = jnp.concatenate([w.T for w in wide], axis=1).astype(BF16)
    back = jnp.concatenate(wide, axis=1).astype(BF16)
    return ahead, back


def output_block(sz, left, fields, held, spot):
    value = nn(left[...], jnp.concatenate(fields, axis=0)).astype(BF16)
    for t in range(sz.chan // SUB):
        held[(t,) + spot if len(spot) == 1 else (spot[1], t)] = value[t * SUB : (t + 1) * SUB]


def output_kernel(sz, middle, *refs):
    forward, adjoint, weight = refs[:4], refs[4:8], refs[8]
    ahead, back, high_out, high_grad, out4, grad4, low_out, low_grad, sem = refs[10:]
    wide_ahead, wide_back = output_weights(weight)
    ahead[...] = wide_ahead
    back[...] = wide_back

    def half(low, count, held_out, held_grad):
        def step(g, carry):
            for u in range(ROWS):
                n = g * ROWS + u
                output_block(sz, ahead, [f[low + n] for f in forward], held_out, (n,))
                output_block(sz, back, [f[low + n] for f in adjoint], held_grad, (n,))
            return carry

        lax.fori_loop(0, count // ROWS, step, 0)

    half(0, middle, low_out, low_grad)
    part = pl.ds(0, middle)
    copies = [
        pltpu.make_async_copy(low_out, out4.at[:, part], sem.at[0]),
        pltpu.make_async_copy(low_grad, grad4.at[:, part], sem.at[1]),
    ]
    for copy in copies:
        copy.start()
    half(middle, sz.blocks - middle, high_out, high_grad)
    for copy in copies:
        copy.wait()


def base_outputs(sz, middle, forward, adjoint, weight, token):
    groups = sz.chan // SUB
    high = shape((groups, sz.blocks - middle, SUB, sz.blk), BF16)
    whole = shape((groups, sz.blocks, SUB, sz.blk), BF16)
    wide = shape((sz.chan, weight.shape[0] * sz.chan), BF16)
    args = [*forward, *adjoint, weight, token]
    return call(
        functools.partial(output_kernel, sz, middle),
        [VMEM] * len(args),
        [VMEM] * 4 + [HBM] * 2,
        [wide, wide, high, high, whole, whole],
        [pltpu.VMEM((groups, middle, SUB, sz.blk), BF16)] * 2 + [pltpu.SemaphoreType.DMA((2,))],
        16 * sz.blocks * sz.chan * sz.chan * sz.blk,
        6 << 20,
        10,
    )(*args)


def fixed_blocks(sz, meta, which, weights, fields, last, held):
    for r, h, j in sz.couplings():
        if r in which:
            for side, spot, first in ((0, sz.rows, sz.first_row), (1, sz.sends, sz.first_send)):
                i = meta[spot + j]
                stack = [f[i] for f in fields[3 * side : 3 * side + 3]]
                stack.append(last[side][meta[first + j]].astype(BF16))
                output_block(sz, weights[side], stack, held[side], (None, j))


def fixed_copies(sz, meta, which, over, held, outs, sem):
    copies = []
    for side, spot in ((0, sz.rows), (1, sz.sends)):
        seen = [meta[spot + j] for r, h, j in sz.couplings() if r in over]
        for r, h, j in sz.couplings():
            if r in which:
                i = meta[spot + j]
                fresh = jnp.bool_(True)
                for other in seen:
                    fresh = jnp.logical_and(fresh, other != i)
                seen.append(i)
                copy = pltpu.make_async_copy(
                    held[side].at[j], outs[side].at[:, i], sem.at[side, j]
                )
                copies.append((fresh, copy))
    return copies


def early_kernel(sz, which, low, *refs):
    meta_in, across, psel, qsel = refs[:4]
    got, refs = dict(zip(which, refs[4 : 4 + len(which)])), refs[4 + len(which) :]
    weights, fields, high = refs[:2], refs[2:8], refs[8:10]
    pacc, qacc, held_out, held_grad, out4, grad4, meta, sem, sem_base = refs[13:]
    part = pl.ds(low, high[0].shape[1])
    base = [
        pltpu.make_async_copy(high[0], out4.at[:, part], sem_base.at[0]),
        pltpu.make_async_copy(high[1], grad4.at[:, part], sem_base.at[1]),
    ]
    for copy in base:
        copy.start()
    add_coupled(sz, 2.0, (meta_in, meta, sem), got, across, psel, qsel, pacc, qacc, which)
    fixed_blocks(sz, meta, which, weights, fields, (pacc, qacc), (held_out, held_grad))
    for copy in base:
        copy.wait()


def early_outputs(sz, low, meta, across, picked, got, which, weights, fields, high, token, outs):
    args = [meta, across, *picked, *(got[r] for r in which), *weights, *fields, *high, token]
    whole = [shape(out.shape, BF16) for out in outs]
    held = shape((sz.pairs, sz.chan // SUB, SUB, sz.blk), BF16)
    return call(
        functools.partial(early_kernel, sz, which, low),
        [VMEM] * len(args) + [HBM] * 2,
        [VMEM] * 4 + [HBM] * 2,
        [sz.picked, sz.picked, held, held] + whole,
        table_copy(sz) + [pltpu.SemaphoreType.DMA((2,))],
        8 * sz.pairs * sz.chan * sz.blk * sz.blk,
        4 << 20,
        8,
        {len(args): 4, len(args) + 1: 5},
    )(*args, *outs)


def fix_kernel(sz, axis, early, late, *refs):
    meta_in, across, psel, qsel = refs[:4]
    got, refs = dict(zip(late, refs[4 : 4 + len(late)])), refs[4 + len(late) :]
    weights, fields, fixed = refs[:2], refs[2:8], refs[8:10]
    mine, theirs = refs[10:12]
    out4, grad4, grad_w, pacc, qacc, held_out, held_grad, total, meta, sem, sem_out, sem_w = refs[14:]
    held, outs = (held_out, held_grad), (out4, grad4)
    odd = lax.rem(lax.axis_index(axis), 2) == 1
    top = jnp.where(odd, theirs[...], mine[...])
    low = jnp.where(odd, mine[...], theirs[...])
    zeroth, first = top[:, : sz.chan], low[:, : sz.chan]
    total[0] = zeroth
    total[1] = first
    total[2] = 2.0 * low[:, sz.chan :] - zeroth
    total[3] = 2.0 * top[:, sz.chan :] - first
    weight_copy = pltpu.make_async_copy(total, grad_w, sem_w)
    weight_copy.start()
    add_coupled(sz, 2.0, (meta_in, meta, sem), got, across, psel, qsel, pacc, qacc, late)
    copies = fixed_copies(sz, meta, early, late, fixed, outs, sem_out)
    for fresh, copy in copies:
        pl.when(fresh)(copy.start)
    fixed_blocks(sz, meta, late, weights, fields, (pacc, qacc), held)
    last = fixed_copies(sz, meta, late, [], held, outs, sem_out)
    for fresh, copy in last:
        pl.when(fresh)(copy.start)
    for fresh, copy in copies + last:
        pl.when(fresh)(copy.wait)
    weight_copy.wait()


def fix_outputs(
    sz, axis, meta, across, picked, got, early, late, weights, fields, fixed, mine, theirs, outs
):
    args = [meta, across, *picked, *(got[r] for r in late), *weights, *fields, *fixed]
    args += [mine, theirs]
    whole = [shape(out.shape, BF16) for out in outs]
    held = pltpu.VMEM((sz.pairs, sz.chan // SUB, SUB, sz.blk), BF16)
    total = (4, sz.chan, sz.chan)
    return call(
        functools.partial(fix_kernel, sz, axis, early, late),
        [VMEM] * len(args) + [HBM] * 2,
        [HBM] * 3,
        whole + [shape(total, F32)],
        [pltpu.VMEM(sz.picked.shape, F32)] * 2
        + [held, held, pltpu.VMEM(total, F32)]
        + table_copy(sz)
        + [pltpu.SemaphoreType.DMA((2, sz.pairs)), pltpu.SemaphoreType.DMA],
        8 * len(late) * sz.hb * sz.chan * sz.blk * sz.blk,
        2 << 20,
        8,
        {len(args): 0, len(args) + 1: 1},
    )(*args, *outs)


def add_kernel(gated, inputs, *refs):
    mine, theirs = refs[:2]
    outs = refs[inputs:]
    if gated:
        outs[2][...] = refs[2][...]
    outs[0][...] = mine[...] + theirs[...]
    if len(outs) > 1:
        outs[1][...] = jnp.zeros(outs[1].shape, F32)


def add(mine, theirs, pay, after, last=False):
    outs = [shape(mine.shape, F32)] + ([] if last else [TOKEN])
    args = [mine, theirs]
    if pay is not None:
        outs.append(shape(pay.shape, BF16))
        args.append(pay)
    args += after
    return call(
        functools.partial(add_kernel, pay is not None, len(args)),
        [VMEM] * len(args),
        [VMEM] * len(outs),
        outs,
        [],
        mine.size,
        12 * mine.size,
        2,
    )(*args)


def from_partner(values, bit):
    count = lax.axis_size("dom")
    route = []
    for low in range(count):
        high = low | 1 << bit
        if high != low and high < count:
            route += [(low, high), (high, low)]
    return lax.ppermute(values, "dom", route)


def local(
    features,
    cheb_weight,
    lap_tiles,
    col_index,
    cross_tiles,
    send_index,
    row_index,
    pair_on,
    blk_live,
    cotangent,
):
    sz = Sizes(features, lap_tiles, cross_tiles)
    split = (sz.chan // SUB, SUB, sz.blocks, sz.blk)
    x4 = features.reshape(split).transpose(0, 2, 1, 3)
    u4 = cotangent.reshape(split).transpose(0, 2, 1, 3)
    coupling = cross_tiles.reshape(sz.pairs, sz.blk, sz.blk)
    send, row = send_index.transpose(0, 2, 1), row_index.transpose(0, 2, 1)

    packed = pack(sz, x4, u4, coupling, send, row, pair_on, blk_live, col_index.T)
    t0, s0, cross, across, meta, col = packed[:6]
    everyone = range(sz.rounds)
    got = [from_partner(pay, bit) for bit, pay in enumerate(packed[6:])]
    *base, psel, qsel, tiles, turned, gram0 = first_products(sz, meta, col, lap_tiles, t0, s0)
    t1, s1, pays = join(sz, meta, cross, base, [across, psel, qsel, *got], True)

    got = [from_partner(pay, bit) for bit, pay in enumerate(pays)]
    fields = (t1, s1, t0, s0)
    *base, psel, qsel, gram = local_products(sz, meta, col, tiles, turned, fields)
    *picked, mine, given = correct(
        sz, "dom", meta, across, (psel, qsel), got, gram0, gram, s1
    )
    theirs = from_partner(given, 0)
    t2, s2, pays = join(sz, meta, cross, base, picked, False)

    state = {}

    middle = sz.blocks // (2 * ROWS) * ROWS

    def window_early_rows(token):
        fields = (t2, s2, t1, s1)
        state["part"] = part_products(sz, meta, col, tiles, turned, fields, None, token)
        return None

    def window_late_rows(token):
        fields = (t2, s2, t1, s1)
        t3, _, _, s3, *state["picked"] = part_products(
            sz, meta, col, tiles, turned, fields, state["part"], token
        )
        state["last"] = (t3, s3)
        return state["picked"][0]

    def window_outputs(token):
        t3, s3 = state["last"]
        *state["weights"], left, right, out4, grad4 = base_outputs(
            sz, middle, (t0, t1, t2, t3), (s0, s1, s2, s3), cheb_weight, token
        )
        state["high"], state["outs"] = [left, right], [out4, grad4]
        return state["weights"][0]

    windows = [window_early_rows, window_late_rows, window_outputs]
    bits = list(reversed(range(1, (lax.axis_size("dom") - 1).bit_length())))
    pays, got = list(pays), [None] * sz.rounds
    history = (t0, t1, t2, s0, s1, s2)
    got[0] = from_partner(pays[0], 0)
    early = [0] + [bit for bit in bits[:-1] if bit < sz.rounds]
    late = [bit for bit in everyone if bit not in early]
    mine, token, *rest = add(mine, theirs, pays[bits[0]] if bits[0] < sz.rounds else None, [])
    held = [got[0]]
    for at, bit in enumerate(bits):
        if bit < sz.rounds:
            pays[bit] = rest[0]
        theirs = from_partner(mine, bit)
        if bit < sz.rounds:
            got[bit] = from_partner(pays[bit], bit)
        if at < len(windows):
            token = windows[at](token)
        last = at + 1 == len(bits)
        gated = not last and bits[at + 1] < sz.rounds
        after = ([] if token is None else [token]) + held
        held = [got[bit]] if bit < sz.rounds else []
        if last:
            (mine,) = add(mine, theirs, None, after, True)
        else:
            mine, token, *rest = add(mine, theirs, pays[bits[at + 1]] if gated else None, after)
    theirs = from_partner(mine, 0)
    *picked, left, right, out4, grad4 = early_outputs(
        sz,
        middle,
        meta,
        across,
        state["picked"],
        got,
        early,
        state["weights"],
        history,
        state["high"],
        mine,
        state["outs"],
    )
    out4, grad4, grad_w = fix_outputs(
        sz,
        "dom",
        meta,
        across,
        picked,
        got,
        early,
        late,
        state["weights"],
        history,
        [left, right],
        mine,
        theirs,
        [out4, grad4],
    )
    conv_out = out4.transpose(0, 2, 1, 3).reshape(features.shape)
    grad_x = grad4.transpose(0, 2, 1, 3).reshape(features.shape)
    return (conv_out, grad_x, grad_w)


def solution(mesh):
    in_specs = (
        P(None, "dom"),
        P(),
        P("dom", None, None, None),
        P("dom", None),
        P("dom", None, None, None, None),
        P("dom", None, None),
        P("dom", None, None),
        P("dom", None),
        P("dom"),
        P(None, "dom"),
    )
    out_specs = (P(None, "dom"), P(None, "dom"), P())
    return jax.shard_map(local, mesh=mesh, in_specs=in_specs, out_specs=out_specs, check_vma=False)
```

```python
import functools

import jax
import jax.numpy as jnp
from jax import lax
from jax.experimental import pallas as pl
from jax.experimental.pallas import tpu as pltpu
from jax.sharding import PartitionSpec as P


F32 = jnp.float32
BF16 = jnp.bfloat16
SUB = 8
LANES = 128
ROWS_FIRST = 8
ROWS_PART = 16
ROWS = 32

VMEM = pl.BlockSpec(memory_space=pltpu.VMEM)
SMEM = pl.BlockSpec(memory_space=pltpu.SMEM)
HBM = pl.BlockSpec(memory_space=pltpu.HBM)
TOKEN = jax.ShapeDtypeStruct((SUB, LANES), F32)


def shape(dims, dtype):
    return jax.ShapeDtypeStruct(dims, dtype)


def nn(a, b):
    return lax.dot_general(a, b, (((1,), (0,)), ((), ())), preferred_element_type=F32)


class Sizes:
    def __init__(self, features, lap_tiles, cross_tiles):
        self.chan = features.shape[0]
        self.blocks, self.nz, self.blk = lap_tiles.shape[:3]
        self.rounds, self.hb = cross_tiles.shape[1:3]
        self.pairs = self.rounds * self.hb
        self.rows = 0
        self.sends = self.pairs
        self.first_row = 2 * self.pairs
        self.first_send = 3 * self.pairs
        self.flags = 4 * self.pairs
        self.live = self.flags + self.rounds
        self.meta = self.live + 1
        self.half = self.hb * self.chan
        self.field = shape((self.blocks, self.chan, self.blk), BF16)
        self.picked = shape((self.pairs, self.chan, self.blk), F32)
        self.pay = shape((2 * self.half, self.blk), BF16)

    def couplings(self):
        return [(r, h, r * self.hb + h) for r in range(self.rounds) for h in range(self.hb)]

    def forward_part(self, h):
        return pl.ds(h * self.chan, self.chan)

    def adjoint_part(self, h):
        return pl.ds(self.half + h * self.chan, self.chan)


def call(kernel, in_specs, out_specs, out_shape, scratch, flops, moved, limit, aliases=None):
    return pl.pallas_call(
        kernel,
        in_specs=in_specs,
        out_specs=out_specs,
        out_shape=out_shape,
        scratch_shapes=scratch,
        input_output_aliases=aliases or {},
        compiler_params=pltpu.CompilerParams(vmem_limit_bytes=limit << 20),
        cost_estimate=pl.CostEstimate(flops=flops, bytes_accessed=moved, transcendentals=0),
    )


def fill_pays(sz, meta, tnew, snew, cross, pays):
    for r, h, j in sz.couplings():
        pays[r][sz.forward_part(h), :] = tnew[meta[sz.sends + j]]
        term = nn(snew[meta[sz.rows + j]], cross[j])
        factor = meta[sz.flags + r].astype(F32)
        pays[r][sz.adjoint_part(h), :] = (factor * term).astype(BF16)


def pack_kernel(sz, *refs):
    x4, u4, coupling, send, row, pair, live_s, col = refs[:8]
    xb, ub, cross, across, meta, col_out = refs[8:14]
    pays = refs[14 : 14 + sz.rounds]
    send_s, row_s, pair_s, sem_x, sem_u, sem_t, sem_i = refs[14 + sz.rounds :]
    small = [
        pltpu.make_async_copy(send, send_s, sem_i.at[0]),
        pltpu.make_async_copy(row, row_s, sem_i.at[1]),
        pltpu.make_async_copy(pair, pair_s, sem_i.at[2]),
    ]
    tiles = pltpu.make_async_copy(coupling, cross, sem_t)
    copies = []
    for t in range(sz.chan // SUB):
        part = pl.ds(t * SUB, SUB)
        copies.append(pltpu.make_async_copy(x4.at[t], xb.at[:, part, :], sem_x.at[t]))
        copies.append(pltpu.make_async_copy(u4.at[t], ub.at[:, part, :], sem_u.at[t]))
    copies.append(pltpu.make_async_copy(col, col_out, sem_i.at[3]))
    for copy in small + [tiles] + copies:
        copy.start()
    for copy in small:
        copy.wait()
    count = live_s[0]
    rows = [lax.rem(row_s[0, h, r], count) for r, h, _ in sz.couplings()]
    sends = [lax.rem(send_s[0, h, r], count) for r, h, _ in sz.couplings()]
    for values, spot, first in (
        (rows, sz.rows, sz.first_row),
        (sends, sz.sends, sz.first_send),
    ):
        for j, value in enumerate(values):
            earliest = jnp.int32(j)
            for q in reversed(range(j)):
                earliest = jnp.where(values[q] == value, q, earliest)
            meta[spot + j] = value
            meta[first + j] = earliest
    for r in range(sz.rounds):
        meta[sz.flags + r] = pair_s[0, r]
    meta[sz.live] = count
    tiles.wait()
    for j in range(sz.pairs):
        across[j] = cross[j].T
    for copy in copies:
        copy.wait()

    def clear(i, carry):
        xb[i] = jnp.zeros(xb.shape[1:], BF16)
        ub[i] = jnp.zeros(ub.shape[1:], BF16)
        return carry

    lax.fori_loop(count, sz.blocks, clear, 0)
    fill_pays(sz, meta, xb, ub, cross, pays)


def keep(array):
    return pltpu.with_memory_space_constraint(array, pltpu.HBM)


def pack(sz, *args):
    args = [array if array.size == 1 else keep(array) for array in args]
    _, _, _, send, row, pair, _, col = args
    groups = sz.chan // SUB
    cross = shape((sz.pairs, sz.blk, sz.blk), BF16)
    table = pltpu.SMEM((sz.meta,), jnp.int32)
    return call(
        functools.partial(pack_kernel, sz),
        [HBM] * 6 + [SMEM, HBM],
        [VMEM] * 4 + [SMEM, SMEM] + [VMEM] * sz.rounds,
        [sz.field, sz.field, cross, cross, table, pltpu.SMEM(col.shape, jnp.int32)]
        + [sz.pay] * sz.rounds,
        [
            pltpu.SMEM(send.shape, jnp.int32),
            pltpu.SMEM(row.shape, jnp.int32),
            pltpu.SMEM(pair.shape, jnp.int32),
            pltpu.SemaphoreType.DMA((groups,)),
            pltpu.SemaphoreType.DMA((groups,)),
            pltpu.SemaphoreType.DMA,
            pltpu.SemaphoreType.DMA((4,)),
        ],
        1000,
        4 << 20,
        8,
    )(*args)


def big_steps(count):
    return (count + ROWS - 1) // ROWS


def part_steps(count):
    return (count + ROWS_PART - 1) // ROWS_PART


def clear_sums(sz, summed):
    def clear(i, carry):
        summed[i] = jnp.zeros(summed.shape[1:], F32)
        return carry

    lax.fori_loop(0, sz.blocks, clear, 0, unroll=4)


def scatter_terms(sz, summed, cols, terms):
    for m in range(sz.nz):
        summed[cols[m]] = summed[cols[m]] + terms[:, m * sz.blk : (m + 1) * sz.blk]


def finish_local(sz, meta, held, adjoint, tnew, snew, psel, qsel):
    count = meta[sz.live]

    def finish(g, carry):
        for u in range(ROWS):
            i = g * ROWS + u
            snew[i] = adjoint(i).astype(BF16)
        return carry

    lax.fori_loop(0, big_steps(count), finish, 0)

    def dead(i, carry):
        tnew[i] = jnp.zeros(tnew.shape[1:], BF16)
        snew[i] = jnp.zeros(snew.shape[1:], BF16)
        return carry

    lax.fori_loop(count, sz.blocks, dead, 0)
    for j in range(sz.pairs):
        psel[j] = held[meta[sz.rows + j]]
        qsel[j] = adjoint(meta[sz.sends + j])


def first_kernel(sz, *refs):
    meta, col, tiles_hbm, t0, s0 = refs[:5]
    tnew, snew, psel, qsel, tiles, turned, gram, held, summed, sem = refs[5:]
    count = meta[sz.live]
    steps = big_steps(count)
    loads = steps * (ROWS // ROWS_FIRST)

    def fetch(g):
        part = pl.ds(g * ROWS_FIRST, ROWS_FIRST)
        return pltpu.make_async_copy(tiles_hbm.at[part], tiles.at[part], sem.at[g])

    def start(g, carry):
        fetch(g).start()
        return carry

    lax.fori_loop(0, loads, start, 0)
    clear_sums(sz, summed)

    def products(g, total):
        spots = [g * ROWS + u for u in range(ROWS)]
        left = jnp.concatenate([t0[i] for i in spots], axis=1)
        return total + nn(left, jnp.concatenate([s0[i].T for i in spots], axis=0))

    gram[...] = lax.fori_loop(0, steps, products, jnp.zeros(gram.shape, F32))

    def block_row(i):
        cols = [col[m, i] for m in range(sz.nz)]
        parts = [tiles[i, m] for m in range(sz.nz)]
        flipped = [part.T for part in parts]
        for m in range(sz.nz):
            turned[i, pl.ds(m * sz.blk, sz.blk), :] = flipped[m]
        gathered = jnp.concatenate([t0[c] for c in cols], axis=1)
        forward = nn(gathered, jnp.concatenate(flipped, axis=0))
        held[i] = forward
        tnew[i] = forward.astype(BF16)
        scatter_terms(sz, summed, cols, nn(s0[i], jnp.concatenate(parts, axis=1)))

    def stepper(rows):
        def step(g, carry):
            for part in range(rows // ROWS_FIRST):
                fetch(g * (rows // ROWS_FIRST) + part).wait()
            for u in range(rows):
                block_row(g * rows + u)
            return carry

        return step

    short = ROWS // ROWS_PART
    lax.fori_loop(0, short, stepper(ROWS_PART), 0)
    lax.fori_loop(1, steps, stepper(ROWS), 0)
    finish_local(sz, meta, held, lambda i: summed[i], tnew, snew, psel, qsel)


def first_products(sz, meta, col, tiles, t0, s0):
    turned = shape((sz.blocks, sz.nz * sz.blk, sz.blk), BF16)
    return call(
        functools.partial(first_kernel, sz),
        [SMEM, SMEM, HBM, VMEM, VMEM],
        [VMEM] * 7,
        [sz.field, sz.field, sz.picked, sz.picked, shape(tiles.shape, BF16), turned]
        + [shape((sz.chan, sz.chan), F32)],
        [pltpu.VMEM((sz.blocks, sz.chan, sz.blk), F32)] * 2
        + [pltpu.SemaphoreType.DMA((sz.blocks // ROWS_FIRST,))],
        4 * sz.blocks * sz.nz * sz.chan * sz.blk * sz.blk,
        12 << 20,
        24,
    )(meta, col, keep(tiles), t0, s0)


def row_products(sz, col, low, high, rows, arrays, tnew, held, summed):
    tiles, turned, tcur, scur, tprev = arrays

    def block_row(i):
        cols = [col[m, i] for m in range(sz.nz)]
        gathered = jnp.concatenate([tcur[c] for c in cols], axis=1)
        forward = 2.0 * nn(gathered, turned[i]) - tprev[i].astype(F32)
        held[i] = forward
        tnew[i] = forward.astype(BF16)
        wide = jnp.concatenate([tiles[i, m] for m in range(sz.nz)], axis=1)
        scatter_terms(sz, summed, cols, nn(scur[i], wide))

    def step(g, carry):
        for u in range(rows):
            block_row(g * rows + u)
        return carry

    lax.fori_loop(low, high, step, 0)


def local_kernel(sz, *refs):
    meta, col, tiles, turned, tcur, scur, tprev, sprev = refs[:8]
    tnew, snew, psel, qsel, gram, held, summed = refs[8:]
    clear_sums(sz, summed)
    steps = big_steps(meta[sz.live])
    arrays = (tiles, turned, tcur, scur, tprev)
    row_products(sz, col, 0, steps, ROWS, arrays, tnew, held, summed)

    def adjoint(i):
        return 2.0 * summed[i] - sprev[i].astype(F32)

    finish_local(sz, meta, held, adjoint, tnew, snew, psel, qsel)

    def products(g, total):
        left, right = [], []
        for u in range(ROWS):
            i = g * ROWS + u
            left.append(jnp.concatenate([tcur[i], tnew[i]], axis=0))
            right.append(jnp.concatenate([sprev[i], scur[i]], axis=0).T)
        return total + nn(jnp.concatenate(left, axis=1), jnp.concatenate(right, axis=0))

    gram[...] = lax.fori_loop(0, steps, products, jnp.zeros(gram.shape, F32))


def local_products(sz, meta, col, tiles, turned, fields):
    gram = shape((2 * sz.chan, 2 * sz.chan), F32)
    return call(
        functools.partial(local_kernel, sz),
        [SMEM] * 2 + [VMEM] * 6,
        [VMEM] * 5,
        [sz.field, sz.field, sz.picked, sz.picked, gram],
        [pltpu.VMEM((sz.blocks, sz.chan, sz.blk), F32)] * 2,
        4 * sz.blocks * sz.nz * sz.chan * sz.blk * sz.blk,
        12 << 20,
        24,
    )(meta, col, tiles, turned, *fields)


def early_rows_kernel(sz, *refs):
    meta, col, tiles, turned, tcur, scur, tprev, _ = refs[:8]
    tnew, held, summed = refs[8:]
    clear_sums(sz, summed)
    cut = (3 * part_steps(meta[sz.live])) // 4
    arrays = (tiles, turned, tcur, scur, tprev)
    row_products(sz, col, 0, cut, ROWS_PART, arrays, tnew, held, summed)


def late_rows_kernel(sz, *refs):
    meta, col, tiles, turned, tcur, scur, tprev, sprev = refs[:8]
    tnew, held, summed, snew, psel, qsel = refs[12:]
    steps = part_steps(meta[sz.live])
    arrays = (tiles, turned, tcur, scur, tprev)
    row_products(sz, col, (3 * steps) // 4, steps, ROWS_PART, arrays, tnew, held, summed)

    def adjoint(i):
        return 2.0 * summed[i] - sprev[i].astype(F32)

    finish_local(sz, meta, held, adjoint, tnew, snew, psel, qsel)


def part_products(sz, meta, col, tiles, turned, fields, before, token):
    sums = shape((sz.blocks, sz.chan, sz.blk), F32)
    args = [meta, col, tiles, turned, *fields]
    outs, aliases = [sz.field, sums, sums], {}
    if before is None:
        args[-1] = token
    else:
        aliases = {len(args) + k: k for k in range(3)}
        args += [*before, token]
        outs += [sz.field, sz.picked, sz.picked]
    return call(
        functools.partial(early_rows_kernel if before is None else late_rows_kernel, sz),
        [SMEM] * 2 + [VMEM] * (len(args) - 2),
        [VMEM] * len(outs),
        outs,
        [],
        2 * sz.blocks * sz.nz * sz.chan * sz.blk * sz.blk,
        6 << 20,
        8,
        aliases,
    )(*args)


def add_coupled(sz, scale, meta, got, across, psel, qsel, pacc, qacc, which):
    for j in range(sz.pairs):
        pacc[j] = psel[j]
        qacc[j] = qsel[j]
    some = [(r, h, j) for r, h, j in sz.couplings() if r in which]
    terms = {j: nn(got[r][sz.forward_part(h), :], across[j]) for r, h, j in some}
    for r, h, j in some:
        terms[j] = (scale * meta[sz.flags + r].astype(F32)) * terms[j]
        spot = meta[sz.first_row + j]
        pacc[spot] = pacc[spot] + terms[j]
        spot = meta[sz.first_send + j]
        qacc[spot] = qacc[spot] + scale * got[r][sz.adjoint_part(h), :].astype(F32)
    return terms


def correct_kernel(sz, axis, *refs):
    meta, across, psel, qsel, gram0, gram, sold = refs[:7]
    got, refs = refs[7 : 7 + sz.rounds], refs[7 + sz.rounds :]
    pacc, qacc, keep_half, give_half, whole = refs
    which = range(sz.rounds)
    terms = add_coupled(sz, 2.0, meta, got, across, psel, qsel, pacc, qacc, which)
    left = jnp.concatenate([terms[j].astype(BF16) for j in range(sz.pairs)], axis=1)
    right = [sold[meta[sz.rows + j]].T for j in range(sz.pairs)]
    extra = nn(left, jnp.concatenate(right, axis=0))
    one, two = pl.ds(0, sz.chan), pl.ds(sz.chan, sz.chan)
    whole[one, one] = gram0[...]
    whole[two, one] = gram[one, one]
    whole[two, two] = gram[one, two]
    whole[one, two] = gram[two, two] + extra
    odd = lax.rem(lax.axis_index(axis), 2)
    keep_half[...] = whole[pl.ds(pl.multiple_of(odd * sz.chan, sz.chan), sz.chan), :]
    give_half[...] = whole[pl.ds(pl.multiple_of((1 - odd) * sz.chan, sz.chan), sz.chan), :]


def correct(sz, axis, meta, across, picked, got, gram0, gram, sold):
    args = [meta, across, *picked, gram0, gram, sold, *got]
    half = shape((sz.chan, 2 * sz.chan), F32)
    return call(
        functools.partial(correct_kernel, sz, axis),
        [SMEM] + [VMEM] * (len(args) - 1),
        [VMEM] * 4,
        [sz.picked, sz.picked, half, half],
        [pltpu.VMEM((2 * sz.chan, 2 * sz.chan), F32)],
        4 * sz.pairs * sz.chan * sz.blk * sz.blk,
        3 << 20,
        8,
    )(*args)


def patch(sz, meta, cross, tnew, snew, pacc, qacc, pays):
    for j in range(sz.pairs):
        tnew[meta[sz.rows + j]] = pacc[meta[sz.first_row + j]].astype(BF16)
        snew[meta[sz.sends + j]] = qacc[meta[sz.first_send + j]].astype(BF16)
    fill_pays(sz, meta, tnew, snew, cross, pays)


def start_kernel(sz, *refs):
    meta, cross, _, _, across, psel, qsel = refs[:7]
    got, refs = refs[7 : 7 + sz.rounds], refs[7 + sz.rounds :]
    tnew, snew = refs[:2]
    pacc, qacc = refs[-2:]
    add_coupled(sz, 1.0, meta, got, across, psel, qsel, pacc, qacc, range(sz.rounds))
    patch(sz, meta, cross, tnew, snew, pacc, qacc, refs[2:-2])


def join_kernel(sz, *refs):
    meta, cross, _, _, pacc, qacc, tnew, snew = refs[:8]
    patch(sz, meta, cross, tnew, snew, pacc, qacc, refs[8:])


def join(sz, meta, cross, base, rest, first):
    args = [meta, cross, *base, *rest]
    outs = [sz.field, sz.field] + [sz.pay] * sz.rounds
    outs = call(
        functools.partial(start_kernel if first else join_kernel, sz),
        [SMEM] + [VMEM] * (len(args) - 1),
        [VMEM] * len(outs),
        outs,
        [pltpu.VMEM(sz.picked.shape, F32)] * 2 if first else [],
        2 * sz.pairs * sz.chan * sz.blk * sz.blk,
        5 << 20,
        8,
        {2: 0, 3: 1},
    )(*args)
    return outs[0], outs[1], outs[2:]


def output_weights(weight):
    wide = [weight[k].astype(F32) for k in range(weight.shape[0])]
    ahead = jnp.concatenate([w.T for w in wide], axis=1).astype(BF16)
    back = jnp.concatenate(wide, axis=1).astype(BF16)
    return ahead, back


def output_block(sz, left, fields, held, spot):
    value = nn(left[...], jnp.concatenate(fields, axis=0)).astype(BF16)
    for t in range(sz.chan // SUB):
        held[(t,) + spot if len(spot) == 1 else (spot[1], t)] = value[t * SUB : (t + 1) * SUB]


def output_kernel(sz, middle, *refs):
    forward, adjoint, weight = refs[:4], refs[4:8], refs[8]
    ahead, back, high_out, high_grad, out4, grad4, low_out, low_grad, sem = refs[10:]
    wide_ahead, wide_back = output_weights(weight)
    ahead[...] = wide_ahead
    back[...] = wide_back

    def half(low, count, held_out, held_grad):
        def step(g, carry):
            for u in range(ROWS):
                n = g * ROWS + u
                output_block(sz, ahead, [f[low + n] for f in forward], held_out, (n,))
                output_block(sz, back, [f[low + n] for f in adjoint], held_grad, (n,))
            return carry

        lax.fori_loop(0, count // ROWS, step, 0)

    half(0, middle, low_out, low_grad)
    part = pl.ds(0, middle)
    copies = [
        pltpu.make_async_copy(low_out, out4.at[:, part], sem.at[0]),
        pltpu.make_async_copy(low_grad, grad4.at[:, part], sem.at[1]),
    ]
    for copy in copies:
        copy.start()
    half(middle, sz.blocks - middle, high_out, high_grad)
    for copy in copies:
        copy.wait()


def base_outputs(sz, middle, forward, adjoint, weight, token):
    groups = sz.chan // SUB
    high = shape((groups, sz.blocks - middle, SUB, sz.blk), BF16)
    whole = shape((groups, sz.blocks, SUB, sz.blk), BF16)
    wide = shape((sz.chan, weight.shape[0] * sz.chan), BF16)
    args = [*forward, *adjoint, weight, token]
    return call(
        functools.partial(output_kernel, sz, middle),
        [VMEM] * len(args),
        [VMEM] * 4 + [HBM] * 2,
        [wide, wide, high, high, whole, whole],
        [pltpu.VMEM((groups, middle, SUB, sz.blk), BF16)] * 2 + [pltpu.SemaphoreType.DMA((2,))],
        16 * sz.blocks * sz.chan * sz.chan * sz.blk,
        6 << 20,
        10,
    )(*args)


def fixed_blocks(sz, meta, which, weights, fields, last, held):
    for r, h, j in sz.couplings():
        if r in which:
            for side, spot, first in ((0, sz.rows, sz.first_row), (1, sz.sends, sz.first_send)):
                i = meta[spot + j]
                stack = [f[i] for f in fields[3 * side : 3 * side + 3]]
                stack.append(last[side][meta[first + j]].astype(BF16))
                output_block(sz, weights[side], stack, held[side], (None, j))


def fixed_copies(sz, meta, which, over, held, outs, sem):
    copies = []
    for side, spot in ((0, sz.rows), (1, sz.sends)):
        seen = [meta[spot + j] for r, h, j in sz.couplings() if r in over]
        for r, h, j in sz.couplings():
            if r in which:
                i = meta[spot + j]
                fresh = jnp.bool_(True)
                for other in seen:
                    fresh = jnp.logical_and(fresh, other != i)
                seen.append(i)
                copy = pltpu.make_async_copy(
                    held[side].at[j], outs[side].at[:, i], sem.at[side, j]
                )
                copies.append((fresh, copy))
    return copies


def early_kernel(sz, which, low, *refs):
    meta, across, psel, qsel = refs[:4]
    got, refs = dict(zip(which, refs[4 : 4 + len(which)])), refs[4 + len(which) :]
    weights, fields, high = refs[:2], refs[2:8], refs[8:10]
    pacc, qacc, held_out, held_grad, out4, grad4, sem_base = refs[13:]
    part = pl.ds(low, high[0].shape[1])
    base = [
        pltpu.make_async_copy(high[0], out4.at[:, part], sem_base.at[0]),
        pltpu.make_async_copy(high[1], grad4.at[:, part], sem_base.at[1]),
    ]
    for copy in base:
        copy.start()
    add_coupled(sz, 2.0, meta, got, across, psel, qsel, pacc, qacc, which)
    fixed_blocks(sz, meta, which, weights, fields, (pacc, qacc), (held_out, held_grad))
    for copy in base:
        copy.wait()


def early_outputs(sz, low, meta, across, picked, got, which, weights, fields, high, token, outs):
    args = [meta, across, *picked, *(got[r] for r in which), *weights, *fields, *high, token]
    whole = [shape(out.shape, BF16) for out in outs]
    held = shape((sz.pairs, sz.chan // SUB, SUB, sz.blk), BF16)
    return call(
        functools.partial(early_kernel, sz, which, low),
        [SMEM] + [VMEM] * (len(args) - 1) + [HBM] * 2,
        [VMEM] * 4 + [HBM] * 2,
        [sz.picked, sz.picked, held, held] + whole,
        [pltpu.SemaphoreType.DMA((2,))],
        8 * sz.pairs * sz.chan * sz.blk * sz.blk,
        4 << 20,
        8,
        {len(args): 4, len(args) + 1: 5},
    )(*args, *outs)


def fix_kernel(sz, axis, early, late, *refs):
    meta, across, psel, qsel = refs[:4]
    got, refs = dict(zip(late, refs[4 : 4 + len(late)])), refs[4 + len(late) :]
    weights, fields, fixed = refs[:2], refs[2:8], refs[8:10]
    mine, theirs = refs[10:12]
    out4, grad4, grad_w, pacc, qacc, held_out, held_grad, total, sem_out, sem_w = refs[14:]
    held, outs = (held_out, held_grad), (out4, grad4)
    odd = lax.rem(lax.axis_index(axis), 2) == 1
    top = jnp.where(odd, theirs[...], mine[...])
    low = jnp.where(odd, mine[...], theirs[...])
    zeroth, first = top[:, : sz.chan], low[:, : sz.chan]
    total[0] = zeroth
    total[1] = first
    total[2] = 2.0 * low[:, sz.chan :] - zeroth
    total[3] = 2.0 * top[:, sz.chan :] - first
    weight_copy = pltpu.make_async_copy(total, grad_w, sem_w)
    weight_copy.start()
    add_coupled(sz, 2.0, meta, got, across, psel, qsel, pacc, qacc, late)
    copies = fixed_copies(sz, meta, early, late, fixed, outs, sem_out)
    for fresh, copy in copies:
        pl.when(fresh)(copy.start)
    fixed_blocks(sz, meta, late, weights, fields, (pacc, qacc), held)
    last = fixed_copies(sz, meta, late, [], held, outs, sem_out)
    for fresh, copy in last:
        pl.when(fresh)(copy.start)
    for fresh, copy in copies + last:
        pl.when(fresh)(copy.wait)
    weight_copy.wait()


def fix_outputs(
    sz, axis, meta, across, picked, got, early, late, weights, fields, fixed, mine, theirs, outs
):
    args = [meta, across, *picked, *(got[r] for r in late), *weights, *fields, *fixed]
    args += [mine, theirs]
    whole = [shape(out.shape, BF16) for out in outs]
    held = pltpu.VMEM((sz.pairs, sz.chan // SUB, SUB, sz.blk), BF16)
    total = (4, sz.chan, sz.chan)
    return call(
        functools.partial(fix_kernel, sz, axis, early, late),
        [SMEM] + [VMEM] * (len(args) - 1) + [HBM] * 2,
        [HBM] * 3,
        whole + [shape(total, F32)],
        [pltpu.VMEM(sz.picked.shape, F32)] * 2
        + [held, held, pltpu.VMEM(total, F32)]
        + [pltpu.SemaphoreType.DMA((2, sz.pairs)), pltpu.SemaphoreType.DMA],
        8 * len(late) * sz.hb * sz.chan * sz.blk * sz.blk,
        2 << 20,
        8,
        {len(args): 0, len(args) + 1: 1},
    )(*args, *outs)


def add_kernel(gated, inputs, *refs):
    mine, theirs = refs[:2]
    outs = refs[inputs:]
    if gated:
        outs[2][...] = refs[2][...]
    outs[0][...] = mine[...] + theirs[...]
    if len(outs) > 1:
        outs[1][...] = jnp.zeros(outs[1].shape, F32)


def add(mine, theirs, pay, after, last=False):
    outs = [shape(mine.shape, F32)] + ([] if last else [TOKEN])
    args = [mine, theirs]
    if pay is not None:
        outs.append(shape(pay.shape, BF16))
        args.append(pay)
    args += after
    return call(
        functools.partial(add_kernel, pay is not None, len(args)),
        [VMEM] * len(args),
        [VMEM] * len(outs),
        outs,
        [],
        mine.size,
        12 * mine.size,
        2,
    )(*args)


def from_partner(values, bit):
    count = lax.axis_size("dom")
    route = []
    for low in range(count):
        high = low | 1 << bit
        if high != low and high < count:
            route += [(low, high), (high, low)]
    return lax.ppermute(values, "dom", route)


def local(
    features,
    cheb_weight,
    lap_tiles,
    col_index,
    cross_tiles,
    send_index,
    row_index,
    pair_on,
    blk_live,
    cotangent,
):
    sz = Sizes(features, lap_tiles, cross_tiles)
    split = (sz.chan // SUB, SUB, sz.blocks, sz.blk)
    x4 = features.reshape(split).transpose(0, 2, 1, 3)
    u4 = cotangent.reshape(split).transpose(0, 2, 1, 3)
    coupling = cross_tiles.reshape(sz.pairs, sz.blk, sz.blk)
    send, row = send_index.transpose(0, 2, 1), row_index.transpose(0, 2, 1)

    packed = pack(sz, x4, u4, coupling, send, row, pair_on, blk_live, col_index.T)
    t0, s0, cross, across, meta, col = packed[:6]
    everyone = range(sz.rounds)
    got = [from_partner(pay, bit) for bit, pay in enumerate(packed[6:])]
    *base, psel, qsel, tiles, turned, gram0 = first_products(sz, meta, col, lap_tiles, t0, s0)
    t1, s1, pays = join(sz, meta, cross, base, [across, psel, qsel, *got], True)

    got = [from_partner(pay, bit) for bit, pay in enumerate(pays)]
    fields = (t1, s1, t0, s0)
    *base, psel, qsel, gram = local_products(sz, meta, col, tiles, turned, fields)
    *picked, mine, given = correct(
        sz, "dom", meta, across, (psel, qsel), got, gram0, gram, s1
    )
    theirs = from_partner(given, 0)
    t2, s2, pays = join(sz, meta, cross, base, picked, False)

    state = {}

    middle = sz.blocks // (2 * ROWS) * ROWS

    def window_early_rows(token):
        fields = (t2, s2, t1, s1)
        state["part"] = part_products(sz, meta, col, tiles, turned, fields, None, token)
        return None

    def window_late_rows(token):
        fields = (t2, s2, t1, s1)
        t3, _, _, s3, *state["picked"] = part_products(
            sz, meta, col, tiles, turned, fields, state["part"], token
        )
        state["last"] = (t3, s3)
        return state["picked"][0]

    def window_outputs(token):
        t3, s3 = state["last"]
        *state["weights"], left, right, out4, grad4 = base_outputs(
            sz, middle, (t0, t1, t2, t3), (s0, s1, s2, s3), cheb_weight, token
        )
        state["high"], state["outs"] = [left, right], [out4, grad4]
        return state["weights"][0]

    windows = [window_early_rows, window_late_rows, window_outputs]
    bits = list(reversed(range(1, (lax.axis_size("dom") - 1).bit_length())))
    pays, got = list(pays), [None] * sz.rounds
    history = (t0, t1, t2, s0, s1, s2)
    got[0] = from_partner(pays[0], 0)
    early = [0] + [bit for bit in bits[:-1] if bit < sz.rounds]
    late = [bit for bit in everyone if bit not in early]
    mine, token, *rest = add(mine, theirs, pays[bits[0]] if bits[0] < sz.rounds else None, [])
    held = [got[0]]
    for at, bit in enumerate(bits):
        if bit < sz.rounds:
            pays[bit] = rest[0]
        theirs = from_partner(mine, bit)
        if bit < sz.rounds:
            got[bit] = from_partner(pays[bit], bit)
        if at < len(windows):
            token = windows[at](token)
        last = at + 1 == len(bits)
        gated = not last and bits[at + 1] < sz.rounds
        after = ([] if token is None else [token]) + held
        held = [got[bit]] if bit < sz.rounds else []
        if last:
            (mine,) = add(mine, theirs, None, after, True)
        else:
            mine, token, *rest = add(mine, theirs, pays[bits[at + 1]] if gated else None, after)
    theirs = from_partner(mine, 0)
    *picked, left, right, out4, grad4 = early_outputs(
        sz,
        middle,
        meta,
        across,
        state["picked"],
        got,
        early,
        state["weights"],
        history,
        state["high"],
        mine,
        state["outs"],
    )
    out4, grad4, grad_w = fix_outputs(
        sz,
        "dom",
        meta,
        across,
        picked,
        got,
        early,
        late,
        state["weights"],
        history,
        [left, right],
        mine,
        theirs,
        [out4, grad4],
    )
    conv_out = out4.transpose(0, 2, 1, 3).reshape(features.shape)
    grad_x = grad4.transpose(0, 2, 1, 3).reshape(features.shape)
    return (conv_out, grad_x, grad_w)


def solution(mesh):
    in_specs = (
        P(None, "dom"),
        P(),
        P("dom", None, None, None),
        P("dom", None),
        P("dom", None, None, None, None),
        P("dom", None, None),
        P("dom", None, None),
        P("dom", None),
        P("dom"),
        P(None, "dom"),
    )
    out_specs = (P(None, "dom"), P(None, "dom"), P())
    return jax.shard_map(local, mesh=mesh, in_specs=in_specs, out_specs=out_specs, check_vma=False)
```

```python
import functools

import jax
import jax.numpy as jnp
from jax import lax
from jax.experimental import pallas as pl
from jax.experimental.pallas import tpu as pltpu
from jax.sharding import PartitionSpec as P


F32 = jnp.float32
BF16 = jnp.bfloat16
SUB = 8
LANES = 128
ROWS_FIRST = 8
ROWS_PART = 16
ROWS = 32

VMEM = pl.BlockSpec(memory_space=pltpu.VMEM)
SMEM = pl.BlockSpec(memory_space=pltpu.SMEM)
HBM = pl.BlockSpec(memory_space=pltpu.HBM)
TOKEN = jax.ShapeDtypeStruct((SUB, LANES), F32)


def shape(dims, dtype):
    return jax.ShapeDtypeStruct(dims, dtype)


def nn(a, b):
    return lax.dot_general(a, b, (((1,), (0,)), ((), ())), preferred_element_type=F32)


class Sizes:
    def __init__(self, features, lap_tiles, cross_tiles):
        self.chan = features.shape[0]
        self.blocks, self.nz, self.blk = lap_tiles.shape[:3]
        self.rounds, self.hb = cross_tiles.shape[1:3]
        self.pairs = self.rounds * self.hb
        self.rows = 0
        self.sends = self.pairs
        self.first_row = 2 * self.pairs
        self.first_send = 3 * self.pairs
        self.flags = 4 * self.pairs
        self.live = self.flags + self.rounds
        self.meta = self.live + 1
        self.half = self.hb * self.chan
        self.field = shape((self.blocks, self.chan, self.blk), BF16)
        self.picked = shape((self.pairs, self.chan, self.blk), F32)
        self.pay = shape((2 * self.half, self.blk), BF16)

    def couplings(self):
        return [(r, h, r * self.hb + h) for r in range(self.rounds) for h in range(self.hb)]

    def forward_part(self, h):
        return pl.ds(h * self.chan, self.chan)

    def adjoint_part(self, h):
        return pl.ds(self.half + h * self.chan, self.chan)


def call(kernel, in_specs, out_specs, out_shape, scratch, flops, moved, limit, aliases=None):
    return pl.pallas_call(
        kernel,
        in_specs=in_specs,
        out_specs=out_specs,
        out_shape=out_shape,
        scratch_shapes=scratch,
        input_output_aliases=aliases or {},
        compiler_params=pltpu.CompilerParams(vmem_limit_bytes=limit << 20),
        cost_estimate=pl.CostEstimate(flops=flops, bytes_accessed=moved, transcendentals=0),
    )


def fill_pays(sz, meta, tnew, snew, cross, pays):
    for r, h, j in sz.couplings():
        pays[r][sz.forward_part(h), :] = tnew[meta[sz.sends + j]]
        term = nn(snew[meta[sz.rows + j]], cross[j])
        factor = meta[sz.flags + r].astype(F32)
        pays[r][sz.adjoint_part(h), :] = (factor * term).astype(BF16)


def pack_kernel(sz, *refs):
    x4, u4, coupling, send, row, pair, live_s, col = refs[:8]
    xb, ub, cross, across, meta, col_out = refs[8:14]
    pays = refs[14 : 14 + sz.rounds]
    send_s, row_s, pair_s, sem_x, sem_u, sem_t, sem_i = refs[14 + sz.rounds :]
    small = [
        pltpu.make_async_copy(send, send_s, sem_i.at[0]),
        pltpu.make_async_copy(row, row_s, sem_i.at[1]),
        pltpu.make_async_copy(pair, pair_s, sem_i.at[2]),
    ]
    tiles = pltpu.make_async_copy(coupling, cross, sem_t)
    copies = []
    for t in range(sz.chan // SUB):
        part = pl.ds(t * SUB, SUB)
        copies.append(pltpu.make_async_copy(x4.at[t], xb.at[:, part, :], sem_x.at[t]))
        copies.append(pltpu.make_async_copy(u4.at[t], ub.at[:, part, :], sem_u.at[t]))
    copies.append(pltpu.make_async_copy(col, col_out, sem_i.at[3]))
    for copy in small + [tiles] + copies:
        copy.start()
    for copy in small:
        copy.wait()
    count = live_s[0]
    rows = [lax.rem(row_s[0, h, r], count) for r, h, _ in sz.couplings()]
    sends = [lax.rem(send_s[0, h, r], count) for r, h, _ in sz.couplings()]
    for values, spot, first in (
        (rows, sz.rows, sz.first_row),
        (sends, sz.sends, sz.first_send),
    ):
        for j, value in enumerate(values):
            earliest = jnp.int32(j)
            for q in reversed(range(j)):
                earliest = jnp.where(values[q] == value, q, earliest)
            meta[spot + j] = value
            meta[first + j] = earliest
    for r in range(sz.rounds):
        meta[sz.flags + r] = pair_s[0, r]
    meta[sz.live] = count
    tiles.wait()
    for j in range(sz.pairs):
        across[j] = cross[j].T
    for copy in copies:
        copy.wait()

    def clear(i, carry):
        xb[i] = jnp.zeros(xb.shape[1:], BF16)
        ub[i] = jnp.zeros(ub.shape[1:], BF16)
        return carry

    lax.fori_loop(count, sz.blocks, clear, 0)
    fill_pays(sz, meta, xb, ub, cross, pays)


def keep(array):
    return pltpu.with_memory_space_constraint(array, pltpu.HBM)


def pack(sz, *args):
    args = [array if array.size == 1 else keep(array) for array in args]
    _, _, _, send, row, pair, _, col = args
    groups = sz.chan // SUB
    cross = shape((sz.pairs, sz.blk, sz.blk), BF16)
    table = pltpu.SMEM((sz.meta,), jnp.int32)
    return call(
        functools.partial(pack_kernel, sz),
        [HBM] * 6 + [SMEM, HBM],
        [VMEM] * 4 + [SMEM, SMEM] + [VMEM] * sz.rounds,
        [sz.field, sz.field, cross, cross, table, pltpu.SMEM(col.shape, jnp.int32)]
        + [sz.pay] * sz.rounds,
        [
            pltpu.SMEM(send.shape, jnp.int32),
            pltpu.SMEM(row.shape, jnp.int32),
            pltpu.SMEM(pair.shape, jnp.int32),
            pltpu.SemaphoreType.DMA((groups,)),
            pltpu.SemaphoreType.DMA((groups,)),
            pltpu.SemaphoreType.DMA,
            pltpu.SemaphoreType.DMA((4,)),
        ],
        1000,
        4 << 20,
        8,
    )(*args)


def big_steps(count):
    return (count + ROWS - 1) // ROWS


def part_steps(count):
    return (count + ROWS_PART - 1) // ROWS_PART


def clear_sums(sz, summed):
    def clear(i, carry):
        summed[i] = jnp.zeros(summed.shape[1:], F32)
        return carry

    lax.fori_loop(0, sz.blocks, clear, 0, unroll=4)


def scatter_terms(sz, summed, cols, terms):
    for m in range(sz.nz):
        summed[cols[m]] = summed[cols[m]] + terms[:, m * sz.blk : (m + 1) * sz.blk]


def finish_local(sz, meta, held, adjoint, tnew, snew, psel, qsel):
    count = meta[sz.live]

    def finish(g, carry):
        for u in range(ROWS):
            i = g * ROWS + u
            snew[i] = adjoint(i).astype(BF16)
        return carry

    lax.fori_loop(0, big_steps(count), finish, 0)

    def dead(i, carry):
        tnew[i] = jnp.zeros(tnew.shape[1:], BF16)
        snew[i] = jnp.zeros(snew.shape[1:], BF16)
        return carry

    lax.fori_loop(count, sz.blocks, dead, 0)
    for j in range(sz.pairs):
        psel[j] = held[meta[sz.rows + j]]
        qsel[j] = adjoint(meta[sz.sends + j])


def first_kernel(sz, *refs):
    meta, col, tiles_hbm, t0, s0 = refs[:5]
    tnew, snew, psel, qsel, tiles, turned, gram, held, summed, sem = refs[5:]
    count = meta[sz.live]
    steps = big_steps(count)
    loads = steps * (ROWS // ROWS_FIRST)

    def fetch(g):
        part = pl.ds(g * ROWS_FIRST, ROWS_FIRST)
        return pltpu.make_async_copy(tiles_hbm.at[part], tiles.at[part], sem.at[g])

    def start(g, carry):
        fetch(g).start()
        return carry

    lax.fori_loop(0, loads, start, 0)
    clear_sums(sz, summed)

    def products(g, total):
        spots = [g * ROWS + u for u in range(ROWS)]
        left = jnp.concatenate([t0[i] for i in spots], axis=1)
        return total + nn(left, jnp.concatenate([s0[i].T for i in spots], axis=0))

    gram[...] = lax.fori_loop(0, steps, products, jnp.zeros(gram.shape, F32))

    def block_row(i):
        cols = [col[m, i] for m in range(sz.nz)]
        parts = [tiles[i, m] for m in range(sz.nz)]
        flipped = [part.T for part in parts]
        for m in range(sz.nz):
            turned[i, pl.ds(m * sz.blk, sz.blk), :] = flipped[m]
        gathered = jnp.concatenate([t0[c] for c in cols], axis=1)
        forward = nn(gathered, jnp.concatenate(flipped, axis=0))
        held[i] = forward
        tnew[i] = forward.astype(BF16)
        scatter_terms(sz, summed, cols, nn(s0[i], jnp.concatenate(parts, axis=1)))

    def stepper(rows):
        def step(g, carry):
            for part in range(rows // ROWS_FIRST):
                fetch(g * (rows // ROWS_FIRST) + part).wait()
            for u in range(rows):
                block_row(g * rows + u)
            return carry

        return step

    short = ROWS // ROWS_PART
    lax.fori_loop(0, short, stepper(ROWS_PART), 0)
    lax.fori_loop(1, steps, stepper(ROWS), 0)
    finish_local(sz, meta, held, lambda i: summed[i], tnew, snew, psel, qsel)


def first_products(sz, meta, col, tiles, t0, s0):
    turned = shape((sz.blocks, sz.nz * sz.blk, sz.blk), BF16)
    return call(
        functools.partial(first_kernel, sz),
        [SMEM, SMEM, HBM, VMEM, VMEM],
        [VMEM] * 7,
        [sz.field, sz.field, sz.picked, sz.picked, shape(tiles.shape, BF16), turned]
        + [shape((sz.chan, sz.chan), F32)],
        [pltpu.VMEM((sz.blocks, sz.chan, sz.blk), F32)] * 2
        + [pltpu.SemaphoreType.DMA((sz.blocks // ROWS_FIRST,))],
        4 * sz.blocks * sz.nz * sz.chan * sz.blk * sz.blk,
        12 << 20,
        24,
    )(meta, col, keep(tiles), t0, s0)


def row_products(sz, col, low, high, rows, arrays, tnew, held, summed):
    tiles, turned, tcur, scur, tprev = arrays

    def block_row(i):
        cols = [col[m, i] for m in range(sz.nz)]
        gathered = jnp.concatenate([tcur[c] for c in cols], axis=1)
        forward = 2.0 * nn(gathered, turned[i]) - tprev[i].astype(F32)
        held[i] = forward
        tnew[i] = forward.astype(BF16)
        wide = jnp.concatenate([tiles[i, m] for m in range(sz.nz)], axis=1)
        scatter_terms(sz, summed, cols, nn(scur[i], wide))

    def step(g, carry):
        for u in range(rows):
            block_row(g * rows + u)
        return carry

    lax.fori_loop(low, high, step, 0)


def local_kernel(sz, *refs):
    meta, col, tiles, turned, tcur, scur, tprev, sprev = refs[:8]
    tnew, snew, psel, qsel, gram, held, summed = refs[8:]
    clear_sums(sz, summed)
    steps = big_steps(meta[sz.live])
    arrays = (tiles, turned, tcur, scur, tprev)
    row_products(sz, col, 0, steps, ROWS, arrays, tnew, held, summed)

    def adjoint(i):
        return 2.0 * summed[i] - sprev[i].astype(F32)

    finish_local(sz, meta, held, adjoint, tnew, snew, psel, qsel)

    def products(g, total):
        left, right = [], []
        for u in range(ROWS):
            i = g * ROWS + u
            left.append(jnp.concatenate([tcur[i], tnew[i]], axis=0))
            right.append(jnp.concatenate([sprev[i], scur[i]], axis=0).T)
        return total + nn(jnp.concatenate(left, axis=1), jnp.concatenate(right, axis=0))

    gram[...] = lax.fori_loop(0, steps, products, jnp.zeros(gram.shape, F32))


def local_products(sz, meta, col, tiles, turned, fields):
    gram = shape((2 * sz.chan, 2 * sz.chan), F32)
    return call(
        functools.partial(local_kernel, sz),
        [SMEM] * 2 + [VMEM] * 6,
        [VMEM] * 5,
        [sz.field, sz.field, sz.picked, sz.picked, gram],
        [pltpu.VMEM((sz.blocks, sz.chan, sz.blk), F32)] * 2,
        4 * sz.blocks * sz.nz * sz.chan * sz.blk * sz.blk,
        12 << 20,
        24,
    )(meta, col, tiles, turned, *fields)


def early_rows_kernel(sz, *refs):
    meta, col, tiles, turned, tcur, scur, tprev, _ = refs[:8]
    tnew, held, summed = refs[8:]
    clear_sums(sz, summed)
    cut = part_steps(meta[sz.live]) // 2
    arrays = (tiles, turned, tcur, scur, tprev)
    row_products(sz, col, 0, cut, ROWS_PART, arrays, tnew, held, summed)


def late_rows_kernel(sz, *refs):
    meta, col, tiles, turned, tcur, scur, tprev, sprev = refs[:8]
    tnew, held, summed, snew, psel, qsel = refs[12:]
    steps = part_steps(meta[sz.live])
    arrays = (tiles, turned, tcur, scur, tprev)
    row_products(sz, col, steps // 2, steps, ROWS_PART, arrays, tnew, held, summed)

    def adjoint(i):
        return 2.0 * summed[i] - sprev[i].astype(F32)

    finish_local(sz, meta, held, adjoint, tnew, snew, psel, qsel)


def part_products(sz, meta, col, tiles, turned, fields, before, token):
    sums = shape((sz.blocks, sz.chan, sz.blk), F32)
    args = [meta, col, tiles, turned, *fields]
    outs, aliases = [sz.field, sums, sums], {}
    if before is None:
        args[-1] = token
    else:
        aliases = {len(args) + k: k for k in range(3)}
        args += [*before, token]
        outs += [sz.field, sz.picked, sz.picked]
    return call(
        functools.partial(early_rows_kernel if before is None else late_rows_kernel, sz),
        [SMEM] * 2 + [VMEM] * (len(args) - 2),
        [VMEM] * len(outs),
        outs,
        [],
        2 * sz.blocks * sz.nz * sz.chan * sz.blk * sz.blk,
        6 << 20,
        8,
        aliases,
    )(*args)


def add_coupled(sz, scale, meta, got, across, psel, qsel, pacc, qacc, which):
    for j in range(sz.pairs):
        pacc[j] = psel[j]
        qacc[j] = qsel[j]
    some = [(r, h, j) for r, h, j in sz.couplings() if r in which]
    terms = {j: nn(got[r][sz.forward_part(h), :], across[j]) for r, h, j in some}
    for r, h, j in some:
        terms[j] = (scale * meta[sz.flags + r].astype(F32)) * terms[j]
        spot = meta[sz.first_row + j]
        pacc[spot] = pacc[spot] + terms[j]
        spot = meta[sz.first_send + j]
        qacc[spot] = qacc[spot] + scale * got[r][sz.adjoint_part(h), :].astype(F32)
    return terms


def correct_kernel(sz, axis, *refs):
    meta, across, psel, qsel, gram0, gram, sold = refs[:7]
    got, refs = refs[7 : 7 + sz.rounds], refs[7 + sz.rounds :]
    pacc, qacc, keep_half, give_half, whole = refs
    which = range(sz.rounds)
    terms = add_coupled(sz, 2.0, meta, got, across, psel, qsel, pacc, qacc, which)
    left = jnp.concatenate([terms[j].astype(BF16) for j in range(sz.pairs)], axis=1)
    right = [sold[meta[sz.rows + j]].T for j in range(sz.pairs)]
    extra = nn(left, jnp.concatenate(right, axis=0))
    one, two = pl.ds(0, sz.chan), pl.ds(sz.chan, sz.chan)
    whole[one, one] = gram0[...]
    whole[two, one] = gram[one, one]
    whole[two, two] = gram[one, two]
    whole[one, two] = gram[two, two] + extra
    odd = lax.rem(lax.axis_index(axis), 2)
    keep_half[...] = whole[pl.ds(pl.multiple_of(odd * sz.chan, sz.chan), sz.chan), :]
    give_half[...] = whole[pl.ds(pl.multiple_of((1 - odd) * sz.chan, sz.chan), sz.chan), :]


def correct(sz, axis, meta, across, picked, got, gram0, gram, sold):
    args = [meta, across, *picked, gram0, gram, sold, *got]
    half = shape((sz.chan, 2 * sz.chan), F32)
    return call(
        functools.partial(correct_kernel, sz, axis),
        [SMEM] + [VMEM] * (len(args) - 1),
        [VMEM] * 4,
        [sz.picked, sz.picked, half, half],
        [pltpu.VMEM((2 * sz.chan, 2 * sz.chan), F32)],
        4 * sz.pairs * sz.chan * sz.blk * sz.blk,
        3 << 20,
        8,
    )(*args)


def patch(sz, meta, cross, tnew, snew, pacc, qacc, pays):
    for j in range(sz.pairs):
        tnew[meta[sz.rows + j]] = pacc[meta[sz.first_row + j]].astype(BF16)
        snew[meta[sz.sends + j]] = qacc[meta[sz.first_send + j]].astype(BF16)
    fill_pays(sz, meta, tnew, snew, cross, pays)


def start_kernel(sz, *refs):
    meta, cross, _, _, across, psel, qsel = refs[:7]
    got, refs = refs[7 : 7 + sz.rounds], refs[7 + sz.rounds :]
    tnew, snew = refs[:2]
    pacc, qacc = refs[-2:]
    add_coupled(sz, 1.0, meta, got, across, psel, qsel, pacc, qacc, range(sz.rounds))
    patch(sz, meta, cross, tnew, snew, pacc, qacc, refs[2:-2])


def join_kernel(sz, *refs):
    meta, cross, _, _, pacc, qacc, tnew, snew = refs[:8]
    patch(sz, meta, cross, tnew, snew, pacc, qacc, refs[8:])


def join(sz, meta, cross, base, rest, first):
    args = [meta, cross, *base, *rest]
    outs = [sz.field, sz.field] + [sz.pay] * sz.rounds
    outs = call(
        functools.partial(start_kernel if first else join_kernel, sz),
        [SMEM] + [VMEM] * (len(args) - 1),
        [VMEM] * len(outs),
        outs,
        [pltpu.VMEM(sz.picked.shape, F32)] * 2 if first else [],
        2 * sz.pairs * sz.chan * sz.blk * sz.blk,
        5 << 20,
        8,
        {2: 0, 3: 1},
    )(*args)
    return outs[0], outs[1], outs[2:]


def output_weights(weight):
    wide = [weight[k].astype(F32) for k in range(weight.shape[0])]
    ahead = jnp.concatenate([w.T for w in wide], axis=1).astype(BF16)
    back = jnp.concatenate(wide, axis=1).astype(BF16)
    return ahead, back


def output_block(sz, left, fields, held, spot):
    value = nn(left[...], jnp.concatenate(fields, axis=0)).astype(BF16)
    for t in range(sz.chan // SUB):
        held[(t,) + spot if len(spot) == 1 else (spot[1], t)] = value[t * SUB : (t + 1) * SUB]


def output_kernel(sz, low, *refs):
    forward, adjoint = refs[:4], refs[4:8]
    if low == 0:
        weight, ahead, back, held_out, held_grad = refs[8], *refs[10:]
        wide_ahead, wide_back = output_weights(weight)
        ahead[...] = wide_ahead
        back[...] = wide_back
        copies = []
    else:
        ahead, back, before_out, before_grad = refs[8:12]
        held_out, held_grad, out4, grad4, sem = refs[13:]
        part = pl.ds(0, low)
        copies = [
            pltpu.make_async_copy(before_out, out4.at[:, part], sem.at[0]),
            pltpu.make_async_copy(before_grad, grad4.at[:, part], sem.at[1]),
        ]
    for copy in copies:
        copy.start()

    def step(g, carry):
        for u in range(ROWS_PART):
            n = g * ROWS_PART + u
            output_block(sz, ahead, [f[low + n] for f in forward], held_out, (n,))
            output_block(sz, back, [f[low + n] for f in adjoint], held_grad, (n,))
        return carry

    lax.fori_loop(0, held_out.shape[1] // ROWS_PART, step, 0)
    for copy in copies:
        copy.wait()


def base_outputs(sz, low, high, forward, adjoint, rest, token, orders):
    groups = sz.chan // SUB
    held = shape((groups, high - low, SUB, sz.blk), BF16)
    whole = shape((groups, sz.blocks, SUB, sz.blk), BF16)
    wide = shape((sz.chan, orders * sz.chan), BF16)
    args = [*forward, *adjoint, *rest, token]
    outs = [wide, wide, held, held] if low == 0 else [held, held, whole, whole]
    return call(
        functools.partial(output_kernel, sz, low),
        [VMEM] * len(args),
        [VMEM] * 4 if low == 0 else [VMEM] * 2 + [HBM] * 2,
        outs,
        [pltpu.SemaphoreType.DMA((2,))] if low else [],
        16 * (high - low) * sz.chan * sz.chan * sz.blk,
        6 << 20,
        8,
    )(*args)


def fixed_blocks(sz, meta, which, weights, fields, last, held):
    for r, h, j in sz.couplings():
        if r in which:
            for side, spot, first in ((0, sz.rows, sz.first_row), (1, sz.sends, sz.first_send)):
                i = meta[spot + j]
                stack = [f[i] for f in fields[3 * side : 3 * side + 3]]
                stack.append(last[side][meta[first + j]].astype(BF16))
                output_block(sz, weights[side], stack, held[side], (None, j))


def fixed_copies(sz, meta, which, over, held, outs, sem):
    copies = []
    for side, spot in ((0, sz.rows), (1, sz.sends)):
        seen = [meta[spot + j] for r, h, j in sz.couplings() if r in over]
        for r, h, j in sz.couplings():
            if r in which:
                i = meta[spot + j]
                fresh = jnp.bool_(True)
                for other in seen:
                    fresh = jnp.logical_and(fresh, other != i)
                seen.append(i)
                copy = pltpu.make_async_copy(
                    held[side].at[j], outs[side].at[:, i], sem.at[side, j]
                )
                copies.append((fresh, copy))
    return copies


def early_kernel(sz, which, low, *refs):
    meta, across, psel, qsel = refs[:4]
    got, refs = dict(zip(which, refs[4 : 4 + len(which)])), refs[4 + len(which) :]
    weights, fields, high = refs[:2], refs[2:8], refs[8:10]
    pacc, qacc, held_out, held_grad, out4, grad4, sem_base = refs[13:]
    part = pl.ds(low, high[0].shape[1])
    base = [
        pltpu.make_async_copy(high[0], out4.at[:, part], sem_base.at[0]),
        pltpu.make_async_copy(high[1], grad4.at[:, part], sem_base.at[1]),
    ]
    for copy in base:
        copy.start()
    add_coupled(sz, 2.0, meta, got, across, psel, qsel, pacc, qacc, which)
    fixed_blocks(sz, meta, which, weights, fields, (pacc, qacc), (held_out, held_grad))
    for copy in base:
        copy.wait()


def early_outputs(sz, low, meta, across, picked, got, which, weights, fields, high, token, outs):
    args = [meta, across, *picked, *(got[r] for r in which), *weights, *fields, *high, token]
    whole = [shape(out.shape, BF16) for out in outs]
    held = shape((sz.pairs, sz.chan // SUB, SUB, sz.blk), BF16)
    return call(
        functools.partial(early_kernel, sz, which, low),
        [SMEM] + [VMEM] * (len(args) - 1) + [HBM] * 2,
        [VMEM] * 4 + [HBM] * 2,
        [sz.picked, sz.picked, held, held] + whole,
        [pltpu.SemaphoreType.DMA((2,))],
        8 * sz.pairs * sz.chan * sz.blk * sz.blk,
        4 << 20,
        8,
        {len(args): 4, len(args) + 1: 5},
    )(*args, *outs)


def fix_kernel(sz, axis, early, late, *refs):
    meta, across, psel, qsel = refs[:4]
    got, refs = dict(zip(late, refs[4 : 4 + len(late)])), refs[4 + len(late) :]
    weights, fields, fixed = refs[:2], refs[2:8], refs[8:10]
    mine, theirs = refs[10:12]
    out4, grad4, grad_w, pacc, qacc, held_out, held_grad, total, sem_out, sem_w = refs[14:]
    held, outs = (held_out, held_grad), (out4, grad4)
    odd = lax.rem(lax.axis_index(axis), 2) == 1
    top = jnp.where(odd, theirs[...], mine[...])
    low = jnp.where(odd, mine[...], theirs[...])
    zeroth, first = top[:, : sz.chan], low[:, : sz.chan]
    total[0] = zeroth
    total[1] = first
    total[2] = 2.0 * low[:, sz.chan :] - zeroth
    total[3] = 2.0 * top[:, sz.chan :] - first
    weight_copy = pltpu.make_async_copy(total, grad_w, sem_w)
    weight_copy.start()
    add_coupled(sz, 2.0, meta, got, across, psel, qsel, pacc, qacc, late)
    copies = fixed_copies(sz, meta, early, late, fixed, outs, sem_out)
    for fresh, copy in copies:
        pl.when(fresh)(copy.start)
    fixed_blocks(sz, meta, late, weights, fields, (pacc, qacc), held)
    last = fixed_copies(sz, meta, late, [], held, outs, sem_out)
    for fresh, copy in last:
        pl.when(fresh)(copy.start)
    for fresh, copy in copies + last:
        pl.when(fresh)(copy.wait)
    weight_copy.wait()


def fix_outputs(
    sz, axis, meta, across, picked, got, early, late, weights, fields, fixed, mine, theirs, outs
):
    args = [meta, across, *picked, *(got[r] for r in late), *weights, *fields, *fixed]
    args += [mine, theirs]
    whole = [shape(out.shape, BF16) for out in outs]
    held = pltpu.VMEM((sz.pairs, sz.chan // SUB, SUB, sz.blk), BF16)
    total = (4, sz.chan, sz.chan)
    return call(
        functools.partial(fix_kernel, sz, axis, early, late),
        [SMEM] + [VMEM] * (len(args) - 1) + [HBM] * 2,
        [HBM] * 3,
        whole + [shape(total, F32)],
        [pltpu.VMEM(sz.picked.shape, F32)] * 2
        + [held, held, pltpu.VMEM(total, F32)]
        + [pltpu.SemaphoreType.DMA((2, sz.pairs)), pltpu.SemaphoreType.DMA],
        8 * len(late) * sz.hb * sz.chan * sz.blk * sz.blk,
        2 << 20,
        8,
        {len(args): 0, len(args) + 1: 1},
    )(*args, *outs)


def add_kernel(gated, inputs, *refs):
    mine, theirs = refs[:2]
    outs = refs[inputs:]
    if gated:
        outs[2][...] = refs[2][...]
    outs[0][...] = mine[...] + theirs[...]
    if len(outs) > 1:
        outs[1][...] = jnp.zeros(outs[1].shape, F32)


def add(mine, theirs, pay, after, last=False):
    outs = [shape(mine.shape, F32)] + ([] if last else [TOKEN])
    args = [mine, theirs]
    if pay is not None:
        outs.append(shape(pay.shape, BF16))
        args.append(pay)
    args += after
    return call(
        functools.partial(add_kernel, pay is not None, len(args)),
        [VMEM] * len(args),
        [VMEM] * len(outs),
        outs,
        [],
        mine.size,
        12 * mine.size,
        2,
    )(*args)


def from_partner(values, bit):
    count = lax.axis_size("dom")
    route = []
    for low in range(count):
        high = low | 1 << bit
        if high != low and high < count:
            route += [(low, high), (high, low)]
    return lax.ppermute(values, "dom", route)


def local(
    features,
    cheb_weight,
    lap_tiles,
    col_index,
    cross_tiles,
    send_index,
    row_index,
    pair_on,
    blk_live,
    cotangent,
):
    sz = Sizes(features, lap_tiles, cross_tiles)
    split = (sz.chan // SUB, SUB, sz.blocks, sz.blk)
    x4 = features.reshape(split).transpose(0, 2, 1, 3)
    u4 = cotangent.reshape(split).transpose(0, 2, 1, 3)
    coupling = cross_tiles.reshape(sz.pairs, sz.blk, sz.blk)
    send, row = send_index.transpose(0, 2, 1), row_index.transpose(0, 2, 1)

    packed = pack(sz, x4, u4, coupling, send, row, pair_on, blk_live, col_index.T)
    t0, s0, cross, across, meta, col = packed[:6]
    everyone = range(sz.rounds)
    got = [from_partner(pay, bit) for bit, pay in enumerate(packed[6:])]
    *base, psel, qsel, tiles, turned, gram0 = first_products(sz, meta, col, lap_tiles, t0, s0)
    t1, s1, pays = join(sz, meta, cross, base, [across, psel, qsel, *got], True)

    got = [from_partner(pay, bit) for bit, pay in enumerate(pays)]
    fields = (t1, s1, t0, s0)
    *base, psel, qsel, gram = local_products(sz, meta, col, tiles, turned, fields)
    *picked, mine, given = correct(
        sz, "dom", meta, across, (psel, qsel), got, gram0, gram, s1
    )
    theirs = from_partner(given, 0)
    t2, s2, pays = join(sz, meta, cross, base, picked, False)

    state = {}

    middle = sz.blocks // (2 * ROWS_PART) * ROWS_PART
    orders = cheb_weight.shape[0]

    def window_early_rows(token):
        fields = (t2, s2, t1, s1)
        state["part"] = part_products(sz, meta, col, tiles, turned, fields, None, token)
        return None

    def window_late_rows(token):
        fields = (t2, s2, t1, s1)
        t3, _, _, s3, *state["picked"] = part_products(
            sz, meta, col, tiles, turned, fields, state["part"], token
        )
        state["last"] = (t3, s3)
        return state["picked"][0]

    def window_low(token):
        t3, s3 = state["last"]
        *state["weights"], left, right = base_outputs(
            sz, 0, middle, (t0, t1, t2, t3), (s0, s1, s2, s3), [cheb_weight], token, orders
        )
        state["low"] = [left, right]
        return left

    def window_high(token):
        t3, s3 = state["last"]
        rest = state["weights"] + state["low"]
        left, right, out4, grad4 = base_outputs(
            sz, middle, sz.blocks, (t0, t1, t2, t3), (s0, s1, s2, s3), rest, token, orders
        )
        state["high"], state["outs"] = [left, right], [out4, grad4]
        return left

    windows = [window_early_rows, window_late_rows, window_low, window_high]
    bits = list(reversed(range(1, (lax.axis_size("dom") - 1).bit_length())))
    pays, got = list(pays), [None] * sz.rounds
    history = (t0, t1, t2, s0, s1, s2)
    got[0] = from_partner(pays[0], 0)
    early = [0] + [bit for bit in bits[:-1] if bit < sz.rounds]
    late = [bit for bit in everyone if bit not in early]
    far = pays[bits[0]] if bits[0] < sz.rounds else None
    mine, token, *rest = add(mine, theirs, far, [])
    held = [got[0]]
    for at, bit in enumerate(bits):
        if bit < sz.rounds:
            pays[bit] = rest[0]
        theirs = from_partner(mine, bit)
        if bit < sz.rounds:
            got[bit] = from_partner(pays[bit], bit)
        if at < len(windows):
            token = windows[at](token)
        last = at + 1 == len(bits)
        gated = not last and bits[at + 1] < sz.rounds
        after = ([] if token is None else [token]) + held
        held = [got[bit]] if bit < sz.rounds else []
        if last:
            (mine,) = add(mine, theirs, None, after, True)
        else:
            mine, token, *rest = add(mine, theirs, pays[bits[at + 1]] if gated else None, after)
    theirs = from_partner(mine, 0)
    *picked, left, right, out4, grad4 = early_outputs(
        sz,
        middle,
        meta,
        across,
        state["picked"],
        got,
        early,
        state["weights"],
        history,
        state["high"],
        mine,
        state["outs"],
    )
    out4, grad4, grad_w = fix_outputs(
        sz,
        "dom",
        meta,
        across,
        picked,
        got,
        early,
        late,
        state["weights"],
        history,
        [left, right],
        mine,
        theirs,
        [out4, grad4],
    )
    conv_out = out4.transpose(0, 2, 1, 3).reshape(features.shape)
    grad_x = grad4.transpose(0, 2, 1, 3).reshape(features.shape)
    return (conv_out, grad_x, grad_w)


def solution(mesh):
    in_specs = (
        P(None, "dom"),
        P(),
        P("dom", None, None, None),
        P("dom", None),
        P("dom", None, None, None, None),
        P("dom", None, None),
        P("dom", None, None),
        P("dom", None),
        P("dom"),
        P(None, "dom"),
    )
    out_specs = (P(None, "dom"), P(None, "dom"), P())
    return jax.shard_map(local, mesh=mesh, in_specs=in_specs, out_specs=out_specs, check_vma=False)
```

```python
import functools

import jax
import jax.numpy as jnp
from jax import lax
from jax.experimental import pallas as pl
from jax.experimental.pallas import tpu as pltpu
from jax.sharding import PartitionSpec as P


F32 = jnp.float32
BF16 = jnp.bfloat16
SUB = 8
LANES = 128
ROWS_FIRST = 8
ROWS_PART = 16
ROWS = 32

VMEM = pl.BlockSpec(memory_space=pltpu.VMEM)
SMEM = pl.BlockSpec(memory_space=pltpu.SMEM)
HBM = pl.BlockSpec(memory_space=pltpu.HBM)
TOKEN = jax.ShapeDtypeStruct((SUB, LANES), F32)


def shape(dims, dtype):
    return jax.ShapeDtypeStruct(dims, dtype)


def nn(a, b):
    return lax.dot_general(a, b, (((1,), (0,)), ((), ())), preferred_element_type=F32)


class Sizes:
    def __init__(self, features, lap_tiles, cross_tiles):
        self.chan = features.shape[0]
        self.blocks, self.nz, self.blk = lap_tiles.shape[:3]
        self.rounds, self.hb = cross_tiles.shape[1:3]
        self.pairs = self.rounds * self.hb
        self.rows = 0
        self.sends = self.pairs
        self.first_row = 2 * self.pairs
        self.first_send = 3 * self.pairs
        self.flags = 4 * self.pairs
        self.live = self.flags + self.rounds
        self.meta = self.live + 1
        self.half = self.hb * self.chan
        self.field = shape((self.blocks, self.chan, self.blk), BF16)
        self.picked = shape((self.pairs, self.chan, self.blk), F32)
        self.pay = shape((2 * self.half, self.blk), BF16)

    def couplings(self):
        return [(r, h, r * self.hb + h) for r in range(self.rounds) for h in range(self.hb)]

    def forward_part(self, h):
        return pl.ds(h * self.chan, self.chan)

    def adjoint_part(self, h):
        return pl.ds(self.half + h * self.chan, self.chan)


def call(kernel, in_specs, out_specs, out_shape, scratch, flops, moved, limit, aliases=None):
    return pl.pallas_call(
        kernel,
        in_specs=in_specs,
        out_specs=out_specs,
        out_shape=out_shape,
        scratch_shapes=scratch,
        input_output_aliases=aliases or {},
        compiler_params=pltpu.CompilerParams(vmem_limit_bytes=limit << 20),
        cost_estimate=pl.CostEstimate(flops=flops, bytes_accessed=moved, transcendentals=0),
    )


def fill_pays(sz, meta, tnew, snew, cross, pays):
    for r, h, j in sz.couplings():
        pays[r][sz.forward_part(h), :] = tnew[meta[sz.sends + j]]
        term = nn(snew[meta[sz.rows + j]], cross[j])
        factor = meta[sz.flags + r].astype(F32)
        pays[r][sz.adjoint_part(h), :] = (factor * term).astype(BF16)


def pack_kernel(sz, *refs):
    x4, u4, coupling, send, row, pair, live_s, col = refs[:8]
    xb, ub, cross, across, meta, col_out = refs[8:14]
    pays = refs[14 : 14 + sz.rounds]
    send_s, row_s, pair_s, sem_x, sem_u, sem_t, sem_i = refs[14 + sz.rounds :]
    small = [
        pltpu.make_async_copy(send, send_s, sem_i.at[0]),
        pltpu.make_async_copy(row, row_s, sem_i.at[1]),
        pltpu.make_async_copy(pair, pair_s, sem_i.at[2]),
    ]
    tiles = pltpu.make_async_copy(coupling, cross, sem_t)
    copies = []
    for t in range(sz.chan // SUB):
        part = pl.ds(t * SUB, SUB)
        copies.append(pltpu.make_async_copy(x4.at[t], xb.at[:, part, :], sem_x.at[t]))
        copies.append(pltpu.make_async_copy(u4.at[t], ub.at[:, part, :], sem_u.at[t]))
    copies.append(pltpu.make_async_copy(col, col_out, sem_i.at[3]))
    for copy in small + [tiles] + copies:
        copy.start()
    for copy in small:
        copy.wait()
    count = live_s[0]
    rows = [lax.rem(row_s[0, h, r], count) for r, h, _ in sz.couplings()]
    sends = [lax.rem(send_s[0, h, r], count) for r, h, _ in sz.couplings()]
    for values, spot, first in (
        (rows, sz.rows, sz.first_row),
        (sends, sz.sends, sz.first_send),
    ):
        for j, value in enumerate(values):
            earliest = jnp.int32(j)
            for q in reversed(range(j)):
                earliest = jnp.where(values[q] == value, q, earliest)
            meta[spot + j] = value
            meta[first + j] = earliest
    for r in range(sz.rounds):
        meta[sz.flags + r] = pair_s[0, r]
    meta[sz.live] = count
    tiles.wait()
    for j in range(sz.pairs):
        across[j] = cross[j].T
    for copy in copies:
        copy.wait()

    def clear(i, carry):
        xb[i] = jnp.zeros(xb.shape[1:], BF16)
        ub[i] = jnp.zeros(ub.shape[1:], BF16)
        return carry

    lax.fori_loop(count, sz.blocks, clear, 0)
    fill_pays(sz, meta, xb, ub, cross, pays)


def keep(array):
    return pltpu.with_memory_space_constraint(array, pltpu.HBM)


def pack(sz, *args):
    args = [array if array.size == 1 else keep(array) for array in args]
    _, _, _, send, row, pair, _, col = args
    groups = sz.chan // SUB
    cross = shape((sz.pairs, sz.blk, sz.blk), BF16)
    table = pltpu.SMEM((sz.meta,), jnp.int32)
    return call(
        functools.partial(pack_kernel, sz),
        [HBM] * 6 + [SMEM, HBM],
        [VMEM] * 4 + [SMEM, SMEM] + [VMEM] * sz.rounds,
        [sz.field, sz.field, cross, cross, table, pltpu.SMEM(col.shape, jnp.int32)]
        + [sz.pay] * sz.rounds,
        [
            pltpu.SMEM(send.shape, jnp.int32),
            pltpu.SMEM(row.shape, jnp.int32),
            pltpu.SMEM(pair.shape, jnp.int32),
            pltpu.SemaphoreType.DMA((groups,)),
            pltpu.SemaphoreType.DMA((groups,)),
            pltpu.SemaphoreType.DMA,
            pltpu.SemaphoreType.DMA((4,)),
        ],
        1000,
        4 << 20,
        8,
    )(*args)


def big_steps(count):
    return (count + ROWS - 1) // ROWS


def part_steps(count):
    return (count + ROWS_PART - 1) // ROWS_PART


def clear_sums(sz, summed):
    def clear(i, carry):
        summed[i] = jnp.zeros(summed.shape[1:], F32)
        return carry

    lax.fori_loop(0, sz.blocks, clear, 0, unroll=4)


def scatter_terms(sz, summed, cols, terms):
    for m in range(sz.nz):
        summed[cols[m]] = summed[cols[m]] + terms[:, m * sz.blk : (m + 1) * sz.blk]


def finish_local(sz, meta, held, adjoint, tnew, snew, psel, qsel):
    count = meta[sz.live]

    def finish(g, carry):
        for u in range(ROWS):
            i = g * ROWS + u
            snew[i] = adjoint(i).astype(BF16)
        return carry

    lax.fori_loop(0, big_steps(count), finish, 0)

    def dead(i, carry):
        tnew[i] = jnp.zeros(tnew.shape[1:], BF16)
        snew[i] = jnp.zeros(snew.shape[1:], BF16)
        return carry

    lax.fori_loop(count, sz.blocks, dead, 0)
    for j in range(sz.pairs):
        psel[j] = held[meta[sz.rows + j]]
        qsel[j] = adjoint(meta[sz.sends + j])


def first_kernel(sz, *refs):
    meta, col, tiles_hbm, t0, s0 = refs[:5]
    tnew, snew, psel, qsel, tiles, turned, gram, held, summed, sem = refs[5:]
    count = meta[sz.live]
    steps = big_steps(count)
    loads = steps * (ROWS // ROWS_FIRST)

    def fetch(g):
        part = pl.ds(g * ROWS_FIRST, ROWS_FIRST)
        return pltpu.make_async_copy(tiles_hbm.at[part], tiles.at[part], sem.at[g])

    def start(g, carry):
        fetch(g).start()
        return carry

    lax.fori_loop(0, loads, start, 0)
    clear_sums(sz, summed)

    def products(g, total):
        spots = [g * ROWS + u for u in range(ROWS)]
        left = jnp.concatenate([t0[i] for i in spots], axis=1)
        return total + nn(left, jnp.concatenate([s0[i].T for i in spots], axis=0))

    gram[...] = lax.fori_loop(0, steps, products, jnp.zeros(gram.shape, F32))

    def block_row(i):
        cols = [col[m, i] for m in range(sz.nz)]
        parts = [tiles[i, m] for m in range(sz.nz)]
        flipped = [part.T for part in parts]
        for m in range(sz.nz):
            turned[i, pl.ds(m * sz.blk, sz.blk), :] = flipped[m]
        gathered = jnp.concatenate([t0[c] for c in cols], axis=1)
        forward = nn(gathered, jnp.concatenate(flipped, axis=0))
        held[i] = forward
        tnew[i] = forward.astype(BF16)
        scatter_terms(sz, summed, cols, nn(s0[i], jnp.concatenate(parts, axis=1)))

    def stepper(rows):
        def step(g, carry):
            for part in range(rows // ROWS_FIRST):
                fetch(g * (rows // ROWS_FIRST) + part).wait()
            for u in range(rows):
                block_row(g * rows + u)
            return carry

        return step

    short = ROWS // ROWS_PART
    lax.fori_loop(0, short, stepper(ROWS_PART), 0)
    lax.fori_loop(1, steps, stepper(ROWS), 0)
    finish_local(sz, meta, held, lambda i: summed[i], tnew, snew, psel, qsel)


def first_products(sz, meta, col, tiles, t0, s0):
    turned = shape((sz.blocks, sz.nz * sz.blk, sz.blk), BF16)
    return call(
        functools.partial(first_kernel, sz),
        [SMEM, SMEM, HBM, VMEM, VMEM],
        [VMEM] * 7,
        [sz.field, sz.field, sz.picked, sz.picked, shape(tiles.shape, BF16), turned]
        + [shape((sz.chan, sz.chan), F32)],
        [pltpu.VMEM((sz.blocks, sz.chan, sz.blk), F32)] * 2
        + [pltpu.SemaphoreType.DMA((sz.blocks // ROWS_FIRST,))],
        4 * sz.blocks * sz.nz * sz.chan * sz.blk * sz.blk,
        12 << 20,
        24,
    )(meta, col, keep(tiles), t0, s0)


def row_products(sz, col, low, high, rows, arrays, tnew, held, summed):
    tiles, turned, tcur, scur, tprev = arrays

    def block_row(i):
        cols = [col[m, i] for m in range(sz.nz)]
        gathered = jnp.concatenate([tcur[c] for c in cols], axis=1)
        forward = 2.0 * nn(gathered, turned[i]) - tprev[i].astype(F32)
        held[i] = forward
        tnew[i] = forward.astype(BF16)
        wide = jnp.concatenate([tiles[i, m] for m in range(sz.nz)], axis=1)
        scatter_terms(sz, summed, cols, nn(scur[i], wide))

    def step(g, carry):
        for u in range(rows):
            block_row(g * rows + u)
        return carry

    lax.fori_loop(low, high, step, 0)


def local_kernel(sz, *refs):
    meta, col, tiles, turned, tcur, scur, tprev, sprev = refs[:8]
    tnew, snew, psel, qsel, gram, held, summed = refs[8:]
    clear_sums(sz, summed)
    steps = big_steps(meta[sz.live])
    arrays = (tiles, turned, tcur, scur, tprev)
    row_products(sz, col, 0, steps, ROWS, arrays, tnew, held, summed)

    def adjoint(i):
        return 2.0 * summed[i] - sprev[i].astype(F32)

    finish_local(sz, meta, held, adjoint, tnew, snew, psel, qsel)

    def products(g, total):
        left, right = [], []
        for u in range(ROWS):
            i = g * ROWS + u
            left.append(jnp.concatenate([tcur[i], tnew[i]], axis=0))
            right.append(jnp.concatenate([sprev[i], scur[i]], axis=0).T)
        return total + nn(jnp.concatenate(left, axis=1), jnp.concatenate(right, axis=0))

    gram[...] = lax.fori_loop(0, steps, products, jnp.zeros(gram.shape, F32))


def local_products(sz, meta, col, tiles, turned, fields):
    gram = shape((2 * sz.chan, 2 * sz.chan), F32)
    return call(
        functools.partial(local_kernel, sz),
        [SMEM] * 2 + [VMEM] * 6,
        [VMEM] * 5,
        [sz.field, sz.field, sz.picked, sz.picked, gram],
        [pltpu.VMEM((sz.blocks, sz.chan, sz.blk), F32)] * 2,
        4 * sz.blocks * sz.nz * sz.chan * sz.blk * sz.blk,
        12 << 20,
        24,
    )(meta, col, tiles, turned, *fields)


def early_rows_kernel(sz, *refs):
    meta, col, tiles, turned, tcur, scur, tprev, _ = refs[:8]
    tnew, held, summed = refs[8:]
    clear_sums(sz, summed)
    cut = part_steps(meta[sz.live]) // 2
    arrays = (tiles, turned, tcur, scur, tprev)
    row_products(sz, col, 0, cut, ROWS_PART, arrays, tnew, held, summed)


def late_rows_kernel(sz, *refs):
    meta, col, tiles, turned, tcur, scur, tprev, sprev = refs[:8]
    tnew, held, summed, snew, psel, qsel = refs[12:]
    steps = part_steps(meta[sz.live])
    arrays = (tiles, turned, tcur, scur, tprev)
    row_products(sz, col, steps // 2, steps, ROWS_PART, arrays, tnew, held, summed)

    def adjoint(i):
        return 2.0 * summed[i] - sprev[i].astype(F32)

    finish_local(sz, meta, held, adjoint, tnew, snew, psel, qsel)


def part_products(sz, meta, col, tiles, turned, fields, before, token):
    sums = shape((sz.blocks, sz.chan, sz.blk), F32)
    args = [meta, col, tiles, turned, *fields]
    outs, aliases = [sz.field, sums, sums], {}
    if before is None:
        args[-1] = token
    else:
        aliases = {len(args) + k: k for k in range(3)}
        args += [*before, token]
        outs += [sz.field, sz.picked, sz.picked]
    return call(
        functools.partial(early_rows_kernel if before is None else late_rows_kernel, sz),
        [SMEM] * 2 + [VMEM] * (len(args) - 2),
        [VMEM] * len(outs),
        outs,
        [],
        2 * sz.blocks * sz.nz * sz.chan * sz.blk * sz.blk,
        6 << 20,
        8,
        aliases,
    )(*args)


def add_coupled(sz, scale, meta, got, across, psel, qsel, pacc, qacc, which):
    for j in range(sz.pairs):
        pacc[j] = psel[j]
        qacc[j] = qsel[j]
    some = [(r, h, j) for r, h, j in sz.couplings() if r in which]
    terms = {j: nn(got[r][sz.forward_part(h), :], across[j]) for r, h, j in some}
    for r, h, j in some:
        terms[j] = (scale * meta[sz.flags + r].astype(F32)) * terms[j]
        spot = meta[sz.first_row + j]
        pacc[spot] = pacc[spot] + terms[j]
        spot = meta[sz.first_send + j]
        qacc[spot] = qacc[spot] + scale * got[r][sz.adjoint_part(h), :].astype(F32)
    return terms


def correct_kernel(sz, axis, *refs):
    meta, across, psel, qsel, gram0, gram, sold = refs[:7]
    got, refs = refs[7 : 7 + sz.rounds], refs[7 + sz.rounds :]
    pacc, qacc, keep_half, give_half, whole = refs
    which = range(sz.rounds)
    terms = add_coupled(sz, 2.0, meta, got, across, psel, qsel, pacc, qacc, which)
    left = jnp.concatenate([terms[j].astype(BF16) for j in range(sz.pairs)], axis=1)
    right = [sold[meta[sz.rows + j]].T for j in range(sz.pairs)]
    extra = nn(left, jnp.concatenate(right, axis=0))
    one, two = pl.ds(0, sz.chan), pl.ds(sz.chan, sz.chan)
    whole[one, one] = gram0[...]
    whole[two, one] = gram[one, one]
    whole[two, two] = gram[one, two]
    whole[one, two] = gram[two, two] + extra
    odd = lax.rem(lax.axis_index(axis), 2)
    keep_half[...] = whole[pl.ds(pl.multiple_of(odd * sz.chan, sz.chan), sz.chan), :]
    give_half[...] = whole[pl.ds(pl.multiple_of((1 - odd) * sz.chan, sz.chan), sz.chan), :]


def correct(sz, axis, meta, across, picked, got, gram0, gram, sold):
    args = [meta, across, *picked, gram0, gram, sold, *got]
    half = shape((sz.chan, 2 * sz.chan), F32)
    return call(
        functools.partial(correct_kernel, sz, axis),
        [SMEM] + [VMEM] * (len(args) - 1),
        [VMEM] * 4,
        [sz.picked, sz.picked, half, half],
        [pltpu.VMEM((2 * sz.chan, 2 * sz.chan), F32)],
        4 * sz.pairs * sz.chan * sz.blk * sz.blk,
        3 << 20,
        8,
    )(*args)


def patch(sz, meta, cross, tnew, snew, pacc, qacc, pays):
    for j in range(sz.pairs):
        tnew[meta[sz.rows + j]] = pacc[meta[sz.first_row + j]].astype(BF16)
        snew[meta[sz.sends + j]] = qacc[meta[sz.first_send + j]].astype(BF16)
    fill_pays(sz, meta, tnew, snew, cross, pays)


def start_kernel(sz, *refs):
    meta, cross, _, _, across, psel, qsel = refs[:7]
    got, refs = refs[7 : 7 + sz.rounds], refs[7 + sz.rounds :]
    tnew, snew = refs[:2]
    pacc, qacc = refs[-2:]
    add_coupled(sz, 1.0, meta, got, across, psel, qsel, pacc, qacc, range(sz.rounds))
    patch(sz, meta, cross, tnew, snew, pacc, qacc, refs[2:-2])


def join_kernel(sz, *refs):
    meta, cross, _, _, pacc, qacc, tnew, snew = refs[:8]
    patch(sz, meta, cross, tnew, snew, pacc, qacc, refs[8:])


def join(sz, meta, cross, base, rest, first):
    args = [meta, cross, *base, *rest]
    outs = [sz.field, sz.field] + [sz.pay] * sz.rounds
    outs = call(
        functools.partial(start_kernel if first else join_kernel, sz),
        [SMEM] + [VMEM] * (len(args) - 1),
        [VMEM] * len(outs),
        outs,
        [pltpu.VMEM(sz.picked.shape, F32)] * 2 if first else [],
        2 * sz.pairs * sz.chan * sz.blk * sz.blk,
        5 << 20,
        8,
        {2: 0, 3: 1},
    )(*args)
    return outs[0], outs[1], outs[2:]


def output_weights(weight):
    wide = [weight[k].astype(F32) for k in range(weight.shape[0])]
    ahead = jnp.concatenate([w.T for w in wide], axis=1).astype(BF16)
    back = jnp.concatenate(wide, axis=1).astype(BF16)
    return ahead, back


def output_block(sz, left, fields, held, spot):
    value = nn(left[...], jnp.concatenate(fields, axis=0)).astype(BF16)
    for t in range(sz.chan // SUB):
        held[(t,) + spot if len(spot) == 1 else (spot[1], t)] = value[t * SUB : (t + 1) * SUB]


def output_kernel(sz, low, *refs):
    forward, adjoint = refs[:4], refs[4:8]
    if low == 0:
        weight, ahead, back, held_out, held_grad = refs[8], *refs[10:]
        wide_ahead, wide_back = output_weights(weight)
        ahead[...] = wide_ahead
        back[...] = wide_back
        copies = []
    else:
        ahead, back, before_out, before_grad = refs[8:12]
        held_out, held_grad, out4, grad4, sem = refs[13:]
        part = pl.ds(0, low)
        copies = [
            pltpu.make_async_copy(before_out, out4.at[:, part], sem.at[0]),
            pltpu.make_async_copy(before_grad, grad4.at[:, part], sem.at[1]),
        ]
    for copy in copies:
        copy.start()

    def step(g, carry):
        for u in range(ROWS_PART):
            n = g * ROWS_PART + u
            output_block(sz, ahead, [f[low + n] for f in forward], held_out, (n,))
            output_block(sz, back, [f[low + n] for f in adjoint], held_grad, (n,))
        return carry

    lax.fori_loop(0, held_out.shape[1] // ROWS_PART, step, 0)
    for copy in copies:
        copy.wait()


def base_outputs(sz, low, high, forward, adjoint, rest, token, orders):
    groups = sz.chan // SUB
    held = shape((groups, high - low, SUB, sz.blk), BF16)
    whole = shape((groups, sz.blocks, SUB, sz.blk), BF16)
    wide = shape((sz.chan, orders * sz.chan), BF16)
    args = [*forward, *adjoint, *rest, token]
    outs = [wide, wide, held, held] if low == 0 else [held, held, whole, whole]
    return call(
        functools.partial(output_kernel, sz, low),
        [VMEM] * len(args),
        [VMEM] * 4 if low == 0 else [VMEM] * 2 + [HBM] * 2,
        outs,
        [pltpu.SemaphoreType.DMA((2,))] if low else [],
        16 * (high - low) * sz.chan * sz.chan * sz.blk,
        6 << 20,
        8,
    )(*args)


def fixed_blocks(sz, meta, which, weights, fields, last, held):
    for r, h, j in sz.couplings():
        if r in which:
            for side, spot, first in ((0, sz.rows, sz.first_row), (1, sz.sends, sz.first_send)):
                i = meta[spot + j]
                stack = [f[i] for f in fields[3 * side : 3 * side + 3]]
                stack.append(last[side][meta[first + j]].astype(BF16))
                output_block(sz, weights[side], stack, held[side], (None, j))


def fixed_copies(sz, meta, which, over, held, outs, sem):
    copies = []
    for side, spot in ((0, sz.rows), (1, sz.sends)):
        seen = [meta[spot + j] for r, h, j in sz.couplings() if r in over]
        for r, h, j in sz.couplings():
            if r in which:
                i = meta[spot + j]
                fresh = jnp.bool_(True)
                for other in seen:
                    fresh = jnp.logical_and(fresh, other != i)
                seen.append(i)
                copy = pltpu.make_async_copy(
                    held[side].at[j], outs[side].at[:, i], sem.at[side, j]
                )
                copies.append((fresh, copy))
    return copies


def early_kernel(sz, which, low, *refs):
    meta, across, psel, qsel = refs[:4]
    got, refs = dict(zip(which, refs[4 : 4 + len(which)])), refs[4 + len(which) :]
    weights, fields, high = refs[:2], refs[2:8], refs[8:10]
    pacc, qacc, held_out, held_grad, out4, grad4, sem_base = refs[13:]
    part = pl.ds(low, high[0].shape[1])
    base = [
        pltpu.make_async_copy(high[0], out4.at[:, part], sem_base.at[0]),
        pltpu.make_async_copy(high[1], grad4.at[:, part], sem_base.at[1]),
    ]
    for copy in base:
        copy.start()
    add_coupled(sz, 2.0, meta, got, across, psel, qsel, pacc, qacc, which)
    fixed_blocks(sz, meta, which, weights, fields, (pacc, qacc), (held_out, held_grad))
    for copy in base:
        copy.wait()


def early_outputs(sz, low, meta, across, picked, got, which, weights, fields, high, token, outs):
    args = [meta, across, *picked, *(got[r] for r in which), *weights, *fields, *high, token]
    whole = [shape(out.shape, BF16) for out in outs]
    held = shape((sz.pairs, sz.chan // SUB, SUB, sz.blk), BF16)
    return call(
        functools.partial(early_kernel, sz, which, low),
        [SMEM] + [VMEM] * (len(args) - 1) + [HBM] * 2,
        [VMEM] * 4 + [HBM] * 2,
        [sz.picked, sz.picked, held, held] + whole,
        [pltpu.SemaphoreType.DMA((2,))],
        8 * sz.pairs * sz.chan * sz.blk * sz.blk,
        4 << 20,
        8,
        {len(args): 4, len(args) + 1: 5},
    )(*args, *outs)


def fix_kernel(sz, axis, early, late, *refs):
    meta, across, psel, qsel = refs[:4]
    got, refs = dict(zip(late, refs[4 : 4 + len(late)])), refs[4 + len(late) :]
    weights, fields, fixed = refs[:2], refs[2:8], refs[8:10]
    mine, theirs = refs[10:12]
    out4, grad4, grad_w, pacc, qacc, held_out, held_grad, total, sem_out, sem_w = refs[14:]
    held, outs = (held_out, held_grad), (out4, grad4)
    odd = lax.rem(lax.axis_index(axis), 2) == 1
    top = jnp.where(odd, theirs[...], mine[...])
    low = jnp.where(odd, mine[...], theirs[...])
    zeroth, first = top[:, : sz.chan], low[:, : sz.chan]
    total[0] = zeroth
    total[1] = first
    total[2] = 2.0 * low[:, sz.chan :] - zeroth
    total[3] = 2.0 * top[:, sz.chan :] - first
    weight_copy = pltpu.make_async_copy(total, grad_w, sem_w)
    weight_copy.start()
    add_coupled(sz, 2.0, meta, got, across, psel, qsel, pacc, qacc, late)
    copies = fixed_copies(sz, meta, early, late, fixed, outs, sem_out)
    for fresh, copy in copies:
        pl.when(fresh)(copy.start)
    fixed_blocks(sz, meta, late, weights, fields, (pacc, qacc), held)
    last = fixed_copies(sz, meta, late, [], held, outs, sem_out)
    for fresh, copy in last:
        pl.when(fresh)(copy.start)
    for fresh, copy in copies + last:
        pl.when(fresh)(copy.wait)
    weight_copy.wait()


def fix_outputs(
    sz, axis, meta, across, picked, got, early, late, weights, fields, fixed, mine, theirs, outs
):
    args = [meta, across, *picked, *(got[r] for r in late), *weights, *fields, *fixed]
    args += [mine, theirs]
    whole = [shape(out.shape, BF16) for out in outs]
    held = pltpu.VMEM((sz.pairs, sz.chan // SUB, SUB, sz.blk), BF16)
    total = (4, sz.chan, sz.chan)
    return call(
        functools.partial(fix_kernel, sz, axis, early, late),
        [SMEM] + [VMEM] * (len(args) - 1) + [HBM] * 2,
        [HBM] * 3,
        whole + [shape(total, F32)],
        [pltpu.VMEM(sz.picked.shape, F32)] * 2
        + [held, held, pltpu.VMEM(total, F32)]
        + [pltpu.SemaphoreType.DMA((2, sz.pairs)), pltpu.SemaphoreType.DMA],
        8 * len(late) * sz.hb * sz.chan * sz.blk * sz.blk,
        2 << 20,
        8,
        {len(args): 0, len(args) + 1: 1},
    )(*args, *outs)


def add_kernel(gated, inputs, *refs):
    mine, theirs = refs[:2]
    outs = refs[inputs:]
    if gated:
        outs[2][...] = refs[2][...]
    outs[0][...] = mine[...] + theirs[...]
    if len(outs) > 1:
        outs[1][...] = jnp.zeros(outs[1].shape, F32)


def add(mine, theirs, pay, after, last=False):
    outs = [shape(mine.shape, F32)] + ([] if last else [TOKEN])
    args = [mine, theirs]
    if pay is not None:
        outs.append(shape(pay.shape, BF16))
        args.append(pay)
    args += after
    return call(
        functools.partial(add_kernel, pay is not None, len(args)),
        [VMEM] * len(args),
        [VMEM] * len(outs),
        outs,
        [],
        mine.size,
        12 * mine.size,
        2,
    )(*args)


def from_partner(values, bit):
    count = lax.axis_size("dom")
    route = []
    for low in range(count):
        high = low | 1 << bit
        if high != low and high < count:
            route += [(low, high), (high, low)]
    return lax.ppermute(values, "dom", route)


def local(
    features,
    cheb_weight,
    lap_tiles,
    col_index,
    cross_tiles,
    send_index,
    row_index,
    pair_on,
    blk_live,
    cotangent,
):
    sz = Sizes(features, lap_tiles, cross_tiles)
    split = (sz.chan // SUB, SUB, sz.blocks, sz.blk)
    x4 = features.reshape(split).transpose(0, 2, 1, 3)
    u4 = cotangent.reshape(split).transpose(0, 2, 1, 3)
    coupling = cross_tiles.reshape(sz.pairs, sz.blk, sz.blk)
    send, row = send_index.transpose(0, 2, 1), row_index.transpose(0, 2, 1)

    packed = pack(sz, x4, u4, coupling, send, row, pair_on, blk_live, col_index.T)
    t0, s0, cross, across, meta, col = packed[:6]
    everyone = range(sz.rounds)
    got = []
    for bit, pay in enumerate(packed[6:]):
        got.append(from_partner(pay, bit))
    *base, psel, qsel, tiles, turned, gram0 = first_products(sz, meta, col, lap_tiles, t0, s0)
    t1, s1, pays = join(sz, meta, cross, base, [across, psel, qsel, *got], True)

    got = [from_partner(pay, bit) for bit, pay in enumerate(pays)]
    fields = (t1, s1, t0, s0)
    *base, psel, qsel, gram = local_products(sz, meta, col, tiles, turned, fields)
    *picked, mine, given = correct(
        sz, "dom", meta, across, (psel, qsel), got, gram0, gram, s1
    )
    theirs = from_partner(given, 0)
    t2, s2, pays = join(sz, meta, cross, base, picked, False)

    state = {}

    middle = sz.blocks // (2 * ROWS_PART) * ROWS_PART
    orders = cheb_weight.shape[0]

    def window_early_rows(token):
        fields = (t2, s2, t1, s1)
        state["part"] = part_products(sz, meta, col, tiles, turned, fields, None, token)
        return None

    def window_late_rows(token):
        fields = (t2, s2, t1, s1)
        t3, _, _, s3, *state["picked"] = part_products(
            sz, meta, col, tiles, turned, fields, state["part"], token
        )
        state["last"] = (t3, s3)
        return state["picked"][0]

    def window_low(token):
        t3, s3 = state["last"]
        *state["weights"], left, right = base_outputs(
            sz, 0, middle, (t0, t1, t2, t3), (s0, s1, s2, s3), [cheb_weight], token, orders
        )
        state["low"] = [left, right]
        return left

    def window_high(token):
        t3, s3 = state["last"]
        rest = state["weights"] + state["low"]
        left, right, out4, grad4 = base_outputs(
            sz, middle, sz.blocks, (t0, t1, t2, t3), (s0, s1, s2, s3), rest, token, orders
        )
        state["high"], state["outs"] = [left, right], [out4, grad4]
        return left

    windows = [window_early_rows, window_late_rows, window_low, window_high]
    bits = list(reversed(range(1, (lax.axis_size("dom") - 1).bit_length())))
    pays, got = list(pays), [None] * sz.rounds
    history = (t0, t1, t2, s0, s1, s2)
    got[0] = from_partner(pays[0], 0)
    early = [0] + [bit for bit in bits[:-1] if bit < sz.rounds]
    late = [bit for bit in everyone if bit not in early]
    mine, token, *rest = add(mine, theirs, pays[bits[0]] if bits[0] < sz.rounds else None, [])
    held = [got[0]]
    for at, bit in enumerate(bits):
        if bit < sz.rounds:
            pays[bit] = rest[0]
        theirs = from_partner(mine, bit)
        if bit < sz.rounds:
            got[bit] = from_partner(pays[bit], bit)
        if at < len(windows):
            token = windows[at](token)
        last = at + 1 == len(bits)
        gated = not last and bits[at + 1] < sz.rounds
        after = ([] if token is None else [token]) + held
        held = [got[bit]] if bit < sz.rounds else []
        if last:
            (mine,) = add(mine, theirs, None, after, True)
        else:
            mine, token, *rest = add(mine, theirs, pays[bits[at + 1]] if gated else None, after)
    theirs = from_partner(mine, 0)
    *picked, left, right, out4, grad4 = early_outputs(
        sz,
        middle,
        meta,
        across,
        state["picked"],
        got,
        early,
        state["weights"],
        history,
        state["high"],
        mine,
        state["outs"],
    )
    out4, grad4, grad_w = fix_outputs(
        sz,
        "dom",
        meta,
        across,
        picked,
        got,
        early,
        late,
        state["weights"],
        history,
        [left, right],
        mine,
        theirs,
        [out4, grad4],
    )
    conv_out = out4.transpose(0, 2, 1, 3).reshape(features.shape)
    grad_x = grad4.transpose(0, 2, 1, 3).reshape(features.shape)
    return (conv_out, grad_x, grad_w)


def solution(mesh):
    in_specs = (
        P(None, "dom"),
        P(),
        P("dom", None, None, None),
        P("dom", None),
        P("dom", None, None, None, None),
        P("dom", None, None),
        P("dom", None, None),
        P("dom", None),
        P("dom"),
        P(None, "dom"),
    )
    out_specs = (P(None, "dom"), P(None, "dom"), P())
    return jax.shard_map(local, mesh=mesh, in_specs=in_specs, out_specs=out_specs, check_vma=False)
```
